32 devices in a mesh: dp: 16 (over z, y, core), mp: 2 (over x).
Axes of the slice: x: 2, y: 2, z: 4, core: 2. Of those that a mesh axis runs over, the one named last changes fastest.
Arguments:
- inputs: bfloat16 [64, 320, 1024], P('dp', 'mp'), may hold values from -6 to 6
- teacher: bfloat16 [64, 320, 1024], P('dp', 'mp'), may hold values from -6 to 6
- keep_mask: int32 [64, 320], P('dp'), may hold values from 0 to 1, as said below
- gain_attn: bfloat16 [1024], P('dp'), may hold values from 0.099609375 to 1.8984375
- qkv_weight: bfloat16 [1024, 3, 1024], P('dp', None, 'mp'), may hold values from -0.25 to 0.25
- out_weight: bfloat16 [1024, 1024], P('dp', 'mp'), may hold values from -0.5 to 0.5
- gain_mlp: bfloat16 [1024], P('dp'), may hold values from 0.099609375 to 1.8984375
- up_weight: bfloat16 [1024, 4096], P('dp', 'mp'), may hold values from -0.1875 to 0.1875
- down_weight: bfloat16 [1024, 4096], P('dp', 'mp'), may hold values from -0.125 to 0.125
Outputs:
- output: bfloat16 [64, 320, 1024], P('dp', 'mp')
- loss: float32 [], replicated
- input_grad: float32 [64, 320, 1024], P('dp', 'mp')
- gain_attn_grad: float32 [1024], P('dp')
- qkv_grad: float32 [1024, 3, 1024], P('dp', None, 'mp')
- out_grad: float32 [1024, 1024], P('dp', 'mp')
- gain_mlp_grad: float32 [1024], P('dp')
- up_grad: float32 [1024, 4096], P('dp', 'mp')
- down_grad: float32 [1024, 4096], P('dp', 'mp')
The draws below stay inside these ranges and needn't reach their ends.
Inputs may be any that keep to these rules, and one draw needn't show every extreme that they name: `keep_mask`: the first 64 positions of every image are 1; how many of its other positions an image keeps varies from image to image and from draw to draw.
All inputs are finite; a program needn't handle non-finite values.
Results may differ from the reference program's by a relative error of at most 0.009.
The reference program's roundings to bfloat16 on the way count: a program that leaves them out, or rounds other values in their place, can miss the bound.
Values may be sent and summed in bfloat16 or wider, within the bound.
A program may use at most 96 MiB of HBM per device.

```python
import jax
import jax.numpy as jnp
from jax import lax

D = 1024
HEADS = 16
HDIM = 64
FF = 4096
BUF = 64
SLOTS = 256
MICRO = 2
IMG_MICRO = 2
SEQ = 320
IMAGES = 64
TOKENS = 20480


def permuted_row(row_key):
    return jax.random.permutation(row_key, SLOTS)


def draw_keep_mask(key, part):
    row_keys = jax.random.split(jax.random.fold_in(key, 11), IMAGES)
    orders = jax.vmap(permuted_row)(row_keys).astype(jnp.int32)
    image_index = jnp.arange(IMAGES, dtype=jnp.int32)[:, None]
    slope = jax.random.randint(jax.random.fold_in(key, 23), (), 9 * SLOTS // 16, 15 * SLOTS // 16 + 1, dtype=jnp.int32)
    jitter = jax.random.randint(jax.random.fold_in(key, 37), (IMAGES, 1), 0, SLOTS // 32 + 1, dtype=jnp.int32)
    kept_count = SLOTS // 32 + slope * image_index // IMAGES + jitter
    chosen = (orders < kept_count).astype(jnp.int32)
    return jnp.concatenate([jnp.ones((IMAGES, BUF), jnp.int32), chosen], axis=1)


def with_spikes(values, rng, source, target, blocks, factor):
    def block_of(position):
        return (jnp.arange(values.shape[position]) // (values.shape[position] // blocks)).reshape((-1,) + (1,) * (values.ndim - 1 - position))

    first = jax.random.permutation(rng, blocks)[block_of(target)]
    far = (block_of(target) + blocks // 2) % blocks
    return jnp.where((block_of(source) == first) | (block_of(source) == far), factor * values, values)


def block_scale(rng, dims, cuts, least, largest):
    def one(axis_at, shards_of):
        steps = jax.random.uniform(jax.random.fold_in(jax.random.fold_in(rng, 6), axis_at), (shards_of,), jnp.float32, least / len(cuts), largest / len(cuts))
        return jnp.repeat(jnp.exp(steps), dims[axis_at] // shards_of).reshape((-1,) + (1,) * (len(dims) - axis_at - 1))

    loudness = one(*cuts[0])
    for cut in cuts[1:]:
        loudness = loudness * one(*cut)
    return loudness


def noise(stream_key, extent, scale, most, cuts=(), kind=jnp.bfloat16):
    loudness = block_scale(stream_key, extent, cuts, -0.22, 0.18) if cuts else 1.0
    entries = jax.random.normal(stream_key, extent, jnp.float32) * scale * loudness
    return jnp.minimum(jnp.maximum(entries, -most), most).astype(kind)


def bell_draw_with(own_key, dims, scale, limit, cuts, heavy, held_as=jnp.bfloat16):
    array = scale * jax.random.normal(own_key, dims, jnp.float32)
    if cuts:
        array = array * block_scale(own_key, dims, cuts, -0.22, 0.18)
    return jnp.clip(with_spikes(array, jax.random.fold_in(own_key, 3), *heavy), -limit, limit).astype(held_as)


def setup_inputs(seed: int = 0) -> dict:
    splits = jax.random.split(jax.random.key(seed), 10)
    return {
        "inputs": bell_draw_with(splits[0], (IMAGES, SEQ, D), 1.0, 6.0, ((0, 16), (1, 2)), (0, 2, 16, 2.0)),
        "teacher": noise(splits[1], (IMAGES, SEQ, D), 1.0, 6.0, ((0, 16), (1, 2))),
        "keep_mask": draw_keep_mask(jax.random.fold_in(splits[9], 71), 0),
        "gain_attn": jnp.clip(1.0 + 0.18 * jax.random.normal(splits[3], (D,), jnp.float32), 0.099609375, 1.8984375).astype(jnp.bfloat16),
        "qkv_weight": noise(splits[4], (D, 3, D), (D // 2) ** -0.5, 0.25, ((0, 16), (2, 2))),
        "out_weight": noise(splits[5], (D, D), (D // 8) ** -0.5, 0.5, ((0, 16), (1, 2))),
        "gain_mlp": jnp.clip(1.0 + 0.18 * jax.random.normal(splits[6], (D,), jnp.float32), 0.099609375, 1.8984375).astype(jnp.bfloat16),
        "up_weight": noise(splits[7], (D, FF), D ** -0.5, 0.1875, ((0, 16), (1, 2))),
        "down_weight": noise(splits[8], (D, FF), (FF // 2) ** -0.5, 0.125, ((0, 16), (1, 2))),
    }


norm_epsilon = 1e-06
highest = lax.Precision.HIGHEST

@jax.custom_vjp
def low(v):
    return lax.optimization_barrier(v.astype(jnp.bfloat16)).astype(jnp.float32)

@jax.custom_vjp
def low_back(v):
    return v

def low_keep(v):
    return (low(v), None)

def low_pass(kept, grad):
    return (grad,)

def back_keep(v):
    return (v, None)

def back_low(kept, grad):
    return (low(grad),)
low.defvjp(low_keep, low_pass)
low_back.defvjp(back_keep, back_low)

def layer_norm(values, gain_values):
    centre = values - lax.optimization_barrier(jnp.mean(values, axis=-1, keepdims=True))
    spread = lax.optimization_barrier(jnp.mean(centre * centre, axis=-1, keepdims=True))
    return centre * lax.rsqrt(spread + norm_epsilon) * gain_values

def block_loss(parameters, field_in, keep_rows, target):
    gain_one, gain_two, w_qkv, w_out, w_up, w_down = parameters
    image_count, seq_length, width = field_in.shape
    normed_one = low(layer_norm(field_in, gain_one))
    projected = jnp.einsum('bsd,dcf->bscf', normed_one, w_qkv, precision=highest)
    projected = low(low_back(projected))
    queries = projected[:, :, 0].reshape(image_count, seq_length, HEADS, HDIM)
    key_rows = projected[:, :, 1].reshape(image_count, seq_length, HEADS, HDIM)
    value_rows = projected[:, :, 2].reshape(image_count, seq_length, HEADS, HDIM)
    scores = low_back(jnp.einsum('bqhe,bkhe->bhqk', queries, key_rows, precision=highest) * HDIM ** (-0.5))
    allowed = keep_rows[:, None, None, :] > 0
    scores = jnp.where(allowed, scores, -1e+30)
    weights_soft = low(jax.nn.softmax(scores, axis=-1))
    mixture = jnp.einsum('bhqk,bkhe->bqhe', weights_soft, value_rows, precision=highest)
    mixture = low(low_back(mixture.reshape(image_count, seq_length, width)))
    attended = low_back(jnp.einsum('bsf,df->bsd', mixture, w_out, precision=highest))
    middle = field_in + attended
    normed_two = low(layer_norm(middle, gain_two))
    hidden_in = low_back(jnp.einsum('bsd,df->bsf', normed_two, w_up, precision=highest))
    hidden = low(jax.nn.gelu(hidden_in, approximate=False))
    branch = low_back(jnp.einsum('bsf,df->bsd', hidden, w_down, precision=highest))
    result = middle + branch
    keep_float = keep_rows.astype(jnp.float32)[:, :, None]
    error = result - target
    squared = jnp.sum(keep_float * lax.optimization_barrier(jnp.mean(error * error, axis=-1, keepdims=True)))
    return (result * keep_float, squared)

def reference(inputs, teacher, keep_mask, gain_attn, qkv_weight, out_weight, gain_mlp, up_weight, down_weight):
    parameters = (gain_attn.astype(jnp.float32), gain_mlp.astype(jnp.float32), qkv_weight.astype(jnp.float32), out_weight.astype(jnp.float32), up_weight.astype(jnp.float32), down_weight.astype(jnp.float32))
    field_all = inputs.astype(jnp.float32)
    target_all = teacher.astype(jnp.float32)
    group = IMG_MICRO * MICRO
    blocks = IMAGES // group
    valid_total = jnp.sum(keep_mask).astype(jnp.float32)

    def whole(params_in, field_in):

        def one_block(pieces):
            return block_loss(params_in, pieces[0], pieces[1], pieces[2])
        results, squares = lax.map(jax.checkpoint(one_block), (field_in.reshape(blocks, group, SEQ, D), keep_mask.reshape(blocks, group, SEQ), target_all.reshape(blocks, group, SEQ, D)))
        return (results.reshape(IMAGES, SEQ, D), jnp.sum(squares) / valid_total)
    (result, loss), pullback = jax.vjp(whole, parameters, field_all)
    scale_cot = jnp.asarray(D * TOKENS, jnp.float32) + jnp.zeros_like(loss)
    param_grads, field_grad = pullback((jnp.zeros_like(result), scale_cot))
    return (result.astype(jnp.bfloat16), loss, field_grad, param_grads[0], param_grads[2], param_grads[3], param_grads[1], param_grads[4], param_grads[5])
```

```python
import functools
import jax
import jax.numpy as jnp
from jax import lax
from jax.experimental import pallas as pl
from jax.experimental.pallas import tpu as pltpu
from jax.sharding import PartitionSpec as P

MESH = pl.DeviceIdType.MESH
HDIM = 64
CW = 256
EPS = 1e-06
F32 = jnp.float32
BF = jnp.bfloat16
L1, L3, L4, L5 = 2, 1, 1, 1
RDY = L3 + L4 + L5
NT = (((1,), (1,)), ((), ()))
NN = (((1,), (0,)), ((), ()))


def dot(a, b, dims=NN):
    return lax.dot_general(a, b, dims, preferred_element_type=F32)


class Place:
    def __init__(self, groups):
        self.groups = groups
        dp = lax.axis_index("dp")
        self.x = lax.axis_index("mp")
        self.c = lax.rem(dp, 2)
        self.y = lax.rem(dp // 2, 2)
        self.z = dp // 4

    def at(self, z, y, c, x):
        return {"dp": (z * 2 + y) * 2 + c, "mp": x}

    def far(self, j):
        return self.at(lax.rem(self.z + j, self.groups), self.y, self.c, self.x)

    def over_x(self):
        return self.at(self.z, self.y, self.c, 1 - self.x)

    def over_y(self):
        return self.at(self.z, 1 - self.y, self.c, self.x)

    def over_c(self):
        return self.at(self.z, self.y, 1 - self.c, self.x)

    def partners(self):
        return [self.far(j) for j in range(1, self.groups)] + [
            self.over_x(), self.over_y(), self.over_c()
        ]


def meet(place):
    barrier = pltpu.get_barrier_semaphore()
    partners = place.partners()
    for partner in partners:
        pl.semaphore_signal(barrier, 1, device_id=partner, device_id_type=MESH)
    pl.semaphore_wait(barrier, len(partners))


def both_first(k):
    return (k < 5) | (lax.rem(k, 4) == 1)


def when(cond, body):
    if isinstance(cond, bool):
        if cond:
            body()
    else:
        pl.when(cond)(body)


def fwd_kernel(cfg, xin, tin, wq, wo, wu, wd, small, krow, kcol, *refs):
    (wg_o, at_o, proj_o, lse_o, o_o, h_o, bnt_o, g_o, gp_o, gy_o, gm_o, gmt_o, out_o, xs_o, ts_o, sm_o, loss_o,
     wg, xs, ts, sm, a, proj, o, lse, h, bn, g, gp, zb, y, tb,
     local_sem, send_sem, recv_sem, extra_send, extra_recv, out_sem, misc_sem) = refs
    H, R = cfg["groups"], cfg["rows"]
    NQ, NO, NF = cfg["nq"], cfg["no"], cfg["nf"]
    NCH = NQ + NO + 2 * NF
    IMG, SEQ, D = xs.shape
    HALF = SEQ // 2
    TOK = IMG * SEQ
    FH = wq.shape[1] // 3
    GRP = NQ // 3
    place = Place(H)
    x, yy, z, c = place.x, place.y, place.z, place.c
    scale = HDIM ** (-0.5)

    def remote(ref, k, i, device):
        return pltpu.make_async_remote_copy(
            ref, ref, send_sem.at[k, i], recv_sem.at[k, i], device_id=device, device_id_type=MESH
        )

    def source(k):
        if k < NQ:
            return wq.at[:, pl.ds((k % 3) * FH + (k // 3) * CW, CW)]
        if k < NQ + NO:
            return wo.at[:, pl.ds(CW * (k - NQ), CW)]
        if k < NQ + NO + NF:
            return wu.at[:, pl.ds(CW * (k - NQ - NO), CW)]
        return wd.at[:, pl.ds(CW * (k - NQ - NO - NF), CW)]

    def own(k):
        return pltpu.make_async_copy(source(k), wg.at[k, x, z, yy, c], local_sem.at[k])

    def own_wait(k):
        pltpu.make_async_copy(wq.at[:, pl.ds(0, CW)], wg.at[k, x, z, yy, c], local_sem.at[k]).wait()

    def relay(k):
        first = jnp.where(both_first(k), 1, 1 - c)
        xa = jnp.where(first == 1, 1 - x, x)
        ya = jnp.where(first == 1, yy, 1 - yy)
        return xa, ya, jnp.where(first == 1, x, 1 - x), jnp.where(first == 1, 1 - yy, yy)

    def s1(k):
        own_wait(k)
        for j in range(1, H):
            remote(wg.at[k, x, z, yy, c], k, j - 1, place.far(j)).start()

    def s2(k):
        for j in range(1, H):
            remote(wg.at[k, x, lax.rem(z + H - j, H), yy, c], k, j - 1, place.far(j)).wait_recv()
        xa, ya, xb, yb = relay(k)
        remote(wg.at[k, x, :, yy, c], k, H - 1, place.at(z, ya, c, xa)).start()
        remote(wg.at[k, x, :, yy, c], k, H, place.at(z, yb, c, xb)).start()

    def s3(k):
        xa, ya, xb, yb = relay(k)
        remote(wg.at[k, xa, :, ya, c], k, H - 1, place.at(z, ya, c, xa)).wait_recv()
        remote(wg.at[k, xa, :, ya, c], k, H + 1, place.at(z, yb, c, xb)).start()

    def s4(k):
        xa, ya, xb, yb = relay(k)
        remote(wg.at[k, xb, :, yb, c], k, H, place.at(z, yb, c, xb)).wait_recv()
        remote(wg.at[k, 1 - x, :, 1 - yy, c], k, H + 1, place.at(z, yb, c, xb)).wait_recv()
        remote(wg.at[k, :, :, :, c], k, H + 2, place.over_c()).start()

    def keep_chunk(k):
        return pltpu.make_async_copy(wg.at[k], wg_o.at[k], out_sem.at[k])

    def s5(k):
        remote(wg.at[k, :, :, :, 1 - c], k, H + 2, place.over_c()).wait_recv()
        keep_chunk(k).start()

    def step(t):
        def inside(k):
            return (0 <= k < NCH) if isinstance(k, int) else (k >= 0) & (k < NCH)

        when(inside(t + L1), lambda: s1(t + L1))
        when(inside(t), lambda: s2(t))
        when(inside(t - L3), lambda: s3(t - L3))
        when(inside(t - L3 - L4), lambda: s4(t - L3 - L4))
        when(inside(t - RDY), lambda: s5(t - RDY))

    kept = []

    def keep(src, dst):
        copy = pltpu.make_async_copy(src, dst, misc_sem.at[len(kept)])
        copy.start()
        kept.append(copy)

    def extra(src, dst, i, device):
        return pltpu.make_async_remote_copy(
            src, dst, extra_send.at[i], extra_recv.at[i], device_id=device, device_id_type=MESH
        )

    for k in range(NCH):
        own(k).start()
    mine = pl.ds(HALF * x, HALF)
    xl = pltpu.make_async_copy(xin.at[pl.ds(IMG * x, IMG)], xs.at[:, mine], misc_sem.at[30])
    tl = pltpu.make_async_copy(tin.at[pl.ds(IMG * x, IMG)], ts.at[:, mine], misc_sem.at[31])
    sl = pltpu.make_async_copy(small, sm.at[z, yy, c], misc_sem.at[29])
    xl.start()
    tl.start()
    sl.start()
    meet(place)
    xr = extra(xin.at[pl.ds(IMG * (1 - x), IMG)], xs.at[:, mine], 0, place.over_x())
    tr = extra(tin.at[pl.ds(IMG * (1 - x), IMG)], ts.at[:, mine], 1, place.over_x())
    sl.wait()
    for j in range(1, H):
        extra(sm.at[z, yy, c], sm.at[z, yy, c], 3 + j, place.far(j)).start()
    for k in range(L1):
        s1(k)
    xr.start()
    for j in range(1, H):
        extra(sm.at[z, yy, c], sm.at[lax.rem(z + H - j, H), yy, c], 3 + j, place.far(j)).wait_recv()
    extra(sm.at[:, yy, c], sm.at[:, yy, c], 2, place.over_y()).start()
    step(0)
    extra(sm.at[:, 1 - yy, c], sm.at[:, 1 - yy, c], 2, place.over_y()).wait_recv()
    extra(sm.at[:, :, c], sm.at[:, :, c], 3, place.over_c()).start()
    step(1)
    extra(sm.at[:, :, 1 - c], sm.at[:, :, 1 - c], 3, place.over_c()).wait_recv()
    totals = jnp.sum(sm[...].reshape(H * 4, 8, D), axis=0)
    sm_o[...] = totals
    xl.wait()
    extra(xin.at[pl.ds(IMG * (1 - x), IMG)], xs.at[:, pl.ds(HALF * (1 - x), HALF)], 0, place.over_x()).wait_recv()
    keep(xs, xs_o)

    RB = 32

    def rows_of(ref, r):
        per = SEQ // RB
        return ref[r // per, pl.ds(pl.multiple_of(lax.rem(r, per) * RB, RB), RB)]

    def norm_to(values, gain):
        centre = values - jnp.mean(values, axis=-1, keepdims=True)
        spread = jnp.mean(centre * centre, axis=-1, keepdims=True)
        return (centre * lax.rsqrt(spread + EPS) * gain).astype(BF)

    @pl.loop(0, TOK // RB)
    def _(r):
        a[pl.ds(pl.multiple_of(r * RB, RB), RB)] = norm_to(rows_of(xs, r).astype(F32), sm_o[0:1])

    def transposed(src, dst):
        @pl.loop(0, D // 128)
        def _(d):
            t = jnp.transpose(src[:, pl.ds(pl.multiple_of(d * 128, 128), 128)].astype(F32))
            t = t.reshape(64 // R, 2, R, TOK)
            for p in range(2):
                dst[p, pl.ds(pl.multiple_of(d * 64, 64), 64)] = t[:, p].reshape(64, TOK).astype(BF)

    step(2)
    transposed(a, tb)
    keep(tb, at_o)

    def chunk(k, half):
        return wg[k, half].reshape(D, CW)

    def project(k):
        @pl.loop(0, 2)
        def _(half):
            proj[k, half] = dot(a[...], chunk(k, half)).astype(BF).reshape(IMG, SEQ, CW)

    lane = lax.broadcasted_iota(jnp.int32, (SEQ, CW), 1) // HDIM

    def attend(group, u):
        half, i = u // IMG, lax.rem(u, IMG)
        q = proj[3 * group, half, i]
        key = proj[3 * group + 1, half, i]
        val = proj[3 * group + 2, half, i]
        allowed = krow[IMG * x + i, 0:1] > 0
        total = jnp.zeros((SEQ, CW), F32)
        logs = jnp.zeros((SEQ, 128), F32)
        spot = lax.broadcasted_iota(jnp.int32, (SEQ, 128), 1)
        for head in range(CW // HDIM):
            scores = dot(jnp.where(lane == head, q, 0), key, NT) * scale
            scores = jnp.where(allowed, scores, -1e30)
            top = jnp.max(scores, axis=-1, keepdims=True)
            raised = jnp.exp(scores - top)
            norm = jnp.sum(raised, axis=-1, keepdims=True)
            soft = (raised / norm).astype(BF)
            total = total + dot(soft, jnp.where(lane == head, val, 0))
            logs = jnp.where(spot == head, top + jnp.log(norm), logs)
        o[group, half, i] = total.astype(BF)
        lse[group, half, i] = logs

    for k in range(3):
        step(k + RDY)
        project(k)
    done = 3 + RDY
    for group in range(GRP):
        if group:
            for k in range(3 * group, 3 * group + 3):
                while done <= k + RDY:
                    step(done)
                    done += 1
                project(k)

        @pl.loop(0, 2 * IMG)
        def _(u, group=group, done=done):
            pl.when(lax.rem(u, 2) == 0)(lambda: step(done + u // 2))
            attend(group, u)
        done += IMG
    keep(proj, proj_o)
    keep(lse, lse_o)
    keep(o, o_o)
    while done <= NQ + NO - 1 + RDY:
        step(done)
        done += 1

    def gathered(src, k, half):
        return src[k, half].reshape(TOK, CW)

    for k in range(NO):
        for half in range(2):
            part = dot(gathered(o, k, half), chunk(NQ + k, half), NT)
            if k == 0 and half == 0:
                h[...] = xs[...].reshape(TOK, D).astype(F32) + part
            else:
                h[...] += part
    keep(h, h_o)

    @pl.loop(0, TOK // RB)
    def _(r):
        at = pl.ds(pl.multiple_of(r * RB, RB), RB)
        bn[at] = norm_to(h[at], sm_o[1:2])

    tr.start()
    first_up = NQ + NO

    def gelu(k, half):
        GB = 64

        @pl.loop(0, TOK // GB)
        def _(r):
            at = pl.ds(pl.multiple_of(r * GB, GB), GB)
            v = zb[at]
            cdf = 0.5 * (1.0 + lax.erf(v * 0.7071067811865476))
            g[k, half, at] = (v * cdf).astype(BF)
            gp[k, half, at] = (cdf + v * (jnp.exp(-0.5 * (v * v)) * 0.3989422804014327)).astype(BF)

    @pl.loop(0, NF)
    def _(k):
        step(done + k)

        @pl.loop(0, 2)
        def _(half):
            zb[...] = dot(bn[...], chunk(first_up + k, half))
            gelu(k, half)
    done += NF
    keep(g, g_o)
    keep(gp, gp_o)
    first_down = first_up + NF
    kept[1].wait()
    transposed(bn, tb)
    keep(tb, bnt_o)
    y[...] = h[...]

    @pl.loop(0, NF)
    def _(k):
        step(done + k)

        @pl.loop(0, 2)
        def _(half):
            y[...] += dot(g[k, half], chunk(first_down + k, half), NT)

    tl.wait()
    extra(tin.at[pl.ds(IMG * (1 - x), IMG)], ts.at[:, pl.ds(HALF * (1 - x), HALF)], 1, place.over_x()).wait_recv()
    keep(ts, ts_o)
    loss_o[...] = jnp.zeros_like(loss_o)
    factor = 2.0 * cfg["tokens"] / sm_o[2:3]
    xs_ref = xs

    for copy in kept[:1]:
        copy.wait()

    @pl.loop(0, TOK // RB)
    def _(r):
        at = pl.ds(pl.multiple_of(r * RB, RB), RB)
        per = SEQ // RB
        img, pos = r // per, pl.multiple_of(lax.rem(r, per) * RB, RB)
        res = y[at]
        kept_rows = jnp.tile(kcol[IMG * x + img, pl.ds(pos, RB)], (1, D // 128))
        xs_ref[img, pl.ds(pos, RB)] = (res * kept_rows).astype(BF)
        error = res - ts[img, pl.ds(pos, RB)].astype(F32)
        per_row = jnp.mean(error * error, axis=-1, keepdims=True) * kept_rows[:, :1]
        loss_o[...] += jnp.sum(per_row)
        grad = factor * kept_rows * error
        y[at] = grad
        a[at] = grad.astype(BF)

    keep(xs, out_o)
    keep(y, gy_o)
    keep(a, gm_o)
    kept[8].wait()
    transposed(a, tb)
    keep(tb, gmt_o)
    for n, copy in enumerate(kept):
        if n not in (0, 1, 8):
            copy.wait()
    xr.wait_send()
    tr.wait_send()
    for j in range(1, H):
        extra(sm.at[z, yy, c], sm.at[z, yy, c], 3 + j, place.far(j)).wait_send()
    extra(sm.at[:, yy, c], sm.at[:, yy, c], 2, place.over_y()).wait_send()
    extra(sm.at[:, :, c], sm.at[:, :, c], 3, place.over_c()).wait_send()

    @pl.loop(0, NCH)
    def _(k):
        keep_chunk(k).wait()
        for j in range(1, H):
            remote(wg.at[k, x, z, yy, c], k, j - 1, place.far(j)).wait_send()
        for i in (H - 1, H, H + 1):
            remote(wg.at[k, x, :, yy, c], k, i, place.over_x()).wait_send()
        remote(wg.at[k, :, :, :, c], k, H + 2, place.over_c()).wait_send()


def any_spec():
    return pl.BlockSpec(memory_space=pl.ANY)


def vmem_spec():
    return pl.BlockSpec(memory_space=pltpu.VMEM)


def forward(cfg, xin, tin, wq, wo, wu, wd, small, krow, kcol):
    H, R = cfg["groups"], cfg["rows"]
    NQ, NO, NF = cfg["nq"], cfg["no"], cfg["nf"]
    NCH = NQ + NO + 2 * NF
    IMG = xin.shape[0] // 2
    SEQ, D = 2 * xin.shape[1], xin.shape[2]
    TOK = IMG * SEQ
    GRP = NQ // 3
    wg = (NCH, 2, H, 2, 2, R, CW)
    lhs = (2, D // 2, TOK)
    big = (NF, 2, TOK, CW)
    shapes = [
        (wg, BF), (lhs, BF), ((NQ, 2, IMG, SEQ, CW), BF), ((GRP, 2, IMG, SEQ, 128), F32),
        ((GRP, 2, IMG, SEQ, CW), BF), ((TOK, D), F32), (lhs, BF), (big, BF), (big, BF),
        ((TOK, D), F32), ((TOK, D), BF), (lhs, BF), ((IMG, SEQ, D), BF), ((IMG, SEQ, D), BF), ((IMG, SEQ, D), BF),
        ((8, D), F32), ((8, 128), F32),
    ]
    return pl.pallas_call(
        functools.partial(fwd_kernel, cfg),
        name="gather_forward",
        out_shape=[jax.ShapeDtypeStruct(s, t) for s, t in shapes],
        in_specs=[any_spec()] * 7 + [vmem_spec()] * 2,
        out_specs=[any_spec()] * 15 + [vmem_spec()] * 2,
        scratch_shapes=[
            pltpu.VMEM(wg, BF), pltpu.VMEM((IMG, SEQ, D), BF), pltpu.VMEM((IMG, SEQ, D), BF),
            pltpu.VMEM((H, 2, 2, 8, D), F32), pltpu.VMEM((TOK, D), BF),
            pltpu.VMEM((NQ, 2, IMG, SEQ, CW), BF), pltpu.VMEM((GRP, 2, IMG, SEQ, CW), BF),
            pltpu.VMEM((GRP, 2, IMG, SEQ, 128), F32), pltpu.VMEM((TOK, D), F32), pltpu.VMEM((TOK, D), BF),
            pltpu.VMEM(big, BF), pltpu.VMEM(big, BF), pltpu.VMEM((TOK, CW), F32), pltpu.VMEM((TOK, D), F32),
            pltpu.VMEM(lhs, BF),
            pltpu.SemaphoreType.DMA((NCH,)), pltpu.SemaphoreType.DMA((NCH, H + 3)),
            pltpu.SemaphoreType.DMA((NCH, H + 3)), pltpu.SemaphoreType.DMA((H + 4,)),
            pltpu.SemaphoreType.DMA((H + 4,)), pltpu.SemaphoreType.DMA((NCH,)), pltpu.SemaphoreType.DMA((32,)),
        ],
        compiler_params=pltpu.CompilerParams(
            collective_id=0, has_side_effects=True, vmem_limit_bytes=63 * 2**20
        ),
    )(xin, tin, wq, wo, wu, wd, small, krow, kcol)


def config(inputs, weights):
    rows = weights[0].shape[0]
    dps = lax.axis_size("dp")
    return {
        "groups": dps // 4,
        "rows": rows,
        "nq": weights[0].shape[1] * weights[0].shape[2] // CW,
        "no": weights[1].shape[1] // CW,
        "nf": weights[2].shape[1] // CW,
        "tokens": float(inputs.shape[0] * inputs.shape[1] * dps * lax.axis_size("mp")),
    }


def prepare(inputs, keep_mask, gain_attn, gain_mlp):
    R, D = gain_attn.shape[0], inputs.shape[2]
    dps = D // R
    here = lax.broadcasted_iota(jnp.int32, (1, D), 1) // R == lax.axis_index("dp")
    count = jnp.sum(keep_mask).astype(F32)
    small = jnp.concatenate(
        [
            jnp.where(here, jnp.tile(gain_attn.astype(F32), dps)[None], 0.0),
            jnp.where(here, jnp.tile(gain_mlp.astype(F32), dps)[None], 0.0),
            jnp.full((6, D), count, F32),
        ],
        axis=0,
    )
    mask = keep_mask.astype(F32)
    krow = jnp.broadcast_to(mask[:, None, :], (mask.shape[0], 8, mask.shape[1]))
    kcol = jnp.broadcast_to(mask[:, :, None], mask.shape + (128,))
    return small, krow, kcol


SLOTS = 3
WSLOTS = 4
LAGS = (1, 4, 7, 9)


def bwd_kernel(cfg, wg, at_i, proj_i, lse_i, o_i, h_i, bnt_i, g_i, gp_i, gy_i, gm_i, gmt_i, out_i, xs_i,
               totals, loss_i, krow, *refs):
    (out_o, ig_o, dw_o, stat_o,
     q, snd, rcv, near, farr, dw, wb, gb_buf, gpb, gz, zb, gm, lhs1, lhs2, acc, gh, h, o, go, proj, lse, xb, stat, sbuf,
     core_send, core_recv, credit, near_send, near_recv, far_send, far_recv, extra_send, extra_recv,
     wsem, gsem, misc_sem, dw_sem) = refs
    H, R = cfg["groups"], cfg["rows"]
    NQ, NO, NF = cfg["nq"], cfg["no"], cfg["nf"]
    NCH = NQ + NO + 2 * NF
    IMG, SEQ, D = xb.shape
    HALF = SEQ // 2
    TOK = IMG * SEQ
    GRP = NQ // 3
    place = Place(H)
    x, yy, z, c = place.x, place.y, place.z, place.c
    scale = HDIM ** (-0.5)

    def ident(p):
        ff = jnp.where(lax.rem(p, 2) == 0, NQ + NO + NF + p // 2, NQ + NO + p // 2)
        return jnp.where(p < 2 * NF, ff, jnp.where(p < 2 * NF + NO, p - 2 * NF + NQ, p - 2 * NF - NO))

    def relay(k):
        first = jnp.where(both_first(k), 1, 1 - c)
        xa = jnp.where(first == 1, 1 - x, x)
        ya = jnp.where(first == 1, yy, 1 - yy)
        return xa, ya, jnp.where(first == 1, x, 1 - x), jnp.where(first == 1, 1 - yy, yy)

    loads = []

    def load(src, dst):
        copy = pltpu.make_async_copy(src, dst, misc_sem.at[len(loads)])
        copy.start()
        loads.append(copy)
        return copy

    def wload(n):
        return pltpu.make_async_copy(wg.at[ident(n)], wb.at[lax.rem(n, WSLOTS)], wsem.at[n])

    def gload(j):
        s = lax.rem(j, 2)
        return (pltpu.make_async_copy(g_i.at[j], gb_buf.at[s], gsem.at[j, 0]),
                pltpu.make_async_copy(gp_i.at[j], gpb.at[s], gsem.at[j, 1]))

    gm_l = load(gm_i, gm)
    gmt_l = load(gmt_i, lhs1)
    for j in range(2):
        for copy in gload(jnp.int32(j)):
            copy.start()
    for n in range(WSLOTS):
        wload(jnp.int32(n)).start()
    bnt_l = load(bnt_i, lhs2)
    out_l = load(out_i, xb)
    gy_l = load(gy_i, gh)
    h_l = load(h_i, h)
    o_l = load(o_i, o)
    proj_l = load(proj_i, proj)
    lse_l = load(lse_i, lse)

    def extra(src, dst, i, device):
        return pltpu.make_async_remote_copy(
            src, dst, extra_send.at[i], extra_recv.at[i], device_id=device, device_id_type=MESH
        )

    meet(place)

    def core_copy(p, start=False):
        s = lax.rem(p, SLOTS)
        return pltpu.make_async_remote_copy(
            snd.at[s], rcv.at[s], core_send.at[p], core_recv.at[p], device_id=place.over_c(), device_id_type=MESH
        )

    def near_copy(src, k, i, device):
        return pltpu.make_async_remote_copy(
            src, near.at[k, i], near_send.at[k, i], near_recv.at[k, i], device_id=device, device_id_type=MESH
        )

    def far_copy(k, zd, j):
        return pltpu.make_async_remote_copy(
            q.at[k, x, zd, yy], farr.at[k, j - 1], far_send.at[k, j - 1], far_recv.at[k, j - 1],
            device_id=place.far(j), device_id_type=MESH
        )

    def produce(p, lhs, rhs):
        k = ident(p)
        s = lax.rem(p, SLOTS)
        pl.when(p >= SLOTS)(lambda: core_copy(p - SLOTS).wait_send())

        @pl.loop(0, 2)
        def _(half):
            snd[s, half] = dot(lhs[1 - c], rhs(half)).astype(BF).reshape(H, 2, R, CW)
            q[k, half] = dot(lhs[c], rhs(half)).astype(BF).reshape(H, 2, R, CW)

        pl.when(p >= SLOTS)(lambda: pl.semaphore_wait(credit, 1))
        core_copy(p).start()

    def added(k, xi, yi, others):
        @pl.loop(0, H)
        def _(n):
            total = q[k, xi, n, yi].astype(F32)
            for other in others:
                total = total + near[k, other, n].astype(F32)
            q[k, xi, n, yi] = total.astype(BF)

    def r1(p):
        k = ident(p)
        s = lax.rem(p, SLOTS)
        core_copy(p).wait_recv()

        @pl.loop(0, 2 * H)
        def _(n):
            i, m = n // H, lax.rem(n, H)
            for y2 in range(2):
                q[k, i, m, y2] = (q[k, i, m, y2].astype(F32) + rcv[s, i, m, y2].astype(F32)).astype(BF)

        pl.when(p + SLOTS < NCH)(
            lambda: pl.semaphore_signal(credit, 1, device_id=place.over_c(), device_id_type=MESH)
        )
        xa, ya, xo, yo = relay(k)
        near_copy(q.at[k, 1 - x, :, 1 - yy], k, 0, place.at(z, yo, c, xo)).start()
        near_copy(q.at[k, xo, :, yo], k, 1, place.at(z, yo, c, xo)).start()

    def r2(p):
        k = ident(p)
        xa, ya, xo, yo = relay(k)
        near_copy(q.at[k, 1 - x, :, 1 - yy], k, 0, place.at(z, yo, c, xo)).wait_recv()
        added(k, xa, ya, (0,))
        near_copy(q.at[k, xa, :, ya], k, 2, place.at(z, ya, c, xa)).start()

    def r3(p):
        k = ident(p)
        xa, ya, xo, yo = relay(k)
        near_copy(q.at[k, xo, :, yo], k, 1, place.at(z, yo, c, xo)).wait_recv()
        near_copy(q.at[k, xa, :, ya], k, 2, place.at(z, ya, c, xa)).wait_recv()
        added(k, x, yy, (1, 2))
        for j in range(1, H):
            far_copy(k, lax.rem(z + j, H), j).start()

    def dw_copy(k):
        return pltpu.make_async_copy(dw.at[k], dw_o.at[k], dw_sem.at[k])

    def r4(p):
        k = ident(p)
        total = q[k, x, z, yy].astype(F32)
        for j in range(1, H):
            far_copy(k, lax.rem(z + j, H), j).wait_recv()
            total = total + farr[k, j - 1].astype(F32)
        dw[k] = total
        dw_copy(k).start()

    stages = (r1, r2, r3, r4)

    def tick(p, lags=LAGS):
        for stage, lag in zip(stages, lags):
            n = p - lag
            if isinstance(n, int):
                if 0 <= n < NCH:
                    stage(jnp.int32(n))
            else:
                pl.when((n >= 0) & (n < NCH))(lambda stage=stage, n=n: stage(n))

    gm_l.wait()
    gmt_l.wait()
    bnt_l.wait()

    def wchunk(n, half):
        return wb[lax.rem(n, WSLOTS), half].reshape(D, CW)

    def wnext(n):
        pl.when(n + WSLOTS < NCH)(lambda: wload(n + WSLOTS).start())

    GB = 64
    acc[...] = jnp.zeros_like(acc)

    @pl.loop(0, NF)
    def _(j):
        s = lax.rem(j, 2)
        gl, gpl = gload(j)
        gl.wait()
        produce(2 * j, lhs1, lambda half: gb_buf[s, half])
        gpl.wait()
        wload(2 * j).wait()
        tick(2 * j)

        @pl.loop(0, 2)
        def _(half):
            zb[...] = dot(gm[...], wchunk(2 * j, half))

            @pl.loop(0, TOK // GB)
            def _(r):
                at = pl.ds(pl.multiple_of(r * GB, GB), GB)
                gz[half, at] = (zb[at] * gpb[s, half, at].astype(F32)).astype(BF)

        wnext(2 * j)

        @pl.when(j + 2 < NF)
        def _():
            for copy in gload(j + 2):
                copy.start()

        produce(2 * j + 1, lhs2, lambda half: gz[half])
        tick(2 * j + 1)
        wload(2 * j + 1).wait()

        @pl.loop(0, 2)
        def _(half):
            acc[...] += dot(gz[half], wchunk(2 * j + 1, half), NT)

        wnext(2 * j + 1)

    mine, other = pl.ds(HALF * x, HALF), pl.ds(HALF * (1 - x), HALF)
    out_l.wait()
    out_r = extra(xb.at[:, other], out_o.at[pl.ds(IMG * x, IMG)], 0, place.over_x())
    out_r.start()
    out_c = pltpu.make_async_copy(xb.at[:, mine], out_o.at[pl.ds(IMG * x, IMG)], misc_sem.at[30])
    out_c.start()

    RB = 32

    def norm_back(values, grad, gain):
        centre = values - jnp.mean(values, axis=-1, keepdims=True)
        spread = jnp.mean(centre * centre, axis=-1, keepdims=True)
        scaled = lax.rsqrt(spread + EPS)
        unit = centre * scaled
        e = grad * gain
        first = jnp.mean(e, axis=-1, keepdims=True)
        second = jnp.mean(e * unit, axis=-1, keepdims=True)
        return scaled * (e - first - unit * second), grad * unit

    def fold(v):
        return jnp.sum(v.reshape(RB // 8, 8, D), axis=0)

    stat[...] = jnp.zeros_like(stat)
    gy_l.wait()
    h_l.wait()

    @pl.loop(0, TOK // RB)
    def _(r):
        at = pl.ds(pl.multiple_of(r * RB, RB), RB)
        back, product = norm_back(h[at], acc[at], totals[1:2])
        total = gh[at] + back
        gh[at] = total
        gm[at] = total.astype(BF)
        stat[1] += fold(product)

    def transposed(src, dst):
        @pl.loop(0, D // 128)
        def _(d):
            t = jnp.transpose(src[:, pl.ds(pl.multiple_of(d * 128, 128), 128)].astype(F32))
            t = t.reshape(64 // R, 2, R, TOK)
            for p in range(2):
                dst[p, pl.ds(pl.multiple_of(d * 64, 64), 64)] = t[:, p].reshape(64, TOK).astype(BF)

    at_l = load(at_i, lhs2)
    transposed(gm, lhs1)
    o_l.wait()
    base = 2 * NF
    for k in range(NO):
        produce(jnp.int32(base + k), lhs1, lambda half, k=k: o[k, half].reshape(TOK, CW))
        tick(base + k)
        wload(jnp.int32(base + k)).wait()

        @pl.loop(0, 2)
        def _(half, k=k):
            go[k, half] = dot(gm[...], wchunk(jnp.int32(base + k), half)).astype(BF).reshape(IMG, SEQ, CW)

        wnext(jnp.int32(base + k))
    proj_l.wait()
    lse_l.wait()
    lane = lax.broadcasted_iota(jnp.int32, (SEQ, CW), 1) // HDIM
    TN = (((0,), (0,)), ((), ()))

    def attend_back(group, u):
        half, i = u // IMG, lax.rem(u, IMG)
        qr, kr, vr = 3 * group, 3 * group + 1, 3 * group + 2
        query, key, val = proj[qr, half, i], proj[kr, half, i], proj[vr, half, i]
        grad = go[group, half, i]
        logs = lse[group, half, i]
        allowed = krow[IMG * x + i, 0:1] > 0
        gq = jnp.zeros((SEQ, CW), F32)
        gk = jnp.zeros((SEQ, CW), F32)
        gv = jnp.zeros((SEQ, CW), F32)
        for head in range(CW // HDIM):
            of_head = lane == head
            qm = jnp.where(of_head, query, 0)
            gom = jnp.where(of_head, grad, 0)
            scores = jnp.where(allowed, dot(qm, key, NT) * scale, -1e30)
            soft = jnp.exp(scores - logs[:, head:head + 1])
            gsoft = dot(gom, val, NT)
            inner = jnp.sum(gsoft * soft, axis=-1, keepdims=True)
            gs = (soft * (gsoft - inner)).astype(BF)
            gq = gq + dot(gs, jnp.where(of_head, key, 0))
            gk = gk + dot(gs, qm, TN)
            gv = gv + dot(soft.astype(BF), gom, TN)
        proj[qr, half, i] = (gq * scale).astype(BF)
        proj[kr, half, i] = (gk * scale).astype(BF)
        proj[vr, half, i] = gv.astype(BF)

    acc[...] = jnp.zeros_like(acc)
    at_l.wait()
    out_c.wait()
    out_r.wait_send()
    xs_l = load(xs_i, xb)
    pos = [base + NO - lag for lag in LAGS]

    def advance(n, upto):
        for i, stage in enumerate(stages):
            for _ in range(n):
                if pos[i] < upto:
                    stage(jnp.int32(pos[i]))
                    pos[i] += 1

    for group in range(GRP):
        for i in range(1):
            advance(1, base + NO + 3 * group)

        @pl.loop(0, 2 * IMG)
        def _(u, group=group):
            attend_back(group, u)

        for k in range(3 * group, 3 * group + 3):
            p = base + NO + k
            produce(jnp.int32(p), lhs2, lambda half, k=k: proj[k, half].reshape(TOK, CW))
            advance(2, p)
            wload(jnp.int32(p)).wait()

            @pl.loop(0, 2)
            def _(half, k=k, p=p):
                acc[...] += dot(proj[k, half].reshape(TOK, CW), wchunk(jnp.int32(p), half), NT)

            wnext(jnp.int32(p))

    xs_l.wait()
    advance(2, NCH)

    @pl.loop(0, TOK // RB)
    def _(r):
        at = pl.ds(pl.multiple_of(r * RB, RB), RB)
        per = SEQ // RB
        img, row = r // per, pl.multiple_of(lax.rem(r, per) * RB, RB)
        back, product = norm_back(xb[img, pl.ds(row, RB)].astype(F32), acc[at], totals[0:1])
        xb[img, pl.ds(row, RB)] = (gh[at] + back).astype(BF)
        stat[0] += fold(product)

    ig_r = extra(xb.at[:, other], ig_o.at[pl.ds(IMG * x, IMG)], 1, place.over_x())
    ig_r.start()
    ig_c = pltpu.make_async_copy(xb.at[:, mine], ig_o.at[pl.ds(IMG * x, IMG)], misc_sem.at[31])
    ig_c.start()

    row = lax.broadcasted_iota(jnp.int32, (8, D), 0)
    small = jnp.where(row == 0, jnp.sum(stat[0], axis=0, keepdims=True),
                      jnp.where(row == 1, jnp.sum(stat[1], axis=0, keepdims=True),
                                jnp.tile(loss_i[...], (1, D // 128))))
    for n, partner in enumerate((place.over_c(), place.over_y(), place.over_x())):
        sbuf[2 * n] = small
        copy = extra(sbuf.at[2 * n], sbuf.at[2 * n + 1], 2 + n, partner)
        copy.start()
        advance(2, NCH)
        copy.wait()
        small = small + sbuf[2 * n + 1]
    stat_o[z] = small
    for j in range(1, H):
        extra(stat_o.at[z], stat_o.at[z], 4 + j, place.far(j)).start()
    while pos[-1] < NCH:
        advance(1, NCH)
    for j in range(1, H):
        copy = extra(stat_o.at[z], stat_o.at[lax.rem(z + H - j, H)], 4 + j, place.far(j))
        copy.wait()

    out_r.wait_recv()
    ig_r.wait()
    ig_c.wait()

    @pl.loop(NCH - SLOTS, NCH)
    def _(p):
        core_copy(p).wait_send()

    @pl.loop(0, NCH)
    def _(k):
        dw_copy(k).wait()
        for i in range(3):
            near_copy(q.at[k, x, :, yy], k, i, place.over_x()).wait_send()
        for j in range(1, H):
            far_copy(k, z, j).wait_send()


def backward(cfg, saved, krow):
    (wg, at, proj, lse, o, h, bnt, g, gp, gy, gm, gmt, out, xs, ts, totals, loss) = saved
    H, R = cfg["groups"], cfg["rows"]
    NQ, NO, NF = cfg["nq"], cfg["no"], cfg["nf"]
    NCH = NQ + NO + 2 * NF
    IMG, SEQ, D = xs.shape
    TOK = IMG * SEQ
    lhs = (2, D // 2, TOK)
    half = (2, H, 2, R, CW)
    vm = pltpu.VMEM
    dma = pltpu.SemaphoreType.DMA
    return pl.pallas_call(
        functools.partial(bwd_kernel, cfg),
        name="backward_reduce",
        out_shape=[
            jax.ShapeDtypeStruct((2 * IMG, SEQ // 2, D), BF), jax.ShapeDtypeStruct((2 * IMG, SEQ // 2, D), BF),
            jax.ShapeDtypeStruct((NCH, R, CW), F32), jax.ShapeDtypeStruct((H, 8, D), F32),
        ],
        in_specs=[any_spec()] * 14 + [vmem_spec()] * 3,
        out_specs=[any_spec()] * 3 + [vmem_spec()],
        scratch_shapes=[
            vm((NCH,) + half, BF), vm((SLOTS,) + half, BF), vm((SLOTS,) + half, BF),
            vm((NCH, 3, H, R, CW), BF), vm((NCH, H - 1, R, CW), BF), vm((NCH, R, CW), F32),
            vm((WSLOTS, 2, H, 2, 2, R, CW), BF), vm((2, 2, TOK, CW), BF), vm((2, 2, TOK, CW), BF),
            vm((2, TOK, CW), BF), vm((TOK, CW), F32), vm((TOK, D), BF), vm(lhs, BF), vm(lhs, BF),
            vm((TOK, D), F32), vm((TOK, D), F32), vm((TOK, D), F32), vm(o.shape, BF), vm(o.shape, BF),
            vm(proj.shape, BF), vm(lse.shape, F32), vm(xs.shape, BF), vm((2, 8, D), F32), vm((6, 8, D), F32),
            dma((NCH,)), dma((NCH,)), pltpu.SemaphoreType.REGULAR, dma((NCH, 3)), dma((NCH, 3)),
            dma((NCH, H - 1)), dma((NCH, H - 1)), dma((H + 4,)), dma((H + 4,)),
            dma((NCH,)), dma((NF, 2)), dma((32,)), dma((NCH,)),
        ],
        compiler_params=pltpu.CompilerParams(
            collective_id=1, has_side_effects=True, vmem_limit_bytes=63 * 2**20
        ),
    )(wg, at, proj, lse, o, h, bnt, g, gp, gy, gm, gmt, out, xs, totals, loss, krow)


def per_device(
    inputs, teacher, keep_mask, gain_attn, qkv_weight, out_weight, gain_mlp, up_weight, down_weight
):
    cfg = config(inputs, (qkv_weight, out_weight, up_weight, down_weight))
    R, NQ, NO, NF = cfg["rows"], cfg["nq"], cfg["no"], cfg["nf"]
    small, krow, kcol = prepare(inputs, keep_mask, gain_attn, gain_mlp)
    saved = forward(
        cfg, inputs, teacher, qkv_weight.reshape(R, -1), out_weight, up_weight, down_weight, small, krow, kcol
    )
    output, grad_in, dw, stats = backward(cfg, saved, krow)
    total = jnp.sum(stats, axis=0)
    start = lax.axis_index("dp") * R
    gains = lax.dynamic_slice(total, (0, start), (2, R))
    loss = total[2, 0] / saved[15][2, 0]
    qkv = dw[:NQ].reshape(NQ // 3, 3, R, CW).transpose(2, 1, 0, 3).reshape(qkv_weight.shape)

    def columns(first, count):
        return dw[first:first + count].transpose(1, 0, 2).reshape(R, count * CW)

    return (
        output,
        loss,
        grad_in.astype(F32),
        gains[0],
        qkv,
        columns(NQ, NO),
        gains[1],
        columns(NQ + NO, NF),
        columns(NQ + NO + NF, NF),
    )


def solution(mesh):
    rows = P("dp", "mp", None)
    weight = P("dp", "mp")
    qkv = P("dp", None, "mp")
    return jax.shard_map(
        per_device,
        mesh=mesh,
        in_specs=(rows, rows, P("dp", None), P("dp"), qkv, weight, P("dp"), weight, weight),
        out_specs=(rows, P(), rows, P("dp"), qkv, weight, P("dp"), weight, weight),
        check_vma=False,
    )
```

```python
import functools
import jax
import jax.numpy as jnp
from jax import lax
from jax.experimental import pallas as pl
from jax.experimental.pallas import tpu as pltpu
from jax.sharding import PartitionSpec as P

MESH = pl.DeviceIdType.MESH
HDIM = 64
CW = 256
EPS = 1e-06
F32 = jnp.float32
BF = jnp.bfloat16
PIECES = 5
T_FIRST = 6
L1, L3, L4, L5 = 4, 1, 1, 1
RDY = L3 + L4 + L5
NT = (((1,), (1,)), ((), ()))
NN = (((1,), (0,)), ((), ()))


def dot(a, b, dims=NN):
    return lax.dot_general(a, b, dims, preferred_element_type=F32)


class Place:
    def __init__(self, groups):
        self.groups = groups
        dp = lax.axis_index("dp")
        self.x = lax.axis_index("mp")
        self.c = lax.rem(dp, 2)
        self.y = lax.rem(dp // 2, 2)
        self.z = dp // 4

    def at(self, z, y, c, x):
        return {"dp": (z * 2 + y) * 2 + c, "mp": x}

    def far(self, j):
        return self.at(lax.rem(self.z + j, self.groups), self.y, self.c, self.x)

    def over_x(self):
        return self.at(self.z, self.y, self.c, 1 - self.x)

    def over_y(self):
        return self.at(self.z, 1 - self.y, self.c, self.x)

    def over_c(self):
        return self.at(self.z, self.y, 1 - self.c, self.x)

    def partners(self):
        return [self.far(j) for j in range(1, self.groups)] + [
            self.over_x(), self.over_y(), self.over_c()
        ]


def meet(place):
    barrier = pltpu.get_barrier_semaphore()
    partners = place.partners()
    for partner in partners:
        pl.semaphore_signal(barrier, 1, device_id=partner, device_id_type=MESH)
    pl.semaphore_wait(barrier, len(partners))


def both_first(k):
    return (k < PIECES) | ((k >= T_FIRST) & (k < T_FIRST + PIECES))


def when(cond, body):
    if isinstance(cond, bool):
        if cond:
            body()
    else:
        pl.when(cond)(body)


def fwd_kernel(cfg, xin, tin, wq, wo, wu, wd, small, krow, kcol, *refs):
    (wg_o, at_o, proj_o, lse_o, o_o, h_o, bnt_o, g_o, gp_o, gy_o, gm_o, gmt_o, out_o, xs_o, ts_o, sm_o, loss_o,
     wg, xs, ts, sm, a, proj, o, lse, h, bn, g, gp, zb, y, tb,
     local_sem, send_sem, recv_sem, extra_send, extra_recv, piece_send, piece_recv, out_sem, misc_sem) = refs
    H, R = cfg["groups"], cfg["rows"]
    NQ, NO, NF = cfg["nq"], cfg["no"], cfg["nf"]
    NCH = NQ + NO + 2 * NF
    IMG, SEQ, D = xs.shape
    HALF = SEQ // 2
    TOK = IMG * SEQ
    FH = wq.shape[1] // 3
    GRP = NQ // 3
    place = Place(H)
    x, yy, z, c = place.x, place.y, place.z, place.c
    scale = HDIM ** (-0.5)

    def remote(ref, k, i, device):
        return pltpu.make_async_remote_copy(
            ref, ref, send_sem.at[k, i], recv_sem.at[k, i], device_id=device, device_id_type=MESH
        )

    def source(k):
        if k < NQ:
            return wq.at[:, pl.ds((k % 3) * FH + (k // 3) * CW, CW)]
        if k < NQ + NO:
            return wo.at[:, pl.ds(CW * (k - NQ), CW)]
        if k < NQ + NO + NF:
            return wu.at[:, pl.ds(CW * (k - NQ - NO), CW)]
        return wd.at[:, pl.ds(CW * (k - NQ - NO - NF), CW)]

    def own(k):
        return pltpu.make_async_copy(source(k), wg.at[k, x, z, yy, c], local_sem.at[k])

    def own_wait(k):
        pltpu.make_async_copy(wq.at[:, pl.ds(0, CW)], wg.at[k, x, z, yy, c], local_sem.at[k]).wait()

    def relay(k):
        first = jnp.where(both_first(k), 1, 1 - c)
        xa = jnp.where(first == 1, 1 - x, x)
        ya = jnp.where(first == 1, yy, 1 - yy)
        return xa, ya, jnp.where(first == 1, x, 1 - x), jnp.where(first == 1, 1 - yy, yy)

    def s1(k):
        own_wait(k)
        for j in range(1, H):
            remote(wg.at[k, x, z, yy, c], k, j - 1, place.far(j)).start()

    def s2(k):
        for j in range(1, H):
            remote(wg.at[k, x, lax.rem(z + H - j, H), yy, c], k, j - 1, place.far(j)).wait_recv()
        xa, ya, xb, yb = relay(k)
        remote(wg.at[k, x, :, yy, c], k, H - 1, place.at(z, ya, c, xa)).start()
        remote(wg.at[k, x, :, yy, c], k, H, place.at(z, yb, c, xb)).start()

    def s3(k):
        xa, ya, xb, yb = relay(k)
        remote(wg.at[k, xa, :, ya, c], k, H - 1, place.at(z, ya, c, xa)).wait_recv()
        remote(wg.at[k, xa, :, ya, c], k, H + 1, place.at(z, yb, c, xb)).start()

    def s4(k):
        xa, ya, xb, yb = relay(k)
        remote(wg.at[k, xb, :, yb, c], k, H, place.at(z, yb, c, xb)).wait_recv()
        remote(wg.at[k, 1 - x, :, 1 - yy, c], k, H + 1, place.at(z, yb, c, xb)).wait_recv()
        remote(wg.at[k, :, :, :, c], k, H + 2, place.over_c()).start()

    def keep_chunk(k):
        return pltpu.make_async_copy(wg.at[k], wg_o.at[k], out_sem.at[k])

    def s5(k):
        remote(wg.at[k, :, :, :, 1 - c], k, H + 2, place.over_c()).wait_recv()
        keep_chunk(k).start()

    PR = HALF // PIECES

    def piece(i, n, to):
        src, dst = ((xin, xs), (tin, ts))[i]
        return pltpu.make_async_remote_copy(
            src.at[pl.ds(IMG * (1 - x), IMG), pl.ds(PR * n, PR)], dst.at[:, pl.ds(HALF * to + PR * n, PR)],
            piece_send.at[i, n], piece_recv.at[i, n], device_id=place.over_x(), device_id_type=MESH
        )

    def piece_at(t):
        for i, first in ((0, 0), (1, T_FIRST)):
            n = t - first
            when((0 <= n < PIECES) if isinstance(n, int) else (n >= 0) & (n < PIECES),
                 lambda i=i, n=n: piece(i, n, x).start())

    def pieces_in(i):
        for n in range(PIECES):
            piece(i, n, 1 - x).wait_recv()

    def step(t):
        def inside(k):
            return (0 <= k < NCH) if isinstance(k, int) else (k >= 0) & (k < NCH)

        when(inside(t + L1), lambda: s1(t + L1))
        piece_at(t)
        when(inside(t), lambda: s2(t))
        when(inside(t - L3), lambda: s3(t - L3))
        when(inside(t - L3 - L4), lambda: s4(t - L3 - L4))
        when(inside(t - RDY), lambda: s5(t - RDY))

    kept = []

    def keep(src, dst):
        copy = pltpu.make_async_copy(src, dst, misc_sem.at[len(kept)])
        copy.start()
        kept.append(copy)

    def extra(src, dst, i, device):
        return pltpu.make_async_remote_copy(
            src, dst, extra_send.at[i], extra_recv.at[i], device_id=device, device_id_type=MESH
        )

    for k in range(NCH):
        own(k).start()
    mine = pl.ds(HALF * x, HALF)
    xl = pltpu.make_async_copy(xin.at[pl.ds(IMG * x, IMG)], xs.at[:, mine], misc_sem.at[30])
    tl = pltpu.make_async_copy(tin.at[pl.ds(IMG * x, IMG)], ts.at[:, mine], misc_sem.at[31])
    sl = pltpu.make_async_copy(small, sm.at[z, yy, c], misc_sem.at[29])
    xl.start()
    tl.start()
    sl.start()
    meet(place)
    sl.wait()
    for j in range(1, H):
        extra(sm.at[z, yy, c], sm.at[z, yy, c], 3 + j, place.far(j)).start()
    for k in range(L1):
        s1(k)
    for j in range(1, H):
        extra(sm.at[z, yy, c], sm.at[lax.rem(z + H - j, H), yy, c], 3 + j, place.far(j)).wait_recv()
    extra(sm.at[:, yy, c], sm.at[:, yy, c], 2, place.over_y()).start()
    step(0)
    extra(sm.at[:, 1 - yy, c], sm.at[:, 1 - yy, c], 2, place.over_y()).wait_recv()
    extra(sm.at[:, :, c], sm.at[:, :, c], 3, place.over_c()).start()
    step(1)
    extra(sm.at[:, :, 1 - c], sm.at[:, :, 1 - c], 3, place.over_c()).wait_recv()
    totals = jnp.sum(sm[...].reshape(H * 4, 8, D), axis=0)
    sm_o[...] = totals
    xl.wait()
    for t in range(2, PIECES):
        step(t)
    pieces_in(0)
    keep(xs, xs_o)

    RB = 32

    def rows_of(ref, r):
        per = SEQ // RB
        return ref[r // per, pl.ds(pl.multiple_of(lax.rem(r, per) * RB, RB), RB)]

    def norm_to(values, gain):
        centre = values - jnp.mean(values, axis=-1, keepdims=True)
        spread = jnp.mean(centre * centre, axis=-1, keepdims=True)
        return (centre * lax.rsqrt(spread + EPS) * gain).astype(BF)

    @pl.loop(0, TOK // RB)
    def _(r):
        a[pl.ds(pl.multiple_of(r * RB, RB), RB)] = norm_to(rows_of(xs, r).astype(F32), sm_o[0:1])

    def transposed(src, dst):
        @pl.loop(0, D // 128)
        def _(d):
            t = jnp.transpose(src[:, pl.ds(pl.multiple_of(d * 128, 128), 128)].astype(F32))
            t = t.reshape(64 // R, 2, R, TOK)
            for p in range(2):
                dst[p, pl.ds(pl.multiple_of(d * 64, 64), 64)] = t[:, p].reshape(64, TOK).astype(BF)

    transposed(a, tb)
    keep(tb, at_o)

    def chunk(k, half):
        return wg[k, half].reshape(D, CW)

    def project(k):
        @pl.loop(0, 2)
        def _(half):
            proj[k, half] = dot(a[...], chunk(k, half)).astype(BF).reshape(IMG, SEQ, CW)

    lane = lax.broadcasted_iota(jnp.int32, (SEQ, CW), 1) // HDIM

    def attend(group, u):
        half, i = u // IMG, lax.rem(u, IMG)
        q = proj[3 * group, half, i]
        key = proj[3 * group + 1, half, i]
        val = proj[3 * group + 2, half, i]
        allowed = krow[IMG * x + i, 0:1] > 0
        total = jnp.zeros((SEQ, CW), F32)
        logs = jnp.zeros((SEQ, 128), F32)
        spot = lax.broadcasted_iota(jnp.int32, (SEQ, 128), 1)
        for head in range(CW // HDIM):
            scores = dot(jnp.where(lane == head, q, 0), key, NT) * scale
            scores = jnp.where(allowed, scores, -1e30)
            top = jnp.max(scores, axis=-1, keepdims=True)
            raised = jnp.exp(scores - top)
            norm = jnp.sum(raised, axis=-1, keepdims=True)
            soft = (raised / norm).astype(BF)
            total = total + dot(soft, jnp.where(lane == head, val, 0))
            logs = jnp.where(spot == head, top + jnp.log(norm), logs)
        o[group, half, i] = total.astype(BF)
        lse[group, half, i] = logs

    done = PIECES
    for k in range(3):
        while done <= k + RDY:
            step(done)
            done += 1
        project(k)
    for group in range(GRP):
        if group:
            for k in range(3 * group, 3 * group + 3):
                while done <= k + RDY:
                    step(done)
                    done += 1
                project(k)

        @pl.loop(0, 2 * IMG)
        def _(u, group=group, done=done):
            pl.when(lax.rem(u, 2) == 0)(lambda: step(done + u // 2))
            attend(group, u)
        done += IMG
    keep(proj, proj_o)
    keep(lse, lse_o)
    keep(o, o_o)
    while done <= NQ + NO - 1 + RDY:
        step(done)
        done += 1

    def gathered(src, k, half):
        return src[k, half].reshape(TOK, CW)

    for k in range(NO):
        for half in range(2):
            part = dot(gathered(o, k, half), chunk(NQ + k, half), NT)
            if k == 0 and half == 0:
                h[...] = xs[...].reshape(TOK, D).astype(F32) + part
            else:
                h[...] += part
    keep(h, h_o)

    @pl.loop(0, TOK // RB)
    def _(r):
        at = pl.ds(pl.multiple_of(r * RB, RB), RB)
        bn[at] = norm_to(h[at], sm_o[1:2])

    first_up = NQ + NO

    def gelu(k, half):
        GB = 64

        @pl.loop(0, TOK // GB)
        def _(r):
            at = pl.ds(pl.multiple_of(r * GB, GB), GB)
            v = zb[at]
            cdf = 0.5 * (1.0 + lax.erf(v * 0.7071067811865476))
            g[k, half, at] = (v * cdf).astype(BF)
            gp[k, half, at] = (cdf + v * (jnp.exp(-0.5 * (v * v)) * 0.3989422804014327)).astype(BF)

    @pl.loop(0, NF)
    def _(k):
        step(done + k)

        @pl.loop(0, 2)
        def _(half):
            zb[...] = dot(bn[...], chunk(first_up + k, half))
            gelu(k, half)
    done += NF
    keep(g, g_o)
    keep(gp, gp_o)
    first_down = first_up + NF
    kept[1].wait()
    transposed(bn, tb)
    keep(tb, bnt_o)
    y[...] = h[...]

    @pl.loop(0, NF)
    def _(k):
        step(done + k)

        @pl.loop(0, 2)
        def _(half):
            y[...] += dot(g[k, half], chunk(first_down + k, half), NT)

    tl.wait()
    pieces_in(1)
    keep(ts, ts_o)
    loss_o[...] = jnp.zeros_like(loss_o)
    factor = 2.0 * cfg["tokens"] / sm_o[2:3]
    xs_ref = xs

    for copy in kept[:1]:
        copy.wait()

    @pl.loop(0, TOK // RB)
    def _(r):
        at = pl.ds(pl.multiple_of(r * RB, RB), RB)
        per = SEQ // RB
        img, pos = r // per, pl.multiple_of(lax.rem(r, per) * RB, RB)
        res = y[at]
        kept_rows = jnp.tile(kcol[IMG * x + img, pl.ds(pos, RB)], (1, D // 128))
        xs_ref[img, pl.ds(pos, RB)] = (res * kept_rows).astype(BF)
        error = res - ts[img, pl.ds(pos, RB)].astype(F32)
        per_row = jnp.mean(error * error, axis=-1, keepdims=True) * kept_rows[:, :1]
        loss_o[...] += jnp.sum(per_row)
        grad = factor * kept_rows * error
        y[at] = grad
        a[at] = grad.astype(BF)

    keep(xs, out_o)
    keep(y, gy_o)
    keep(a, gm_o)
    kept[8].wait()
    transposed(a, tb)
    keep(tb, gmt_o)
    for n, copy in enumerate(kept):
        if n not in (0, 1, 8):
            copy.wait()
    for i in range(2):
        for n in range(PIECES):
            piece(i, n, x).wait_send()
    for j in range(1, H):
        extra(sm.at[z, yy, c], sm.at[z, yy, c], 3 + j, place.far(j)).wait_send()
    extra(sm.at[:, yy, c], sm.at[:, yy, c], 2, place.over_y()).wait_send()
    extra(sm.at[:, :, c], sm.at[:, :, c], 3, place.over_c()).wait_send()

    @pl.loop(0, NCH)
    def _(k):
        keep_chunk(k).wait()
        for j in range(1, H):
            remote(wg.at[k, x, z, yy, c], k, j - 1, place.far(j)).wait_send()
        for i in (H - 1, H, H + 1):
            remote(wg.at[k, x, :, yy, c], k, i, place.over_x()).wait_send()
        remote(wg.at[k, :, :, :, c], k, H + 2, place.over_c()).wait_send()


def any_spec():
    return pl.BlockSpec(memory_space=pl.ANY)


def vmem_spec():
    return pl.BlockSpec(memory_space=pltpu.VMEM)


def forward(cfg, xin, tin, wq, wo, wu, wd, small, krow, kcol):
    H, R = cfg["groups"], cfg["rows"]
    NQ, NO, NF = cfg["nq"], cfg["no"], cfg["nf"]
    NCH = NQ + NO + 2 * NF
    IMG = xin.shape[0] // 2
    SEQ, D = 2 * xin.shape[1], xin.shape[2]
    TOK = IMG * SEQ
    GRP = NQ // 3
    wg = (NCH, 2, H, 2, 2, R, CW)
    lhs = (2, D // 2, TOK)
    big = (NF, 2, TOK, CW)
    shapes = [
        (wg, BF), (lhs, BF), ((NQ, 2, IMG, SEQ, CW), BF), ((GRP, 2, IMG, SEQ, 128), F32),
        ((GRP, 2, IMG, SEQ, CW), BF), ((TOK, D), F32), (lhs, BF), (big, BF), (big, BF),
        ((TOK, D), F32), ((TOK, D), BF), (lhs, BF), ((IMG, SEQ, D), BF), ((IMG, SEQ, D), BF), ((IMG, SEQ, D), BF),
        ((8, D), F32), ((8, 128), F32),
    ]
    return pl.pallas_call(
        functools.partial(fwd_kernel, cfg),
        name="gather_forward",
        out_shape=[jax.ShapeDtypeStruct(s, t) for s, t in shapes],
        in_specs=[any_spec()] * 7 + [vmem_spec()] * 2,
        out_specs=[any_spec()] * 15 + [vmem_spec()] * 2,
        scratch_shapes=[
            pltpu.VMEM(wg, BF), pltpu.VMEM((IMG, SEQ, D), BF), pltpu.VMEM((IMG, SEQ, D), BF),
            pltpu.VMEM((H, 2, 2, 8, D), F32), pltpu.VMEM((TOK, D), BF),
            pltpu.VMEM((NQ, 2, IMG, SEQ, CW), BF), pltpu.VMEM((GRP, 2, IMG, SEQ, CW), BF),
            pltpu.VMEM((GRP, 2, IMG, SEQ, 128), F32), pltpu.VMEM((TOK, D), F32), pltpu.VMEM((TOK, D), BF),
            pltpu.VMEM(big, BF), pltpu.VMEM(big, BF), pltpu.VMEM((TOK, CW), F32), pltpu.VMEM((TOK, D), F32),
            pltpu.VMEM(lhs, BF),
            pltpu.SemaphoreType.DMA((NCH,)), pltpu.SemaphoreType.DMA((NCH, H + 3)),
            pltpu.SemaphoreType.DMA((NCH, H + 3)), pltpu.SemaphoreType.DMA((H + 4,)),
            pltpu.SemaphoreType.DMA((H + 4,)), pltpu.SemaphoreType.DMA((2, PIECES)),
            pltpu.SemaphoreType.DMA((2, PIECES)), pltpu.SemaphoreType.DMA((NCH,)), pltpu.SemaphoreType.DMA((32,)),
        ],
        compiler_params=pltpu.CompilerParams(
            collective_id=0, has_side_effects=True, vmem_limit_bytes=63 * 2**20
        ),
    )(xin, tin, wq, wo, wu, wd, small, krow, kcol)


def config(inputs, weights):
    rows = weights[0].shape[0]
    dps = lax.axis_size("dp")
    return {
        "groups": dps // 4,
        "rows": rows,
        "nq": weights[0].shape[1] * weights[0].shape[2] // CW,
        "no": weights[1].shape[1] // CW,
        "nf": weights[2].shape[1] // CW,
        "tokens": float(inputs.shape[0] * inputs.shape[1] * dps * lax.axis_size("mp")),
    }


def prepare(inputs, keep_mask, gain_attn, gain_mlp):
    R, D = gain_attn.shape[0], inputs.shape[2]
    dps = D // R
    here = lax.broadcasted_iota(jnp.int32, (1, D), 1) // R == lax.axis_index("dp")
    count = jnp.sum(keep_mask).astype(F32)
    small = jnp.concatenate(
        [
            jnp.where(here, jnp.tile(gain_attn.astype(F32), dps)[None], 0.0),
            jnp.where(here, jnp.tile(gain_mlp.astype(F32), dps)[None], 0.0),
            jnp.full((6, D), count, F32),
        ],
        axis=0,
    )
    mask = keep_mask.astype(F32)
    krow = jnp.broadcast_to(mask[:, None, :], (mask.shape[0], 8, mask.shape[1]))
    kcol = jnp.broadcast_to(mask[:, :, None], mask.shape + (128,))
    return small, krow, kcol


SLOTS = 3
WSLOTS = 4
CALLS = (
    (0, 0, 0, 0, 0), (0, 0, 0, 0, 0), (0, 0, 0, 0, 0), (1, 0, 0, 0, 0), (0, 0, 0, 0, 0),
    (1, 0, 0, 0, 0), (0, 0, 0, 0, 0), (1, 0, 0, 0, 0), (0, 1, 0, 0, 0), (1, 0, 0, 0, 0),
    (0, 1, 0, 0, 0), (1, 0, 0, 0, 0), (0, 0, 0, 0, 0), (1, 0, 0, 0, 0), (0, 1, 0, 0, 0),
    (1, 0, 0, 0, 0), (0, 0, 0, 0, 0), (1, 0, 0, 0, 0), (0, 0, 2, 0, 0), (1, 1, 1, 0, 0),
    (1, 0, 0, 0, 0), (0, 0, 0, 0, 0), (0, 0, 0, 0, 0), (1, 1, 0, 1, 0), (0, 0, 0, 0, 0),
    (1, 0, 0, 1, 0), (0, 0, 0, 0, 0), (1, 1, 1, 1, 0), (1, 0, 0, 0, 0), (0, 1, 0, 0, 0),
    (0, 0, 0, 0, 0), (1, 1, 0, 0, 0), (1, 0, 0, 1, 0), (0, 1, 1, 0, 0), (0, 1, 0, 0, 0),
    (0, 0, 0, 0, 0), (0, 0, 0, 0, 0), (1, 0, 0, 0, 0), (0, 1, 0, 0, 0), (1, 0, 3, 1, 0),
    (0, 1, 3, 0, 0), (0, 1, 0, 1, 0), (0, 1, 1, 1, 0), (0, 0, 0, 0, 0), (0, 0, 1, 1, 0),
    (0, 1, 0, 0, 0), (1, 0, 0, 1, 0), (1, 0, 1, 0, 0), (1, 1, 0, 1, 0), (0, 1, 1, 1, 0),
    (0, 0, 1, 1, 0), (0, 1, 1, 1, 0), (0, 1, 0, 2, 0), (0, 0, 0, 0, 0), (0, 1, 1, 1, 0),
    (0, 0, 0, 0, 0), (1, 0, 0, 1, 0), (1, 0, 1, 0, 0), (1, 1, 1, 0, 0), (0, 1, 0, 1, 0),
)
DRAIN = (
    3, 2, 1, 4, 3, 4, 1, 3, 4, 2, 2, 2, 4, 3, 3, 3, 4,
)
OUT_FIRST = 1


def bwd_kernel(cfg, wg, at_i, proj_i, lse_i, o_i, h_i, bnt_i, g_i, gp_i, gy_i, gm_i, gmt_i, out_i, xs_i,
               totals, loss_i, krow, *refs):
    (out_o, ig_o, dw_o, stat_o,
     q, snd, rcv, near, farr, dw, wb, gb_buf, gpb, gz, zb, gm, lhs1, lhs2, acc, gh, h, o, go, proj, lse, xb, stat, sbuf,
     core_send, core_recv, credit, near_send, near_recv, far_send, far_recv, extra_send, extra_recv, piece_send, piece_recv,
     wsem, gsem, misc_sem, dw_sem) = refs
    H, R = cfg["groups"], cfg["rows"]
    NQ, NO, NF = cfg["nq"], cfg["no"], cfg["nf"]
    NCH = NQ + NO + 2 * NF
    IMG, SEQ, D = xb.shape
    HALF = SEQ // 2
    TOK = IMG * SEQ
    GRP = NQ // 3
    place = Place(H)
    x, yy, z, c = place.x, place.y, place.z, place.c
    scale = HDIM ** (-0.5)

    def ident(p):
        ff = jnp.where(lax.rem(p, 2) == 0, NQ + NO + NF + p // 2, NQ + NO + p // 2)
        return jnp.where(p < 2 * NF, ff, jnp.where(p < 2 * NF + NO, p - 2 * NF + NQ, p - 2 * NF - NO))

    def relay(p):
        both = (p >= OUT_FIRST) & (p < OUT_FIRST + PIECES)
        first = jnp.where(both, 1, 1 - c)
        xa = jnp.where(first == 1, 1 - x, x)
        ya = jnp.where(first == 1, yy, 1 - yy)
        return xa, ya, jnp.where(first == 1, x, 1 - x), jnp.where(first == 1, 1 - yy, yy)

    loads = []

    def load(src, dst):
        copy = pltpu.make_async_copy(src, dst, misc_sem.at[len(loads)])
        copy.start()
        loads.append(copy)
        return copy

    def wload(n):
        return pltpu.make_async_copy(wg.at[ident(n)], wb.at[lax.rem(n, WSLOTS)], wsem.at[n])

    def gload(j):
        s = lax.rem(j, 2)
        return (pltpu.make_async_copy(g_i.at[j], gb_buf.at[s], gsem.at[j, 0]),
                pltpu.make_async_copy(gp_i.at[j], gpb.at[s], gsem.at[j, 1]))

    gm_l = load(gm_i, gm)
    gmt_l = load(gmt_i, lhs1)
    for j in range(2):
        for copy in gload(jnp.int32(j)):
            copy.start()
    for n in range(WSLOTS):
        wload(jnp.int32(n)).start()
    bnt_l = load(bnt_i, lhs2)
    out_l = load(out_i, xb)
    gy_l = load(gy_i, gh)
    h_l = load(h_i, h)
    o_l = load(o_i, o)
    proj_l = load(proj_i, proj)
    lse_l = load(lse_i, lse)

    def extra(src, dst, i, device):
        return pltpu.make_async_remote_copy(
            src, dst, extra_send.at[i], extra_recv.at[i], device_id=device, device_id_type=MESH
        )

    meet(place)

    def core_copy(p, start=False):
        s = lax.rem(p, SLOTS)
        return pltpu.make_async_remote_copy(
            snd.at[s], rcv.at[s], core_send.at[p], core_recv.at[p], device_id=place.over_c(), device_id_type=MESH
        )

    def near_copy(src, k, i, device):
        return pltpu.make_async_remote_copy(
            src, near.at[k, i], near_send.at[k, i], near_recv.at[k, i], device_id=device, device_id_type=MESH
        )

    def far_copy(k, zd, j):
        return pltpu.make_async_remote_copy(
            q.at[k, x, zd, yy], farr.at[k, j - 1], far_send.at[k, j - 1], far_recv.at[k, j - 1],
            device_id=place.far(j), device_id_type=MESH
        )

    def produce(p, lhs, rhs):
        k = ident(p)
        s = lax.rem(p, SLOTS)
        pl.when(p >= SLOTS)(lambda: core_copy(p - SLOTS).wait_send())

        @pl.loop(0, 2)
        def _(half):
            snd[s, half] = dot(lhs[1 - c], rhs(half)).astype(BF).reshape(H, 2, R, CW)
            q[k, half] = dot(lhs[c], rhs(half)).astype(BF).reshape(H, 2, R, CW)

        pl.when(p >= SLOTS)(lambda: pl.semaphore_wait(credit, 1))
        core_copy(p).start()

    def added(k, xi, yi, others):
        @pl.loop(0, H)
        def _(n):
            total = q[k, xi, n, yi].astype(F32)
            for other in others:
                total = total + near[k, other, n].astype(F32)
            q[k, xi, n, yi] = total.astype(BF)

    def r1(p):
        k = ident(p)
        s = lax.rem(p, SLOTS)
        core_copy(p).wait_recv()

        @pl.loop(0, 2 * H)
        def _(n):
            i, m = n // H, lax.rem(n, H)
            for y2 in range(2):
                q[k, i, m, y2] = (q[k, i, m, y2].astype(F32) + rcv[s, i, m, y2].astype(F32)).astype(BF)

        pl.when(p + SLOTS < NCH)(
            lambda: pl.semaphore_signal(credit, 1, device_id=place.over_c(), device_id_type=MESH)
        )
        xa, ya, xo, yo = relay(p)
        near_copy(q.at[k, 1 - x, :, 1 - yy], k, 0, place.at(z, yo, c, xo)).start()
        near_copy(q.at[k, xo, :, yo], k, 1, place.at(z, yo, c, xo)).start()

    def r2(p):
        k = ident(p)
        xa, ya, xo, yo = relay(p)
        near_copy(q.at[k, 1 - x, :, 1 - yy], k, 0, place.at(z, yo, c, xo)).wait_recv()
        added(k, xa, ya, (0,))
        near_copy(q.at[k, xa, :, ya], k, 2, place.at(z, ya, c, xa)).start()

    def r3(p):
        k = ident(p)
        xa, ya, xo, yo = relay(p)
        near_copy(q.at[k, xo, :, yo], k, 1, place.at(z, yo, c, xo)).wait_recv()
        near_copy(q.at[k, xa, :, ya], k, 2, place.at(z, ya, c, xa)).wait_recv()
        added(k, x, yy, (1, 2))
        for j in range(1, H):
            far_copy(k, lax.rem(z + j, H), j).start()

    def dw_copy(k):
        return pltpu.make_async_copy(dw.at[k], dw_o.at[k], dw_sem.at[k])

    def r4(p):
        k = ident(p)
        total = q[k, x, z, yy].astype(F32)
        for j in range(1, H):
            far_copy(k, lax.rem(z + j, H), j).wait_recv()
            total = total + farr[k, j - 1].astype(F32)
        dw[k] = total
        dw_copy(k).start()

    stages = (r1, r2, r3, r4)

    before = [[sum(call[i] for call in CALLS[:n]) for n in range(len(CALLS) + 1)] for i in range(5)]
    place_no = [0]

    def pick(table, index):
        value = jnp.int32(table[0])
        for n in range(1, len(table)):
            if table[n] != table[n - 1]:
                value = jnp.where(index >= n, table[n], value)
        return value

    def serve(numbers, index=None):
        for i in (3, 2, 1, 0):
            counts = [CALLS[n][i] for n in numbers]
            starts = [before[i][n] for n in numbers]
            if index is None:
                for n in range(counts[0]):
                    stages[i](jnp.int32(starts[0] + n))
            elif max(counts) == 1:
                pl.when(pick(counts, index) > 0)(lambda i=i, starts=starts: stages[i](pick(starts, index)))
            elif max(counts) > 1:
                first = pick(starts, index)

                @pl.loop(first, first + pick(counts, index))
                def _(n, i=i):
                    stages[i](n)

    def serve_next():
        serve([place_no[0]])
        place_no[0] += 1

    gm_l.wait()
    gmt_l.wait()
    bnt_l.wait()

    def wchunk(n, half):
        return wb[lax.rem(n, WSLOTS), half].reshape(D, CW)

    def wnext(n):
        pl.when(n + WSLOTS < NCH)(lambda: wload(n + WSLOTS).start())

    GB = 64
    PR = HALF // PIECES
    mine = pl.ds(HALF * x, HALF)

    def piece(i, n):
        return pltpu.make_async_remote_copy(
            xb.at[:, pl.ds(HALF * (1 - x) + PR * n, PR)],
            (out_o, ig_o)[i].at[pl.ds(IMG * x, IMG), pl.ds(PR * n, PR)],
            piece_send.at[i, n], piece_recv.at[i, n], device_id=place.over_x(), device_id_type=MESH
        )

    acc[...] = jnp.zeros_like(acc)
    out_l.wait()
    out_c = pltpu.make_async_copy(xb.at[:, mine], out_o.at[pl.ds(IMG * x, IMG)], misc_sem.at[30])
    out_c.start()

    @pl.loop(0, NF)
    def _(j):
        s = lax.rem(j, 2)
        pl.when(j < PIECES)(lambda: piece(0, j).start())
        gl, gpl = gload(j)
        gl.wait()
        produce(2 * j, lhs1, lambda half: gb_buf[s, half])
        serve([4 * n for n in range(NF)], j)
        gpl.wait()
        wload(2 * j).wait()

        @pl.loop(0, 2)
        def _(half):
            zb[...] = dot(gm[...], wchunk(2 * j, half))

            @pl.loop(0, TOK // GB)
            def _(r):
                at = pl.ds(pl.multiple_of(r * GB, GB), GB)
                gz[half, at] = (zb[at] * gpb[s, half, at].astype(F32)).astype(BF)

        wnext(2 * j)

        @pl.when(j + 2 < NF)
        def _():
            for copy in gload(j + 2):
                copy.start()

        serve([4 * n + 1 for n in range(NF)], j)
        produce(2 * j + 1, lhs2, lambda half: gz[half])
        serve([4 * n + 2 for n in range(NF)], j)
        wload(2 * j + 1).wait()

        @pl.loop(0, 2)
        def _(half):
            acc[...] += dot(gz[half], wchunk(2 * j + 1, half), NT)

        wnext(2 * j + 1)
        serve([4 * n + 3 for n in range(NF)], j)

    place_no[0] = 4 * NF
    RB = 32

    def norm_back(values, grad, gain):
        centre = values - jnp.mean(values, axis=-1, keepdims=True)
        spread = jnp.mean(centre * centre, axis=-1, keepdims=True)
        scaled = lax.rsqrt(spread + EPS)
        unit = centre * scaled
        e = grad * gain
        first = jnp.mean(e, axis=-1, keepdims=True)
        second = jnp.mean(e * unit, axis=-1, keepdims=True)
        return scaled * (e - first - unit * second), grad * unit

    def fold(v):
        return jnp.sum(v.reshape(RB // 8, 8, D), axis=0)

    base = 2 * NF
    stat[...] = jnp.zeros_like(stat)
    gy_l.wait()
    h_l.wait()

    for part in range(2):
        count = TOK // RB // 2

        @pl.loop(part * count, (part + 1) * count)
        def _(r):
            at = pl.ds(pl.multiple_of(r * RB, RB), RB)
            back, product = norm_back(h[at], acc[at], totals[1:2])
            total = gh[at] + back
            gh[at] = total
            gm[at] = total.astype(BF)
            stat[1] += fold(product)

        serve_next()

    def transposed(src, dst):
        @pl.loop(0, D // 128)
        def _(d):
            t = jnp.transpose(src[:, pl.ds(pl.multiple_of(d * 128, 128), 128)].astype(F32))
            t = t.reshape(64 // R, 2, R, TOK)
            for p in range(2):
                dst[p, pl.ds(pl.multiple_of(d * 64, 64), 64)] = t[:, p].reshape(64, TOK).astype(BF)

    at_l = load(at_i, lhs2)
    transposed(gm, lhs1)
    o_l.wait()
    for k in range(NO):
        produce(jnp.int32(base + k), lhs1, lambda half, k=k: o[k, half].reshape(TOK, CW))
        serve_next()
        wload(jnp.int32(base + k)).wait()

        @pl.loop(0, 2)
        def _(half, k=k):
            go[k, half] = dot(gm[...], wchunk(jnp.int32(base + k), half)).astype(BF).reshape(IMG, SEQ, CW)

        wnext(jnp.int32(base + k))
        serve_next()
    proj_l.wait()
    lse_l.wait()
    lane = lax.broadcasted_iota(jnp.int32, (SEQ, CW), 1) // HDIM
    TN = (((0,), (0,)), ((), ()))

    def attend_back(group, u):
        half, i = u // IMG, lax.rem(u, IMG)
        qr, kr, vr = 3 * group, 3 * group + 1, 3 * group + 2
        query, key, val = proj[qr, half, i], proj[kr, half, i], proj[vr, half, i]
        grad = go[group, half, i]
        logs = lse[group, half, i]
        allowed = krow[IMG * x + i, 0:1] > 0
        gq = jnp.zeros((SEQ, CW), F32)
        gk = jnp.zeros((SEQ, CW), F32)
        gv = jnp.zeros((SEQ, CW), F32)
        for head in range(CW // HDIM):
            of_head = lane == head
            qm = jnp.where(of_head, query, 0)
            gom = jnp.where(of_head, grad, 0)
            scores = jnp.where(allowed, dot(qm, key, NT) * scale, -1e30)
            soft = jnp.exp(scores - logs[:, head:head + 1])
            gsoft = dot(gom, val, NT)
            inner = jnp.sum(gsoft * soft, axis=-1, keepdims=True)
            gs = (soft * (gsoft - inner)).astype(BF)
            gq = gq + dot(gs, jnp.where(of_head, key, 0))
            gk = gk + dot(gs, qm, TN)
            gv = gv + dot(soft.astype(BF), gom, TN)
        proj[qr, half, i] = (gq * scale).astype(BF)
        proj[kr, half, i] = (gk * scale).astype(BF)
        proj[vr, half, i] = gv.astype(BF)

    acc[...] = jnp.zeros_like(acc)
    at_l.wait()
    out_c.wait()
    for n in range(PIECES):
        piece(0, n).wait_send()
    xs_l = load(xs_i, xb)

    for group in range(GRP):
        numbers = [place_no[0] + u for u in range(2 * IMG)]
        place_no[0] += 2 * IMG

        @pl.loop(0, 2 * IMG)
        def _(u, numbers=numbers, group=group):
            serve(numbers, u)
            attend_back(group, u)

        for k in range(3 * group, 3 * group + 3):
            serve_next()
            produce(jnp.int32(base + NO + k), lhs2, lambda half, k=k: proj[k, half].reshape(TOK, CW))

        for k in range(3 * group, 3 * group + 3):
            p = base + NO + k
            serve_next()
            wload(jnp.int32(p)).wait()

            @pl.loop(0, 2)
            def _(half, k=k, p=p):
                acc[...] += dot(proj[k, half].reshape(TOK, CW), wchunk(jnp.int32(p), half), NT)

            wnext(jnp.int32(p))

    xs_l.wait()
    serve_next()
    per = SEQ // RB

    def finish(img, row):
        at = pl.ds(pl.multiple_of(img * SEQ + row, RB), RB)
        back, product = norm_back(xb[img, pl.ds(row, RB)].astype(F32), acc[at], totals[0:1])
        xb[img, pl.ds(row, RB)] = (gh[at] + back).astype(BF)
        stat[0] += fold(product)

    @pl.loop(0, PIECES)
    def _(n):
        @pl.loop(0, IMG)
        def _(img):
            finish(img, pl.multiple_of(HALF * (1 - x) + PR * n, RB))

        piece(1, n).start()

    serve_next()

    @pl.loop(0, PIECES)
    def _(n):
        @pl.loop(0, IMG)
        def _(img):
            finish(img, pl.multiple_of(HALF * x + PR * n, RB))

    ig_c = pltpu.make_async_copy(xb.at[:, mine], ig_o.at[pl.ds(IMG * x, IMG)], misc_sem.at[31])
    ig_c.start()

    row = lax.broadcasted_iota(jnp.int32, (8, D), 0)
    small = jnp.where(row == 0, jnp.sum(stat[0], axis=0, keepdims=True),
                      jnp.where(row == 1, jnp.sum(stat[1], axis=0, keepdims=True),
                                jnp.tile(loss_i[...], (1, D // 128))))
    steps = (place.over_c(), place.over_y(), place.over_x())

    def small_sum(n):
        if 1 <= n <= 3:
            extra(sbuf.at[2 * n - 2], sbuf.at[2 * n - 1], 1 + n, steps[n - 1]).wait()
        value = small if n == 0 else sbuf[2 * n - 2] + sbuf[2 * n - 1] if n < 4 else None
        if n < 3:
            sbuf[2 * n] = value
            extra(sbuf.at[2 * n], sbuf.at[2 * n + 1], 2 + n, steps[n]).start()
        elif n == 3:
            stat_o[z] = value
            for j in range(1, H):
                extra(stat_o.at[z], stat_o.at[z], 4 + j, place.far(j)).start()
        else:
            for j in range(1, H):
                extra(stat_o.at[z], stat_o.at[lax.rem(z + H - j, H)], 4 + j, place.far(j)).wait()

    done = [before[i][len(CALLS)] for i in range(5)]
    for i in DRAIN:
        if i < 4:
            stages[i](jnp.int32(done[i]))
        else:
            small_sum(done[i])
        done[i] += 1
    assert done == [NCH] * 4 + [5] and place_no[0] == len(CALLS)

    ig_c.wait()
    for n in range(PIECES):
        piece(0, n).wait_recv()
        piece(1, n).wait()

    @pl.loop(NCH - SLOTS, NCH)
    def _(p):
        core_copy(p).wait_send()

    @pl.loop(0, NCH)
    def _(k):
        dw_copy(k).wait()
        for i in range(3):
            near_copy(q.at[k, x, :, yy], k, i, place.over_x()).wait_send()
        for j in range(1, H):
            far_copy(k, z, j).wait_send()


def backward(cfg, saved, krow):
    (wg, at, proj, lse, o, h, bnt, g, gp, gy, gm, gmt, out, xs, ts, totals, loss) = saved
    H, R = cfg["groups"], cfg["rows"]
    NQ, NO, NF = cfg["nq"], cfg["no"], cfg["nf"]
    NCH = NQ + NO + 2 * NF
    IMG, SEQ, D = xs.shape
    TOK = IMG * SEQ
    lhs = (2, D // 2, TOK)
    half = (2, H, 2, R, CW)
    vm = pltpu.VMEM
    dma = pltpu.SemaphoreType.DMA
    return pl.pallas_call(
        functools.partial(bwd_kernel, cfg),
        name="backward_reduce",
        out_shape=[
            jax.ShapeDtypeStruct((2 * IMG, SEQ // 2, D), BF), jax.ShapeDtypeStruct((2 * IMG, SEQ // 2, D), BF),
            jax.ShapeDtypeStruct((NCH, R, CW), F32), jax.ShapeDtypeStruct((H, 8, D), F32),
        ],
        in_specs=[any_spec()] * 14 + [vmem_spec()] * 3,
        out_specs=[any_spec()] * 3 + [vmem_spec()],
        scratch_shapes=[
            vm((NCH,) + half, BF), vm((SLOTS,) + half, BF), vm((SLOTS,) + half, BF),
            vm((NCH, 3, H, R, CW), BF), vm((NCH, H - 1, R, CW), BF), vm((NCH, R, CW), F32),
            vm((WSLOTS, 2, H, 2, 2, R, CW), BF), vm((2, 2, TOK, CW), BF), vm((2, 2, TOK, CW), BF),
            vm((2, TOK, CW), BF), vm((TOK, CW), F32), vm((TOK, D), BF), vm(lhs, BF), vm(lhs, BF),
            vm((TOK, D), F32), vm((TOK, D), F32), vm((TOK, D), F32), vm(o.shape, BF), vm(o.shape, BF),
            vm(proj.shape, BF), vm(lse.shape, F32), vm(xs.shape, BF), vm((2, 8, D), F32), vm((6, 8, D), F32),
            dma((NCH,)), dma((NCH,)), pltpu.SemaphoreType.REGULAR, dma((NCH, 3)), dma((NCH, 3)),
            dma((NCH, H - 1)), dma((NCH, H - 1)), dma((H + 4,)), dma((H + 4,)), dma((2, PIECES)), dma((2, PIECES)),
            dma((NCH,)), dma((NF, 2)), dma((32,)), dma((NCH,)),
        ],
        compiler_params=pltpu.CompilerParams(
            collective_id=1, has_side_effects=True, vmem_limit_bytes=63 * 2**20
        ),
    )(wg, at, proj, lse, o, h, bnt, g, gp, gy, gm, gmt, out, xs, totals, loss, krow)


def per_device(
    inputs, teacher, keep_mask, gain_attn, qkv_weight, out_weight, gain_mlp, up_weight, down_weight
):
    cfg = config(inputs, (qkv_weight, out_weight, up_weight, down_weight))
    R, NQ, NO, NF = cfg["rows"], cfg["nq"], cfg["no"], cfg["nf"]
    small, krow, kcol = prepare(inputs, keep_mask, gain_attn, gain_mlp)
    saved = forward(
        cfg, inputs, teacher, qkv_weight.reshape(R, -1), out_weight, up_weight, down_weight, small, krow, kcol
    )
    output, grad_in, dw, stats = backward(cfg, saved, krow)
    total = jnp.sum(stats, axis=0)
    start = lax.axis_index("dp") * R
    gains = lax.dynamic_slice(total, (0, start), (2, R))
    loss = total[2, 0] / saved[15][2, 0]
    qkv = dw[:NQ].reshape(NQ // 3, 3, R, CW).transpose(2, 1, 0, 3).reshape(qkv_weight.shape)

    def columns(first, count):
        return dw[first:first + count].transpose(1, 0, 2).reshape(R, count * CW)

    return (
        output,
        loss,
        grad_in.astype(F32),
        gains[0],
        qkv,
        columns(NQ, NO),
        gains[1],
        columns(NQ + NO, NF),
        columns(NQ + NO + NF, NF),
    )


def solution(mesh):
    rows = P("dp", "mp", None)
    weight = P("dp", "mp")
    qkv = P("dp", None, "mp")
    return jax.shard_map(
        per_device,
        mesh=mesh,
        in_specs=(rows, rows, P("dp", None), P("dp"), qkv, weight, P("dp"), weight, weight),
        out_specs=(rows, P(), rows, P("dp"), qkv, weight, P("dp"), weight, weight),
        check_vma=False,
    )
```

```python
import functools
import jax
import jax.numpy as jnp
from jax import lax
from jax.experimental import pallas as pl
from jax.experimental.pallas import tpu as pltpu
from jax.sharding import PartitionSpec as P

MESH = pl.DeviceIdType.MESH
HDIM = 64
CW = 256
EPS = 1e-06
F32 = jnp.float32
BF = jnp.bfloat16
PIECES = 5
BOTH_X = (0, 1, 2, 3, 4, 8, 10, 12, 14, 17)
Z_LAST = (6, 9, 16)
X_WITH = (0, 1, 2, 3, 4)
T_WITH = (10, 12, 14, 15, 17)
FWD_CALLS = (
    (0, 0, 0), (0, 0, 0), (0, 0), (1, 0, 1, 0, 1, 0, 2, 1, 0, 1, 0, 2, 3, 1, 1, 0, 0, 4, 2, 1, 0, 3, 4, 2, 1, 0), (3,), (2,),
    (4, 1), (), (), (), (3, 2, 2, 2, 0), (1, 1, 1),
    (4, 3, 2, 0, 0, 0), (2, 1), (), (4,), (3, 1, 0, 0, 4), (),
    (3, 3), (2, 2), (4, 1, 1), (), (4,), (3, 0),
    (2, 2), (4,), (1, 1), (2, 2, 1, 1, 3, 3, 3, 3, 4), (), (4,),
    (2,), (4,), (3, 1), (4,), (3,), (4,),
    (2, 2, 2), (4,), (2, 2, 1, 1), (3, 4), (), (2,),
    (3,), (3, 2, 3, 4), (3, 4), (3, 4), (3, 4), (4,),
    (3, 4), (3, 4), (4,),
)
NT = (((1,), (1,)), ((), ()))
NN = (((1,), (0,)), ((), ()))


def dot(a, b, dims=NN):
    return lax.dot_general(a, b, dims, preferred_element_type=F32)


class Place:
    def __init__(self, groups):
        self.groups = groups
        dp = lax.axis_index("dp")
        self.x = lax.axis_index("mp")
        self.c = lax.rem(dp, 2)
        self.y = lax.rem(dp // 2, 2)
        self.z = dp // 4

    def at(self, z, y, c, x):
        return {"dp": (z * 2 + y) * 2 + c, "mp": x}

    def far(self, j):
        return self.at(lax.rem(self.z + j, self.groups), self.y, self.c, self.x)

    def over_x(self):
        return self.at(self.z, self.y, self.c, 1 - self.x)

    def over_y(self):
        return self.at(self.z, 1 - self.y, self.c, self.x)

    def over_c(self):
        return self.at(self.z, self.y, 1 - self.c, self.x)

    def partners(self):
        return [self.far(j) for j in range(1, self.groups)] + [
            self.over_x(), self.over_y(), self.over_c()
        ]


def meet(place):
    barrier = pltpu.get_barrier_semaphore()
    partners = place.partners()
    for partner in partners:
        pl.semaphore_signal(barrier, 1, device_id=partner, device_id_type=MESH)
    pl.semaphore_wait(barrier, len(partners))


def member(k, numbers):
    if isinstance(k, int):
        return k in numbers
    found = False
    for n in numbers:
        found = (k == n) | found
    return found


def pick(table, index):
    value = jnp.int32(table[0])
    for n in range(1, len(table)):
        if table[n] != table[n - 1]:
            value = jnp.where(index >= n, table[n], value)
    return value


def when(cond, body):
    if isinstance(cond, bool):
        if cond:
            body()
    else:
        pl.when(cond)(body)


def fwd_kernel(cfg, xin, tin, wq, wo, wu, wd, small, krow, kcol, *refs):
    (wg_o, at_o, proj_o, lse_o, o_o, h_o, bnt_o, g_o, gp_o, gy_o, gm_o, gmt_o, out_o, xs_o, ts_o, sm_o, loss_o,
     wg, xs, ts, sm, a, proj, o, lse, h, bn, g, gp, zb, y, tb,
     local_sem, send_sem, recv_sem, extra_send, extra_recv, piece_send, piece_recv, out_sem, misc_sem) = refs
    H, R = cfg["groups"], cfg["rows"]
    NQ, NO, NF = cfg["nq"], cfg["no"], cfg["nf"]
    NCH = NQ + NO + 2 * NF
    IMG, SEQ, D = xs.shape
    HALF = SEQ // 2
    TOK = IMG * SEQ
    FH = wq.shape[1] // 3
    GRP = NQ // 3
    place = Place(H)
    x, yy, z, c = place.x, place.y, place.z, place.c
    scale = HDIM ** (-0.5)

    def remote(ref, k, i, device):
        return pltpu.make_async_remote_copy(
            ref, ref, send_sem.at[k, i], recv_sem.at[k, i], device_id=device, device_id_type=MESH
        )

    def source(k):
        if k < NQ:
            return wq.at[:, pl.ds((k % 3) * FH + (k // 3) * CW, CW)]
        if k < NQ + NO:
            return wo.at[:, pl.ds(CW * (k - NQ), CW)]
        if k < NQ + NO + NF:
            return wu.at[:, pl.ds(CW * (k - NQ - NO), CW)]
        return wd.at[:, pl.ds(CW * (k - NQ - NO - NF), CW)]

    def own(k):
        return pltpu.make_async_copy(source(k), wg.at[k, x, z, yy, c], local_sem.at[k])

    def own_wait(k):
        pltpu.make_async_copy(wq.at[:, pl.ds(0, CW)], wg.at[k, x, z, yy, c], local_sem.at[k]).wait()

    def relay(k):
        both = member(k, BOTH_X)
        first = jnp.where(both, 1, 1 - c) if not isinstance(both, bool) else (1 if both else 1 - c)
        xa = jnp.where(first == 1, 1 - x, x)
        ya = jnp.where(first == 1, yy, 1 - yy)
        return xa, ya, jnp.where(first == 1, x, 1 - x), jnp.where(first == 1, 1 - yy, yy)

    def either(k, late, early):
        last = member(k, Z_LAST)
        if isinstance(last, bool):
            (late if last else early)()
        else:
            pl.when(last)(late)
            pl.when(jnp.logical_not(last))(early)

    def s1(k):
        own_wait(k)
        own_block = wg.at[k, x, z, yy, c]
        xa, ya, xb, yb = relay(k)

        def late():
            remote(own_block, k, H - 1, place.at(z, ya, c, xa)).start()
            remote(own_block, k, H, place.at(z, yb, c, xb)).start()

        def early():
            for j in range(1, H):
                remote(own_block, k, j - 1, place.far(j)).start()

        either(k, late, early)

    def s2(k):
        xa, ya, xb, yb = relay(k)

        def late():
            block = wg.at[k, xa, z, ya, c]
            remote(block, k, H - 1, place.at(z, ya, c, xa)).wait_recv()
            remote(block, k, H + 1, place.at(z, yb, c, xb)).start()

        def early():
            for j in range(1, H):
                remote(wg.at[k, x, lax.rem(z + H - j, H), yy, c], k, j - 1, place.far(j)).wait_recv()
            piece_at(k)
            remote(wg.at[k, x, :, yy, c], k, H - 1, place.at(z, ya, c, xa)).start()
            remote(wg.at[k, x, :, yy, c], k, H, place.at(z, yb, c, xb)).start()

        either(k, late, early)

    def s3(k):
        xa, ya, xb, yb = relay(k)

        def late():
            remote(wg.at[k, xb, z, yb, c], k, H, place.at(z, yb, c, xb)).wait_recv()
            remote(wg.at[k, 1 - x, z, 1 - yy, c], k, H + 1, place.at(z, yb, c, xb)).wait_recv()
            for j in range(1, H):
                remote(wg.at[k, :, z, :, c], k, j - 1, place.far(j)).start()

        def early():
            remote(wg.at[k, xa, :, ya, c], k, H - 1, place.at(z, ya, c, xa)).wait_recv()
            remote(wg.at[k, xa, :, ya, c], k, H + 1, place.at(z, yb, c, xb)).start()

        either(k, late, early)

    def s4(k):
        xa, ya, xb, yb = relay(k)

        def late():
            for j in range(1, H):
                remote(wg.at[k, :, lax.rem(z + H - j, H), :, c], k, j - 1, place.far(j)).wait_recv()

        def early():
            remote(wg.at[k, xb, :, yb, c], k, H, place.at(z, yb, c, xb)).wait_recv()
            remote(wg.at[k, 1 - x, :, 1 - yy, c], k, H + 1, place.at(z, yb, c, xb)).wait_recv()

        either(k, late, early)
        remote(wg.at[k, :, :, :, c], k, H + 2, place.over_c()).start()

    def keep_chunk(k):
        return pltpu.make_async_copy(wg.at[k], wg_o.at[k], out_sem.at[k])

    def s5(k):
        remote(wg.at[k, :, :, :, 1 - c], k, H + 2, place.over_c()).wait_recv()
        keep_chunk(k).start()

    PR = HALF // PIECES

    def piece(i, n, to):
        src, dst = ((xin, xs), (tin, ts))[i]
        return pltpu.make_async_remote_copy(
            src.at[pl.ds(IMG * (1 - x), IMG), pl.ds(PR * n, PR)], dst.at[:, pl.ds(HALF * to + PR * n, PR)],
            piece_send.at[i, n], piece_recv.at[i, n], device_id=place.over_x(), device_id_type=MESH
        )

    def piece_at(k):
        for i, chunks in enumerate((X_WITH, T_WITH)):
            for n, chunk_no in enumerate(chunks):
                when(k == chunk_no, lambda i=i, n=n: piece(i, n, x).start())

    def pieces_in(i):
        for n in range(PIECES):
            piece(i, n, 1 - x).wait_recv()

    stages = (s1, s2, s3, s4, s5)
    pos = [0] * 5
    place_no = [0]

    def serve():
        for i in FWD_CALLS[place_no[0]]:
            stages[i](pos[i])
            pos[i] += 1
        place_no[0] += 1

    def serve_in(index, calls, starts):
        for i in (4, 3, 2, 1, 0):
            counts = [call.count(i) for call in calls]
            if max(counts):
                first = pick(starts[i], index)

                @pl.loop(first, first + pick(counts, index))
                def _(n, i=i):
                    stages[i](n)

    def served(count):
        calls = FWD_CALLS[place_no[0]:place_no[0] + count]
        place_no[0] += count
        starts = [[pos[i] + sum(call.count(i) for call in calls[:n]) for n in range(count)] for i in range(5)]
        for i in range(5):
            pos[i] += sum(call.count(i) for call in calls)
        return calls, starts

    kept = []

    def keep(src, dst):
        copy = pltpu.make_async_copy(src, dst, misc_sem.at[len(kept)])
        copy.start()
        kept.append(copy)

    def extra(src, dst, i, device):
        return pltpu.make_async_remote_copy(
            src, dst, extra_send.at[i], extra_recv.at[i], device_id=device, device_id_type=MESH
        )

    for k in range(NCH):
        own(k).start()
    mine = pl.ds(HALF * x, HALF)
    xl = pltpu.make_async_copy(xin.at[pl.ds(IMG * x, IMG)], xs.at[:, mine], misc_sem.at[30])
    tl = pltpu.make_async_copy(tin.at[pl.ds(IMG * x, IMG)], ts.at[:, mine], misc_sem.at[31])
    sl = pltpu.make_async_copy(small, sm.at[z, yy, c], misc_sem.at[29])
    xl.start()
    tl.start()
    sl.start()
    meet(place)
    sl.wait()
    for j in range(1, H):
        extra(sm.at[z, yy, c], sm.at[z, yy, c], 3 + j, place.far(j)).start()
    serve()
    for j in range(1, H):
        extra(sm.at[z, yy, c], sm.at[lax.rem(z + H - j, H), yy, c], 3 + j, place.far(j)).wait_recv()
    extra(sm.at[:, yy, c], sm.at[:, yy, c], 2, place.over_y()).start()
    serve()
    extra(sm.at[:, 1 - yy, c], sm.at[:, 1 - yy, c], 2, place.over_y()).wait_recv()
    extra(sm.at[:, :, c], sm.at[:, :, c], 3, place.over_c()).start()
    serve()
    extra(sm.at[:, :, 1 - c], sm.at[:, :, 1 - c], 3, place.over_c()).wait_recv()
    totals = jnp.sum(sm[...].reshape(H * 4, 8, D), axis=0)
    sm_o[...] = totals
    xl.wait()
    serve()
    pieces_in(0)
    keep(xs, xs_o)

    RB = 32

    def rows_of(ref, r):
        per = SEQ // RB
        return ref[r // per, pl.ds(pl.multiple_of(lax.rem(r, per) * RB, RB), RB)]

    def norm_to(values, gain):
        centre = values - jnp.mean(values, axis=-1, keepdims=True)
        spread = jnp.mean(centre * centre, axis=-1, keepdims=True)
        return (centre * lax.rsqrt(spread + EPS) * gain).astype(BF)

    for part in range(2):
        count = TOK // RB // 2

        @pl.loop(part * count, (part + 1) * count)
        def _(r):
            a[pl.ds(pl.multiple_of(r * RB, RB), RB)] = norm_to(rows_of(xs, r).astype(F32), sm_o[0:1])

        serve()

    def transposed(src, dst):
        @pl.loop(0, D // 128)
        def _(d):
            t = jnp.transpose(src[:, pl.ds(pl.multiple_of(d * 128, 128), 128)].astype(F32))
            t = t.reshape(64 // R, 2, R, TOK)
            for p in range(2):
                dst[p, pl.ds(pl.multiple_of(d * 64, 64), 64)] = t[:, p].reshape(64, TOK).astype(BF)

    transposed(a, tb)
    keep(tb, at_o)
    serve()

    def chunk(k, half):
        return wg[k, half].reshape(D, CW)

    def project(k):
        @pl.loop(0, 2)
        def _(half):
            proj[k, half] = dot(a[...], chunk(k, half)).astype(BF).reshape(IMG, SEQ, CW)

    lane = lax.broadcasted_iota(jnp.int32, (SEQ, CW), 1) // HDIM

    def attend(group, u):
        half, i = u // IMG, lax.rem(u, IMG)
        q = proj[3 * group, half, i]
        key = proj[3 * group + 1, half, i]
        val = proj[3 * group + 2, half, i]
        allowed = krow[IMG * x + i, 0:1] > 0
        total = jnp.zeros((SEQ, CW), F32)
        logs = jnp.zeros((SEQ, 128), F32)
        spot = lax.broadcasted_iota(jnp.int32, (SEQ, 128), 1)
        for head in range(CW // HDIM):
            scores = dot(jnp.where(lane == head, q, 0), key, NT) * scale
            scores = jnp.where(allowed, scores, -1e30)
            top = jnp.max(scores, axis=-1, keepdims=True)
            raised = jnp.exp(scores - top)
            norm = jnp.sum(raised, axis=-1, keepdims=True)
            soft = (raised / norm).astype(BF)
            total = total + dot(soft, jnp.where(lane == head, val, 0))
            logs = jnp.where(spot == head, top + jnp.log(norm), logs)
        o[group, half, i] = total.astype(BF)
        lse[group, half, i] = logs

    for group in range(GRP):
        for k in range(3 * group, 3 * group + 3):
            serve()
            project(k)
        places = served(2 * IMG)

        @pl.loop(0, 2 * IMG)
        def _(u, group=group, places=places):
            serve_in(u, *places)
            attend(group, u)

    keep(proj, proj_o)
    keep(lse, lse_o)
    keep(o, o_o)

    def gathered(src, k, half):
        return src[k, half].reshape(TOK, CW)

    h[...] = xs[...].reshape(TOK, D).astype(F32)
    for k in range(NO):
        serve()

        @pl.loop(0, 2)
        def _(half, k=k):
            h[...] += dot(gathered(o, k, half), chunk(NQ + k, half), NT)

    keep(h, h_o)

    for part in range(2):
        count = TOK // RB // 2
        serve()

        @pl.loop(part * count, (part + 1) * count)
        def _(r):
            at = pl.ds(pl.multiple_of(r * RB, RB), RB)
            bn[at] = norm_to(h[at], sm_o[1:2])

    first_up = NQ + NO

    def gelu(k, half):
        GB = 64

        @pl.loop(0, TOK // GB)
        def _(r):
            at = pl.ds(pl.multiple_of(r * GB, GB), GB)
            v = zb[at]
            cdf = 0.5 * (1.0 + lax.erf(v * 0.7071067811865476))
            g[k, half, at] = (v * cdf).astype(BF)
            gp[k, half, at] = (cdf + v * (jnp.exp(-0.5 * (v * v)) * 0.3989422804014327)).astype(BF)

    for k in range(NF):
        for half in range(2):
            serve()
            zb[...] = dot(bn[...], chunk(first_up + k, half))
            gelu(k, half)
    keep(g, g_o)
    keep(gp, gp_o)
    first_down = first_up + NF
    kept[1].wait()
    serve()
    transposed(bn, tb)
    keep(tb, bnt_o)
    serve()
    y[...] = h[...]

    for k in range(NF):
        serve()

        @pl.loop(0, 2)
        def _(half, k=k):
            y[...] += dot(g[k, half], chunk(first_down + k, half), NT)

    assert pos == [NCH] * 5 and place_no[0] == len(FWD_CALLS)
    tl.wait()
    pieces_in(1)
    keep(ts, ts_o)
    zb[0:RB, 0:128] = jnp.zeros((RB, 128), F32)
    factor = 2.0 * cfg["tokens"] / sm_o[2:3]
    xs_ref = xs

    for copy in kept[:1]:
        copy.wait()

    @pl.loop(0, TOK // RB)
    def _(r):
        at = pl.ds(pl.multiple_of(r * RB, RB), RB)
        per = SEQ // RB
        img, pos = r // per, pl.multiple_of(lax.rem(r, per) * RB, RB)
        res = y[at]
        kept_rows = jnp.tile(kcol[IMG * x + img, pl.ds(pos, RB)], (1, D // 128))
        xs_ref[img, pl.ds(pos, RB)] = (res * kept_rows).astype(BF)
        error = res - ts[img, pl.ds(pos, RB)].astype(F32)
        squares = error * error * kept_rows
        part = squares[:, 0:128]
        for n in range(1, D // 128):
            part = part + squares[:, n * 128:(n + 1) * 128]
        zb[0:RB, 0:128] += part
        grad = factor * kept_rows * error
        y[at] = grad
        a[at] = grad.astype(BF)

    loss_o[...] = jnp.zeros_like(loss_o) + jnp.sum(zb[0:RB, 0:128]) * (1.0 / D)
    keep(xs, out_o)
    keep(y, gy_o)
    keep(a, gm_o)
    kept[8].wait()
    transposed(a, tb)
    keep(tb, gmt_o)
    for n, copy in enumerate(kept):
        if n not in (0, 1, 8):
            copy.wait()
    for i in range(2):
        for n in range(PIECES):
            piece(i, n, x).wait_send()
    for j in range(1, H):
        extra(sm.at[z, yy, c], sm.at[z, yy, c], 3 + j, place.far(j)).wait_send()
    extra(sm.at[:, yy, c], sm.at[:, yy, c], 2, place.over_y()).wait_send()
    extra(sm.at[:, :, c], sm.at[:, :, c], 3, place.over_c()).wait_send()

    @pl.loop(0, NCH)
    def _(k):
        keep_chunk(k).wait()

        def late():
            for j in range(1, H):
                remote(wg.at[k, :, z, :, c], k, j - 1, place.far(j)).wait_send()
            for i in (H - 1, H, H + 1):
                remote(wg.at[k, x, z, yy, c], k, i, place.over_x()).wait_send()

        def early():
            for j in range(1, H):
                remote(wg.at[k, x, z, yy, c], k, j - 1, place.far(j)).wait_send()
            for i in (H - 1, H, H + 1):
                remote(wg.at[k, x, :, yy, c], k, i, place.over_x()).wait_send()

        either(k, late, early)
        remote(wg.at[k, :, :, :, c], k, H + 2, place.over_c()).wait_send()


def any_spec():
    return pl.BlockSpec(memory_space=pl.ANY)


def vmem_spec():
    return pl.BlockSpec(memory_space=pltpu.VMEM)


def forward(cfg, xin, tin, wq, wo, wu, wd, small, krow, kcol):
    H, R = cfg["groups"], cfg["rows"]
    NQ, NO, NF = cfg["nq"], cfg["no"], cfg["nf"]
    NCH = NQ + NO + 2 * NF
    IMG = xin.shape[0] // 2
    SEQ, D = 2 * xin.shape[1], xin.shape[2]
    TOK = IMG * SEQ
    GRP = NQ // 3
    wg = (NCH, 2, H, 2, 2, R, CW)
    lhs = (2, D // 2, TOK)
    big = (NF, 2, TOK, CW)
    shapes = [
        (wg, BF), (lhs, BF), ((NQ, 2, IMG, SEQ, CW), BF), ((GRP, 2, IMG, SEQ, 128), F32),
        ((GRP, 2, IMG, SEQ, CW), BF), ((TOK, D), F32), (lhs, BF), (big, BF), (big, BF),
        ((TOK, D), F32), ((TOK, D), BF), (lhs, BF), ((IMG, SEQ, D), BF), ((IMG, SEQ, D), BF), ((IMG, SEQ, D), BF),
        ((8, D), F32), ((8, 128), F32),
    ]
    return pl.pallas_call(
        functools.partial(fwd_kernel, cfg),
        name="gather_forward",
        out_shape=[jax.ShapeDtypeStruct(s, t) for s, t in shapes],
        in_specs=[any_spec()] * 7 + [vmem_spec()] * 2,
        out_specs=[any_spec()] * 15 + [vmem_spec()] * 2,
        scratch_shapes=[
            pltpu.VMEM(wg, BF), pltpu.VMEM((IMG, SEQ, D), BF), pltpu.VMEM((IMG, SEQ, D), BF),
            pltpu.VMEM((H, 2, 2, 8, D), F32), pltpu.VMEM((TOK, D), BF),
            pltpu.VMEM((NQ, 2, IMG, SEQ, CW), BF), pltpu.VMEM((GRP, 2, IMG, SEQ, CW), BF),
            pltpu.VMEM((GRP, 2, IMG, SEQ, 128), F32), pltpu.VMEM((TOK, D), F32), pltpu.VMEM((TOK, D), BF),
            pltpu.VMEM(big, BF), pltpu.VMEM(big, BF), pltpu.VMEM((TOK, CW), F32), pltpu.VMEM((TOK, D), F32),
            pltpu.VMEM(lhs, BF),
            pltpu.SemaphoreType.DMA((NCH,)), pltpu.SemaphoreType.DMA((NCH, H + 3)),
            pltpu.SemaphoreType.DMA((NCH, H + 3)), pltpu.SemaphoreType.DMA((H + 4,)),
            pltpu.SemaphoreType.DMA((H + 4,)), pltpu.SemaphoreType.DMA((2, PIECES)),
            pltpu.SemaphoreType.DMA((2, PIECES)), pltpu.SemaphoreType.DMA((NCH,)), pltpu.SemaphoreType.DMA((32,)),
        ],
        compiler_params=pltpu.CompilerParams(
            collective_id=0, has_side_effects=True, vmem_limit_bytes=63 * 2**20
        ),
    )(xin, tin, wq, wo, wu, wd, small, krow, kcol)


def config(inputs, weights):
    rows = weights[0].shape[0]
    dps = lax.axis_size("dp")
    return {
        "groups": dps // 4,
        "rows": rows,
        "nq": weights[0].shape[1] * weights[0].shape[2] // CW,
        "no": weights[1].shape[1] // CW,
        "nf": weights[2].shape[1] // CW,
        "tokens": float(inputs.shape[0] * inputs.shape[1] * dps * lax.axis_size("mp")),
    }


def prepare(inputs, keep_mask, gain_attn, gain_mlp):
    R, D = gain_attn.shape[0], inputs.shape[2]
    dps = D // R
    here = lax.broadcasted_iota(jnp.int32, (1, D), 1) // R == lax.axis_index("dp")
    count = jnp.sum(keep_mask).astype(F32)
    small = jnp.concatenate(
        [
            jnp.where(here, jnp.tile(gain_attn.astype(F32), dps)[None], 0.0),
            jnp.where(here, jnp.tile(gain_mlp.astype(F32), dps)[None], 0.0),
            jnp.full((6, D), count, F32),
        ],
        axis=0,
    )
    mask = keep_mask.astype(F32)
    krow = jnp.broadcast_to(mask[:, None, :], (mask.shape[0], 8, mask.shape[1]))
    kcol = jnp.broadcast_to(mask[:, :, None], mask.shape + (128,))
    return small, krow, kcol


SLOTS = 3
WSLOTS = 4
CALLS = (
    (0, 0, 0, 0, 0), (0, 0, 0, 0, 0), (0, 0, 0, 0, 0), (1, 0, 0, 0, 0), (0, 0, 0, 0, 0),
    (1, 0, 0, 0, 0), (0, 0, 0, 0, 0), (1, 0, 0, 0, 0), (0, 1, 0, 0, 0), (1, 0, 0, 0, 0),
    (0, 1, 0, 0, 0), (1, 0, 0, 0, 0), (0, 0, 0, 0, 0), (1, 0, 0, 0, 0), (0, 1, 0, 0, 0),
    (1, 0, 0, 0, 0), (0, 0, 0, 0, 0), (1, 0, 0, 0, 0), (0, 0, 2, 0, 0), (1, 1, 1, 0, 0),
    (1, 0, 0, 0, 0), (0, 0, 0, 0, 0), (0, 0, 0, 0, 0), (1, 1, 0, 1, 0), (0, 0, 0, 0, 0),
    (1, 0, 0, 1, 0), (0, 0, 0, 0, 0), (1, 1, 1, 1, 0), (1, 0, 0, 0, 0), (0, 1, 0, 0, 0),
    (0, 0, 0, 0, 0), (1, 1, 0, 0, 0), (1, 0, 0, 1, 0), (0, 1, 1, 0, 0), (0, 1, 0, 0, 0),
    (0, 0, 0, 0, 0), (0, 0, 0, 0, 0), (1, 0, 0, 0, 0), (0, 1, 0, 0, 0), (1, 0, 3, 1, 0),
    (0, 1, 3, 0, 0), (0, 1, 0, 1, 0), (0, 1, 1, 1, 0), (0, 0, 0, 0, 0), (0, 0, 1, 1, 0),
    (0, 1, 0, 0, 0), (1, 0, 0, 1, 0), (1, 0, 1, 0, 0), (1, 1, 0, 1, 0), (0, 1, 1, 1, 0),
    (0, 0, 1, 1, 0), (0, 1, 1, 1, 0), (0, 1, 0, 2, 0), (0, 0, 0, 0, 0), (0, 1, 1, 1, 0),
    (0, 0, 0, 0, 0), (1, 0, 0, 1, 0), (1, 0, 1, 0, 0), (1, 1, 1, 0, 0), (0, 1, 0, 1, 0),
)
DRAIN = (
    3, 2, 1, 4, 3, 4, 1, 3, 4, 2, 2, 2, 4, 3, 3, 3, 4,
)
OUT_FIRST = 1


def bwd_kernel(cfg, wg, at_i, proj_i, lse_i, o_i, h_i, bnt_i, g_i, gp_i, gy_i, gm_i, gmt_i, out_i, xs_i,
               totals, loss_i, krow, *refs):
    (out_o, ig_o, dw_o, stat_o,
     q, snd, rcv, near, farr, dw, wb, gb_buf, gpb, gz, zb, gm, lhs1, lhs2, acc, gh, h, o, go, proj, lse, xb, stat, sbuf,
     core_send, core_recv, credit, near_send, near_recv, far_send, far_recv, extra_send, extra_recv, piece_send, piece_recv,
     wsem, gsem, misc_sem, dw_sem) = refs
    H, R = cfg["groups"], cfg["rows"]
    NQ, NO, NF = cfg["nq"], cfg["no"], cfg["nf"]
    NCH = NQ + NO + 2 * NF
    IMG, SEQ, D = xb.shape
    HALF = SEQ // 2
    TOK = IMG * SEQ
    GRP = NQ // 3
    place = Place(H)
    x, yy, z, c = place.x, place.y, place.z, place.c
    scale = HDIM ** (-0.5)

    def ident(p):
        ff = jnp.where(lax.rem(p, 2) == 0, NQ + NO + NF + p // 2, NQ + NO + p // 2)
        return jnp.where(p < 2 * NF, ff, jnp.where(p < 2 * NF + NO, p - 2 * NF + NQ, p - 2 * NF - NO))

    def relay(p):
        both = (p >= OUT_FIRST) & (p < OUT_FIRST + PIECES)
        first = jnp.where(both, 1, 1 - c)
        xa = jnp.where(first == 1, 1 - x, x)
        ya = jnp.where(first == 1, yy, 1 - yy)
        return xa, ya, jnp.where(first == 1, x, 1 - x), jnp.where(first == 1, 1 - yy, yy)

    loads = []

    def load(src, dst):
        copy = pltpu.make_async_copy(src, dst, misc_sem.at[len(loads)])
        copy.start()
        loads.append(copy)
        return copy

    def wload(n):
        return pltpu.make_async_copy(wg.at[ident(n)], wb.at[lax.rem(n, WSLOTS)], wsem.at[n])

    def gload(j):
        s = lax.rem(j, 2)
        return (pltpu.make_async_copy(g_i.at[j], gb_buf.at[s], gsem.at[j, 0]),
                pltpu.make_async_copy(gp_i.at[j], gpb.at[s], gsem.at[j, 1]))

    gm_l = load(gm_i, gm)
    gmt_l = load(gmt_i, lhs1)
    for j in range(2):
        for copy in gload(jnp.int32(j)):
            copy.start()
    for n in range(WSLOTS):
        wload(jnp.int32(n)).start()
    bnt_l = load(bnt_i, lhs2)
    out_l = load(out_i, xb)
    gy_l = load(gy_i, gh)
    h_l = load(h_i, h)
    o_l = load(o_i, o)
    proj_l = load(proj_i, proj)
    lse_l = load(lse_i, lse)

    def extra(src, dst, i, device):
        return pltpu.make_async_remote_copy(
            src, dst, extra_send.at[i], extra_recv.at[i], device_id=device, device_id_type=MESH
        )

    meet(place)

    def core_copy(p, start=False):
        s = lax.rem(p, SLOTS)
        return pltpu.make_async_remote_copy(
            snd.at[s], rcv.at[s], core_send.at[p], core_recv.at[p], device_id=place.over_c(), device_id_type=MESH
        )

    def near_copy(src, k, i, device):
        return pltpu.make_async_remote_copy(
            src, near.at[k, i], near_send.at[k, i], near_recv.at[k, i], device_id=device, device_id_type=MESH
        )

    def far_copy(k, zd, j):
        return pltpu.make_async_remote_copy(
            q.at[k, x, zd, yy], farr.at[k, j - 1], far_send.at[k, j - 1], far_recv.at[k, j - 1],
            device_id=place.far(j), device_id_type=MESH
        )

    def produce(p, lhs, rhs):
        k = ident(p)
        s = lax.rem(p, SLOTS)
        pl.when(p >= SLOTS)(lambda: core_copy(p - SLOTS).wait_send())

        @pl.loop(0, 2)
        def _(half):
            snd[s, half] = dot(lhs[1 - c], rhs(half)).astype(BF).reshape(H, 2, R, CW)
            q[k, half] = dot(lhs[c], rhs(half)).astype(BF).reshape(H, 2, R, CW)

        pl.when(p >= SLOTS)(lambda: pl.semaphore_wait(credit, 1))
        core_copy(p).start()

    def added(k, xi, yi, others):
        @pl.loop(0, H)
        def _(n):
            total = q[k, xi, n, yi].astype(F32)
            for other in others:
                total = total + near[k, other, n].astype(F32)
            q[k, xi, n, yi] = total.astype(BF)

    def r1(p):
        k = ident(p)
        s = lax.rem(p, SLOTS)
        core_copy(p).wait_recv()

        @pl.loop(0, 2 * H)
        def _(n):
            i, m = n // H, lax.rem(n, H)
            for y2 in range(2):
                q[k, i, m, y2] = (q[k, i, m, y2].astype(F32) + rcv[s, i, m, y2].astype(F32)).astype(BF)

        pl.when(p + SLOTS < NCH)(
            lambda: pl.semaphore_signal(credit, 1, device_id=place.over_c(), device_id_type=MESH)
        )
        xa, ya, xo, yo = relay(p)
        near_copy(q.at[k, 1 - x, :, 1 - yy], k, 0, place.at(z, yo, c, xo)).start()
        near_copy(q.at[k, xo, :, yo], k, 1, place.at(z, yo, c, xo)).start()

    def r2(p):
        k = ident(p)
        xa, ya, xo, yo = relay(p)
        near_copy(q.at[k, 1 - x, :, 1 - yy], k, 0, place.at(z, yo, c, xo)).wait_recv()
        added(k, xa, ya, (0,))
        near_copy(q.at[k, xa, :, ya], k, 2, place.at(z, ya, c, xa)).start()

    def r3(p):
        k = ident(p)
        xa, ya, xo, yo = relay(p)
        near_copy(q.at[k, xo, :, yo], k, 1, place.at(z, yo, c, xo)).wait_recv()
        near_copy(q.at[k, xa, :, ya], k, 2, place.at(z, ya, c, xa)).wait_recv()
        added(k, x, yy, (1, 2))
        for j in range(1, H):
            far_copy(k, lax.rem(z + j, H), j).start()

    def dw_copy(k):
        return pltpu.make_async_copy(dw.at[k], dw_o.at[k], dw_sem.at[k])

    def r4(p):
        k = ident(p)
        total = q[k, x, z, yy].astype(F32)
        for j in range(1, H):
            far_copy(k, lax.rem(z + j, H), j).wait_recv()
            total = total + farr[k, j - 1].astype(F32)
        dw[k] = total
        dw_copy(k).start()

    stages = (r1, r2, r3, r4)

    before = [[sum(call[i] for call in CALLS[:n]) for n in range(len(CALLS) + 1)] for i in range(5)]
    place_no = [0]

    def serve(numbers, index=None):
        for i in (3, 2, 1, 0):
            counts = [CALLS[n][i] for n in numbers]
            starts = [before[i][n] for n in numbers]
            if index is None:
                for n in range(counts[0]):
                    stages[i](jnp.int32(starts[0] + n))
            elif max(counts) == 1:
                pl.when(pick(counts, index) > 0)(lambda i=i, starts=starts: stages[i](pick(starts, index)))
            elif max(counts) > 1:
                first = pick(starts, index)

                @pl.loop(first, first + pick(counts, index))
                def _(n, i=i):
                    stages[i](n)

    def serve_next():
        serve([place_no[0]])
        place_no[0] += 1

    gm_l.wait()
    gmt_l.wait()
    bnt_l.wait()

    def wchunk(n, half):
        return wb[lax.rem(n, WSLOTS), half].reshape(D, CW)

    def wnext(n):
        pl.when(n + WSLOTS < NCH)(lambda: wload(n + WSLOTS).start())

    GB = 64
    PR = HALF // PIECES
    mine = pl.ds(HALF * x, HALF)

    def piece(i, n):
        return pltpu.make_async_remote_copy(
            xb.at[:, pl.ds(HALF * (1 - x) + PR * n, PR)],
            (out_o, ig_o)[i].at[pl.ds(IMG * x, IMG), pl.ds(PR * n, PR)],
            piece_send.at[i, n], piece_recv.at[i, n], device_id=place.over_x(), device_id_type=MESH
        )

    acc[...] = jnp.zeros_like(acc)
    out_l.wait()
    out_c = pltpu.make_async_copy(xb.at[:, mine], out_o.at[pl.ds(IMG * x, IMG)], misc_sem.at[30])
    out_c.start()

    @pl.loop(0, NF)
    def _(j):
        s = lax.rem(j, 2)
        pl.when(j < PIECES)(lambda: piece(0, j).start())
        gl, gpl = gload(j)
        gl.wait()
        produce(2 * j, lhs1, lambda half: gb_buf[s, half])
        serve([4 * n for n in range(NF)], j)
        gpl.wait()
        wload(2 * j).wait()

        @pl.loop(0, 2)
        def _(half):
            zb[...] = dot(gm[...], wchunk(2 * j, half))

            @pl.loop(0, TOK // GB)
            def _(r):
                at = pl.ds(pl.multiple_of(r * GB, GB), GB)
                gz[half, at] = (zb[at] * gpb[s, half, at].astype(F32)).astype(BF)

        wnext(2 * j)

        @pl.when(j + 2 < NF)
        def _():
            for copy in gload(j + 2):
                copy.start()

        serve([4 * n + 1 for n in range(NF)], j)
        produce(2 * j + 1, lhs2, lambda half: gz[half])
        serve([4 * n + 2 for n in range(NF)], j)
        wload(2 * j + 1).wait()

        @pl.loop(0, 2)
        def _(half):
            acc[...] += dot(gz[half], wchunk(2 * j + 1, half), NT)

        wnext(2 * j + 1)
        serve([4 * n + 3 for n in range(NF)], j)

    place_no[0] = 4 * NF
    RB = 32

    def norm_back(values, grad, gain):
        centre = values - jnp.mean(values, axis=-1, keepdims=True)
        spread = jnp.mean(centre * centre, axis=-1, keepdims=True)
        scaled = lax.rsqrt(spread + EPS)
        unit = centre * scaled
        e = grad * gain
        first = jnp.mean(e, axis=-1, keepdims=True)
        second = jnp.mean(e * unit, axis=-1, keepdims=True)
        return scaled * (e - first - unit * second), grad * unit

    def fold(v):
        return jnp.sum(v.reshape(RB // 8, 8, D), axis=0)

    base = 2 * NF
    stat[...] = jnp.zeros_like(stat)
    gy_l.wait()
    h_l.wait()

    for part in range(2):
        count = TOK // RB // 2

        @pl.loop(part * count, (part + 1) * count)
        def _(r):
            at = pl.ds(pl.multiple_of(r * RB, RB), RB)
            back, product = norm_back(h[at], acc[at], totals[1:2])
            total = gh[at] + back
            gh[at] = total
            gm[at] = total.astype(BF)
            stat[1] += fold(product)

        serve_next()

    def transposed(src, dst):
        @pl.loop(0, D // 128)
        def _(d):
            t = jnp.transpose(src[:, pl.ds(pl.multiple_of(d * 128, 128), 128)].astype(F32))
            t = t.reshape(64 // R, 2, R, TOK)
            for p in range(2):
                dst[p, pl.ds(pl.multiple_of(d * 64, 64), 64)] = t[:, p].reshape(64, TOK).astype(BF)

    at_l = load(at_i, lhs2)
    transposed(gm, lhs1)
    o_l.wait()
    for k in range(NO):
        produce(jnp.int32(base + k), lhs1, lambda half, k=k: o[k, half].reshape(TOK, CW))
        serve_next()
        wload(jnp.int32(base + k)).wait()

        @pl.loop(0, 2)
        def _(half, k=k):
            go[k, half] = dot(gm[...], wchunk(jnp.int32(base + k), half)).astype(BF).reshape(IMG, SEQ, CW)

        wnext(jnp.int32(base + k))
        serve_next()
    proj_l.wait()
    lse_l.wait()
    lane = lax.broadcasted_iota(jnp.int32, (SEQ, CW), 1) // HDIM
    TN = (((0,), (0,)), ((), ()))

    def attend_back(group, u):
        half, i = u // IMG, lax.rem(u, IMG)
        qr, kr, vr = 3 * group, 3 * group + 1, 3 * group + 2
        query, key, val = proj[qr, half, i], proj[kr, half, i], proj[vr, half, i]
        grad = go[group, half, i]
        logs = lse[group, half, i]
        allowed = krow[IMG * x + i, 0:1] > 0
        gq = jnp.zeros((SEQ, CW), F32)
        gk = jnp.zeros((SEQ, CW), F32)
        gv = jnp.zeros((SEQ, CW), F32)
        for head in range(CW // HDIM):
            of_head = lane == head
            qm = jnp.where(of_head, query, 0)
            gom = jnp.where(of_head, grad, 0)
            scores = jnp.where(allowed, dot(qm, key, NT) * scale, -1e30)
            soft = jnp.exp(scores - logs[:, head:head + 1])
            gsoft = dot(gom, val, NT)
            inner = jnp.sum(gsoft * soft, axis=-1, keepdims=True)
            gs = (soft * (gsoft - inner)).astype(BF)
            gq = gq + dot(gs, jnp.where(of_head, key, 0))
            gk = gk + dot(gs, qm, TN)
            gv = gv + dot(soft.astype(BF), gom, TN)
        proj[qr, half, i] = (gq * scale).astype(BF)
        proj[kr, half, i] = (gk * scale).astype(BF)
        proj[vr, half, i] = gv.astype(BF)

    acc[...] = jnp.zeros_like(acc)
    at_l.wait()
    out_c.wait()
    for n in range(PIECES):
        piece(0, n).wait_send()
    xs_l = load(xs_i, xb)

    for group in range(GRP):
        numbers = [place_no[0] + u for u in range(2 * IMG)]
        place_no[0] += 2 * IMG

        @pl.loop(0, 2 * IMG)
        def _(u, numbers=numbers, group=group):
            serve(numbers, u)
            attend_back(group, u)

        for k in range(3 * group, 3 * group + 3):
            serve_next()
            produce(jnp.int32(base + NO + k), lhs2, lambda half, k=k: proj[k, half].reshape(TOK, CW))

        for k in range(3 * group, 3 * group + 3):
            p = base + NO + k
            serve_next()
            wload(jnp.int32(p)).wait()

            @pl.loop(0, 2)
            def _(half, k=k, p=p):
                acc[...] += dot(proj[k, half].reshape(TOK, CW), wchunk(jnp.int32(p), half), NT)

            wnext(jnp.int32(p))

    xs_l.wait()
    serve_next()
    per = SEQ // RB

    def finish(img, row):
        at = pl.ds(pl.multiple_of(img * SEQ + row, RB), RB)
        back, product = norm_back(xb[img, pl.ds(row, RB)].astype(F32), acc[at], totals[0:1])
        xb[img, pl.ds(row, RB)] = (gh[at] + back).astype(BF)
        stat[0] += fold(product)

    @pl.loop(0, PIECES)
    def _(n):
        @pl.loop(0, IMG)
        def _(img):
            finish(img, pl.multiple_of(HALF * (1 - x) + PR * n, RB))

        piece(1, n).start()

    serve_next()

    @pl.loop(0, PIECES)
    def _(n):
        @pl.loop(0, IMG)
        def _(img):
            finish(img, pl.multiple_of(HALF * x + PR * n, RB))

    ig_c = pltpu.make_async_copy(xb.at[:, mine], ig_o.at[pl.ds(IMG * x, IMG)], misc_sem.at[31])
    ig_c.start()

    row = lax.broadcasted_iota(jnp.int32, (8, D), 0)
    small = jnp.where(row == 0, jnp.sum(stat[0], axis=0, keepdims=True),
                      jnp.where(row == 1, jnp.sum(stat[1], axis=0, keepdims=True),
                                jnp.tile(loss_i[...], (1, D // 128))))
    steps = (place.over_c(), place.over_y(), place.over_x())

    def small_sum(n):
        if 1 <= n <= 3:
            extra(sbuf.at[2 * n - 2], sbuf.at[2 * n - 1], 1 + n, steps[n - 1]).wait()
        value = small if n == 0 else sbuf[2 * n - 2] + sbuf[2 * n - 1] if n < 4 else None
        if n < 3:
            sbuf[2 * n] = value
            extra(sbuf.at[2 * n], sbuf.at[2 * n + 1], 2 + n, steps[n]).start()
        elif n == 3:
            stat_o[z] = value
            for j in range(1, H):
                extra(stat_o.at[z], stat_o.at[z], 4 + j, place.far(j)).start()
        else:
            for j in range(1, H):
                extra(stat_o.at[z], stat_o.at[lax.rem(z + H - j, H)], 4 + j, place.far(j)).wait()

    done = [before[i][len(CALLS)] for i in range(5)]
    for i in DRAIN:
        if i < 4:
            stages[i](jnp.int32(done[i]))
        else:
            small_sum(done[i])
        done[i] += 1
    assert done == [NCH] * 4 + [5] and place_no[0] == len(CALLS)

    ig_c.wait()
    for n in range(PIECES):
        piece(0, n).wait_recv()
        piece(1, n).wait()

    @pl.loop(NCH - SLOTS, NCH)
    def _(p):
        core_copy(p).wait_send()

    @pl.loop(0, NCH)
    def _(k):
        dw_copy(k).wait()
        for i in range(3):
            near_copy(q.at[k, x, :, yy], k, i, place.over_x()).wait_send()
        for j in range(1, H):
            far_copy(k, z, j).wait_send()


def backward(cfg, saved, krow):
    (wg, at, proj, lse, o, h, bnt, g, gp, gy, gm, gmt, out, xs, ts, totals, loss) = saved
    H, R = cfg["groups"], cfg["rows"]
    NQ, NO, NF = cfg["nq"], cfg["no"], cfg["nf"]
    NCH = NQ + NO + 2 * NF
    IMG, SEQ, D = xs.shape
    TOK = IMG * SEQ
    lhs = (2, D // 2, TOK)
    half = (2, H, 2, R, CW)
    vm = pltpu.VMEM
    dma = pltpu.SemaphoreType.DMA
    return pl.pallas_call(
        functools.partial(bwd_kernel, cfg),
        name="backward_reduce",
        out_shape=[
            jax.ShapeDtypeStruct((2 * IMG, SEQ // 2, D), BF), jax.ShapeDtypeStruct((2 * IMG, SEQ // 2, D), BF),
            jax.ShapeDtypeStruct((NCH, R, CW), F32), jax.ShapeDtypeStruct((H, 8, D), F32),
        ],
        in_specs=[any_spec()] * 14 + [vmem_spec()] * 3,
        out_specs=[any_spec()] * 3 + [vmem_spec()],
        scratch_shapes=[
            vm((NCH,) + half, BF), vm((SLOTS,) + half, BF), vm((SLOTS,) + half, BF),
            vm((NCH, 3, H, R, CW), BF), vm((NCH, H - 1, R, CW), BF), vm((NCH, R, CW), F32),
            vm((WSLOTS, 2, H, 2, 2, R, CW), BF), vm((2, 2, TOK, CW), BF), vm((2, 2, TOK, CW), BF),
            vm((2, TOK, CW), BF), vm((TOK, CW), F32), vm((TOK, D), BF), vm(lhs, BF), vm(lhs, BF),
            vm((TOK, D), F32), vm((TOK, D), F32), vm((TOK, D), F32), vm(o.shape, BF), vm(o.shape, BF),
            vm(proj.shape, BF), vm(lse.shape, F32), vm(xs.shape, BF), vm((2, 8, D), F32), vm((6, 8, D), F32),
            dma((NCH,)), dma((NCH,)), pltpu.SemaphoreType.REGULAR, dma((NCH, 3)), dma((NCH, 3)),
            dma((NCH, H - 1)), dma((NCH, H - 1)), dma((H + 4,)), dma((H + 4,)), dma((2, PIECES)), dma((2, PIECES)),
            dma((NCH,)), dma((NF, 2)), dma((32,)), dma((NCH,)),
        ],
        compiler_params=pltpu.CompilerParams(
            collective_id=1, has_side_effects=True, vmem_limit_bytes=63 * 2**20
        ),
    )(wg, at, proj, lse, o, h, bnt, g, gp, gy, gm, gmt, out, xs, totals, loss, krow)


def per_device(
    inputs, teacher, keep_mask, gain_attn, qkv_weight, out_weight, gain_mlp, up_weight, down_weight
):
    cfg = config(inputs, (qkv_weight, out_weight, up_weight, down_weight))
    R, NQ, NO, NF = cfg["rows"], cfg["nq"], cfg["no"], cfg["nf"]
    small, krow, kcol = prepare(inputs, keep_mask, gain_attn, gain_mlp)
    saved = forward(
        cfg, inputs, teacher, qkv_weight.reshape(R, -1), out_weight, up_weight, down_weight, small, krow, kcol
    )
    output, grad_in, dw, stats = backward(cfg, saved, krow)
    total = jnp.sum(stats, axis=0)
    start = lax.axis_index("dp") * R
    gains = lax.dynamic_slice(total, (0, start), (2, R))
    loss = total[2, 0] / saved[15][2, 0]
    qkv = dw[:NQ].reshape(NQ // 3, 3, R, CW).transpose(2, 1, 0, 3).reshape(qkv_weight.shape)

    def columns(first, count):
        return dw[first:first + count].transpose(1, 0, 2).reshape(R, count * CW)

    return (
        output,
        loss,
        grad_in.astype(F32),
        gains[0],
        qkv,
        columns(NQ, NO),
        gains[1],
        columns(NQ + NO, NF),
        columns(NQ + NO + NF, NF),
    )


def solution(mesh):
    rows = P("dp", "mp", None)
    weight = P("dp", "mp")
    qkv = P("dp", None, "mp")
    return jax.shard_map(
        per_device,
        mesh=mesh,
        in_specs=(rows, rows, P("dp", None), P("dp"), qkv, weight, P("dp"), weight, weight),
        out_specs=(rows, P(), rows, P("dp"), qkv, weight, P("dp"), weight, weight),
        check_vma=False,
    )
```

```python
import functools
import jax
import jax.numpy as jnp
from jax import lax
from jax.experimental import pallas as pl
from jax.experimental.pallas import tpu as pltpu
from jax.sharding import PartitionSpec as P

MESH = pl.DeviceIdType.MESH
HDIM = 64
CW = 256
EPS = 1e-06
F32 = jnp.float32
BF = jnp.bfloat16
PIECES = 5
BOTH_X = (0, 1, 2, 3, 4, 8, 10, 12, 14, 17)
Z_LAST = (6, 9, 16)
X_WITH = (0, 1, 2, 3, 4)
T_WITH = (10, 12, 14, 15, 17)
FWD_CALLS = (
    (0, 0, 0), (0, 0, 0), (0, 0), (1, 0, 1, 0, 1, 0, 2, 1, 0, 1, 0, 2, 3, 1, 1, 0, 0, 4, 2, 1, 0, 3, 4, 2, 1, 0), (3,), (2,),
    (4, 1), (), (), (), (3, 2, 2, 2, 0), (1, 1, 1),
    (4, 3, 2, 0, 0, 0), (2, 1), (), (4,), (3, 1, 0, 0, 4), (),
    (3, 3), (2, 2), (4, 1, 1), (), (4,), (3, 0),
    (2, 2), (4,), (1, 1), (2, 2, 1, 1, 3, 3, 3, 3, 4), (), (4,),
    (2,), (4,), (3, 1), (4,), (3,), (4,),
    (2, 2, 2), (4,), (2, 2, 1, 1), (3, 4), (), (2,),
    (3,), (3, 2, 3, 4), (3, 4), (3, 4), (3, 4), (4,),
    (3, 4), (3, 4), (4,),
)
NT = (((1,), (1,)), ((), ()))
NN = (((1,), (0,)), ((), ()))


def dot(a, b, dims=NN):
    return lax.dot_general(a, b, dims, preferred_element_type=F32)


class Place:
    def __init__(self, groups):
        self.groups = groups
        dp = lax.axis_index("dp")
        self.x = lax.axis_index("mp")
        self.c = lax.rem(dp, 2)
        self.y = lax.rem(dp // 2, 2)
        self.z = dp // 4

    def at(self, z, y, c, x):
        return {"dp": (z * 2 + y) * 2 + c, "mp": x}

    def far(self, j):
        return self.at(lax.rem(self.z + j, self.groups), self.y, self.c, self.x)

    def over_x(self):
        return self.at(self.z, self.y, self.c, 1 - self.x)

    def over_y(self):
        return self.at(self.z, 1 - self.y, self.c, self.x)

    def over_c(self):
        return self.at(self.z, self.y, 1 - self.c, self.x)

    def partners(self):
        return [self.far(j) for j in range(1, self.groups)] + [
            self.over_x(), self.over_y(), self.over_c()
        ]


def meet(place):
    barrier = pltpu.get_barrier_semaphore()
    partners = place.partners()
    for partner in partners:
        pl.semaphore_signal(barrier, 1, device_id=partner, device_id_type=MESH)
    pl.semaphore_wait(barrier, len(partners))


def member(k, numbers):
    if isinstance(k, int):
        return k in numbers
    found = False
    for n in numbers:
        found = (k == n) | found
    return found


def pick(table, index):
    value = jnp.int32(table[0])
    for n in range(1, len(table)):
        if table[n] != table[n - 1]:
            value = jnp.where(index >= n, table[n], value)
    return value


def when(cond, body):
    if isinstance(cond, bool):
        if cond:
            body()
    else:
        pl.when(cond)(body)


def fwd_kernel(cfg, xin, tin, wq, wo, wu, wd, gain_a, gain_m, mask, *refs):
    (wg_o, at_o, proj_o, lse_o, o_o, h_o, bnt_o, g_o, gp_o, gy_o, gm_o, gmt_o, out_o, xs_o, ts_o, sm_o, loss_o,
     wg, xs, ts, sm, own_sm, kpad, kcol, a, proj, o, lse, h, bn, g, gp, zb, y, tb,
     local_sem, send_sem, recv_sem, extra_send, extra_recv, piece_send, piece_recv, out_sem, misc_sem) = refs
    H, R = cfg["groups"], cfg["rows"]
    NQ, NO, NF = cfg["nq"], cfg["no"], cfg["nf"]
    NCH = NQ + NO + 2 * NF
    IMG, SEQ, D = xs.shape
    HALF = SEQ // 2
    TOK = IMG * SEQ
    GRP = NQ // 3
    place = Place(H)
    x, yy, z, c = place.x, place.y, place.z, place.c
    scale = HDIM ** (-0.5)

    def remote(ref, k, i, device):
        return pltpu.make_async_remote_copy(
            ref, ref, send_sem.at[k, i], recv_sem.at[k, i], device_id=device, device_id_type=MESH
        )

    def source(k):
        if k < NQ:
            return wq.at[k % 3, :, pl.ds((k // 3) * CW, CW)]
        if k < NQ + NO:
            return wo.at[:, pl.ds(CW * (k - NQ), CW)]
        if k < NQ + NO + NF:
            return wu.at[:, pl.ds(CW * (k - NQ - NO), CW)]
        return wd.at[:, pl.ds(CW * (k - NQ - NO - NF), CW)]

    def own(k):
        return pltpu.make_async_copy(source(k), wg.at[k, x, z, yy, c], local_sem.at[k])

    def own_wait(k):
        pltpu.make_async_copy(wq.at[0, :, pl.ds(0, CW)], wg.at[k, x, z, yy, c], local_sem.at[k]).wait()

    def relay(k):
        both = member(k, BOTH_X)
        first = jnp.where(both, 1, 1 - c) if not isinstance(both, bool) else (1 if both else 1 - c)
        xa = jnp.where(first == 1, 1 - x, x)
        ya = jnp.where(first == 1, yy, 1 - yy)
        return xa, ya, jnp.where(first == 1, x, 1 - x), jnp.where(first == 1, 1 - yy, yy)

    def either(k, late, early):
        last = member(k, Z_LAST)
        if isinstance(last, bool):
            (late if last else early)()
        else:
            pl.when(last)(late)
            pl.when(jnp.logical_not(last))(early)

    def s1(k):
        own_wait(k)
        own_block = wg.at[k, x, z, yy, c]
        xa, ya, xb, yb = relay(k)

        def late():
            remote(own_block, k, H - 1, place.at(z, ya, c, xa)).start()
            remote(own_block, k, H, place.at(z, yb, c, xb)).start()

        def early():
            for j in range(1, H):
                remote(own_block, k, j - 1, place.far(j)).start()

        either(k, late, early)

    def s2(k):
        xa, ya, xb, yb = relay(k)

        def late():
            block = wg.at[k, xa, z, ya, c]
            remote(block, k, H - 1, place.at(z, ya, c, xa)).wait_recv()
            remote(block, k, H + 1, place.at(z, yb, c, xb)).start()

        def early():
            for j in range(1, H):
                remote(wg.at[k, x, lax.rem(z + H - j, H), yy, c], k, j - 1, place.far(j)).wait_recv()
            piece_at(k)
            remote(wg.at[k, x, :, yy, c], k, H - 1, place.at(z, ya, c, xa)).start()
            remote(wg.at[k, x, :, yy, c], k, H, place.at(z, yb, c, xb)).start()

        either(k, late, early)

    def s3(k):
        xa, ya, xb, yb = relay(k)

        def late():
            remote(wg.at[k, xb, z, yb, c], k, H, place.at(z, yb, c, xb)).wait_recv()
            remote(wg.at[k, 1 - x, z, 1 - yy, c], k, H + 1, place.at(z, yb, c, xb)).wait_recv()
            for j in range(1, H):
                remote(wg.at[k, :, z, :, c], k, j - 1, place.far(j)).start()

        def early():
            remote(wg.at[k, xa, :, ya, c], k, H - 1, place.at(z, ya, c, xa)).wait_recv()
            remote(wg.at[k, xa, :, ya, c], k, H + 1, place.at(z, yb, c, xb)).start()

        either(k, late, early)

    def s4(k):
        xa, ya, xb, yb = relay(k)

        def late():
            for j in range(1, H):
                remote(wg.at[k, :, lax.rem(z + H - j, H), :, c], k, j - 1, place.far(j)).wait_recv()

        def early():
            remote(wg.at[k, xb, :, yb, c], k, H, place.at(z, yb, c, xb)).wait_recv()
            remote(wg.at[k, 1 - x, :, 1 - yy, c], k, H + 1, place.at(z, yb, c, xb)).wait_recv()

        either(k, late, early)
        remote(wg.at[k, :, :, :, c], k, H + 2, place.over_c()).start()

    def keep_chunk(k):
        return pltpu.make_async_copy(wg.at[k], wg_o.at[k], out_sem.at[k])

    def s5(k):
        remote(wg.at[k, :, :, :, 1 - c], k, H + 2, place.over_c()).wait_recv()
        keep_chunk(k).start()

    PR = HALF // PIECES

    def piece(i, n, to):
        src, dst = ((xin, xs), (tin, ts))[i]
        return pltpu.make_async_remote_copy(
            src.at[pl.ds(IMG * (1 - x), IMG), pl.ds(PR * n, PR)], dst.at[:, pl.ds(HALF * to + PR * n, PR)],
            piece_send.at[i, n], piece_recv.at[i, n], device_id=place.over_x(), device_id_type=MESH
        )

    def piece_at(k):
        for i, chunks in enumerate((X_WITH, T_WITH)):
            for n, chunk_no in enumerate(chunks):
                when(k == chunk_no, lambda i=i, n=n: piece(i, n, x).start())

    def pieces_in(i):
        for n in range(PIECES):
            piece(i, n, 1 - x).wait_recv()

    stages = (s1, s2, s3, s4, s5)
    pos = [0] * 5
    place_no = [0]

    def upcoming():
        calls = []
        for i in FWD_CALLS[place_no[0]]:
            calls.append((i, pos[i]))
            pos[i] += 1
        place_no[0] += 1
        return calls

    def serve():
        for i, n in upcoming():
            stages[i](n)

    def serve_in(index, calls, starts):
        for i in (4, 3, 2, 1, 0):
            counts = [call.count(i) for call in calls]
            if max(counts):
                first = pick(starts[i], index)

                @pl.loop(first, first + pick(counts, index))
                def _(n, i=i):
                    stages[i](n)

    def served(count):
        calls = FWD_CALLS[place_no[0]:place_no[0] + count]
        place_no[0] += count
        starts = [[pos[i] + sum(call.count(i) for call in calls[:n]) for n in range(count)] for i in range(5)]
        for i in range(5):
            pos[i] += sum(call.count(i) for call in calls)
        return calls, starts

    kept = []

    def keep(src, dst):
        copy = pltpu.make_async_copy(src, dst, misc_sem.at[len(kept)])
        copy.start()
        kept.append(copy)

    def extra(src, dst, i, device):
        return pltpu.make_async_remote_copy(
            src, dst, extra_send.at[i], extra_recv.at[i], device_id=device, device_id_type=MESH
        )

    for k in range(NCH):
        own(k).start()
    mine = pl.ds(HALF * x, HALF)
    xl = pltpu.make_async_copy(xin.at[pl.ds(IMG * x, IMG)], xs.at[:, mine], misc_sem.at[30])
    tl = pltpu.make_async_copy(tin.at[pl.ds(IMG * x, IMG)], ts.at[:, mine], misc_sem.at[31])
    spread = (lax.broadcasted_iota(jnp.int32, (R, D), 1)
              == lax.broadcasted_iota(jnp.int32, (R, D), 0) + lax.axis_index("dp") * R)
    spread = jnp.where(spread, 1.0, 0.0).astype(BF)
    line = lax.broadcasted_iota(jnp.int32, (8, D), 0)
    own_sm[...] = jnp.where(line == 0, dot(gain_a[...], spread),
                            jnp.where(line == 1, dot(gain_m[...], spread),
                                      jnp.sum(mask[...].astype(F32))))
    sl = pltpu.make_async_copy(own_sm, sm.at[z, yy, c], misc_sem.at[29])
    xl.start()
    tl.start()
    sl.start()
    meet(place)
    sl.wait()
    for j in range(1, H):
        extra(sm.at[z, yy, c], sm.at[z, yy, c], 3 + j, place.far(j)).start()
    serve()
    for j in range(1, H):
        extra(sm.at[z, yy, c], sm.at[lax.rem(z + H - j, H), yy, c], 3 + j, place.far(j)).wait_recv()
    extra(sm.at[:, yy, c], sm.at[:, yy, c], 2, place.over_y()).start()
    serve()
    extra(sm.at[:, 1 - yy, c], sm.at[:, 1 - yy, c], 2, place.over_y()).wait_recv()
    extra(sm.at[:, :, c], sm.at[:, :, c], 3, place.over_c()).start()
    kpad[...] = jnp.zeros_like(kpad)
    for i in range(IMG):
        kpad[:, 0:SEQ] = jnp.broadcast_to(mask[pl.ds(IMG * x + i, 1)].astype(F32), (128, SEQ))
        kcol[i] = jnp.transpose(kpad[...])[0:SEQ]
    serve()
    extra(sm.at[:, :, 1 - c], sm.at[:, :, 1 - c], 3, place.over_c()).wait_recv()
    totals = jnp.sum(sm[...].reshape(H * 4, 8, D), axis=0)
    sm_o[...] = totals
    xl.wait()
    serve()
    pieces_in(0)
    keep(xs, xs_o)

    RB = 32

    def rows_of(ref, r):
        per = SEQ // RB
        return ref[r // per, pl.ds(pl.multiple_of(lax.rem(r, per) * RB, RB), RB)]

    def norm_to(values, gain):
        centre = values - jnp.mean(values, axis=-1, keepdims=True)
        spread = jnp.mean(centre * centre, axis=-1, keepdims=True)
        return (centre * lax.rsqrt(spread + EPS) * gain).astype(BF)

    for part in range(2):
        count = TOK // RB // 2

        @pl.loop(part * count, (part + 1) * count)
        def _(r):
            a[pl.ds(pl.multiple_of(r * RB, RB), RB)] = norm_to(rows_of(xs, r).astype(F32), sm_o[0:1])

        serve()

    def transposed(src, dst):
        @pl.loop(0, D // 128)
        def _(d):
            t = jnp.transpose(src[:, pl.ds(pl.multiple_of(d * 128, 128), 128)].astype(F32))
            t = t.reshape(64 // R, 2, R, TOK)
            for p in range(2):
                dst[p, pl.ds(pl.multiple_of(d * 64, 64), 64)] = t[:, p].reshape(64, TOK).astype(BF)

    transposed(a, tb)
    keep(tb, at_o)
    serve()

    def chunk(k, half):
        return wg[k, half].reshape(D, CW)

    def project(k):
        @pl.loop(0, 2)
        def _(half):
            proj[k, half] = dot(a[...], chunk(k, half)).astype(BF).reshape(IMG, SEQ, CW)

    lane = lax.broadcasted_iota(jnp.int32, (SEQ, CW), 1) // HDIM

    def attend(group, u):
        half, i = u // IMG, lax.rem(u, IMG)
        q = proj[3 * group, half, i]
        key = proj[3 * group + 1, half, i]
        val = proj[3 * group + 2, half, i]
        allowed = mask[pl.ds(IMG * x + i, 1)] > 0
        total = jnp.zeros((SEQ, CW), F32)
        logs = jnp.zeros((SEQ, 128), F32)
        spot = lax.broadcasted_iota(jnp.int32, (SEQ, 128), 1)
        for head in range(CW // HDIM):
            scores = dot(jnp.where(lane == head, q, 0), key, NT) * scale
            scores = jnp.where(allowed, scores, -1e30)
            top = jnp.max(scores, axis=-1, keepdims=True)
            raised = jnp.exp(scores - top)
            norm = jnp.sum(raised, axis=-1, keepdims=True)
            soft = (raised / norm).astype(BF)
            total = total + dot(soft, jnp.where(lane == head, val, 0))
            logs = jnp.where(spot == head, top + jnp.log(norm), logs)
        o[group, half, i] = total.astype(BF)
        lse[group, half, i] = logs

    for group in range(GRP):
        for k in range(3 * group, 3 * group + 3):
            serve()
            project(k)
        places = served(2 * IMG)

        @pl.loop(0, 2 * IMG)
        def _(u, group=group, places=places):
            serve_in(u, *places)
            attend(group, u)

    keep(proj, proj_o)
    keep(lse, lse_o)
    keep(o, o_o)

    def gathered(src, k, half):
        return src[k, half].reshape(TOK, CW)

    h[...] = xs[...].reshape(TOK, D).astype(F32)
    for k in range(NO):
        serve()

        @pl.loop(0, 2)
        def _(half, k=k):
            h[...] += dot(gathered(o, k, half), chunk(NQ + k, half), NT)

    keep(h, h_o)

    for part in range(2):
        count = TOK // RB // 2
        serve()

        @pl.loop(part * count, (part + 1) * count)
        def _(r):
            at = pl.ds(pl.multiple_of(r * RB, RB), RB)
            bn[at] = norm_to(h[at], sm_o[1:2])

    first_up = NQ + NO

    def gelu(k, half):
        GB = 64

        @pl.loop(0, TOK // GB)
        def _(r):
            at = pl.ds(pl.multiple_of(r * GB, GB), GB)
            v = zb[at]
            cdf = 0.5 * (1.0 + lax.erf(v * 0.7071067811865476))
            g[k, half, at] = (v * cdf).astype(BF)
            gp[k, half, at] = (cdf + v * (jnp.exp(-0.5 * (v * v)) * 0.3989422804014327)).astype(BF)

    for k in range(NF):
        serve()
        calls = upcoming()

        @pl.loop(0, 2)
        def _(half, k=k, calls=calls):
            @pl.when(half == 1)
            def _():
                for i, n in calls:
                    stages[i](n)

            zb[...] = dot(bn[...], chunk(first_up + k, half))
            gelu(k, half)

    keep(g, g_o)
    keep(gp, gp_o)
    first_down = first_up + NF
    kept[1].wait()
    serve()
    transposed(bn, tb)
    keep(tb, bnt_o)
    serve()
    y[...] = h[...]

    for k in range(NF):
        serve()

        @pl.loop(0, 2)
        def _(half, k=k):
            y[...] += dot(g[k, half], chunk(first_down + k, half), NT)

    assert pos == [NCH] * 5 and place_no[0] == len(FWD_CALLS)
    tl.wait()
    pieces_in(1)
    keep(ts, ts_o)
    zb[0:RB, 0:128] = jnp.zeros((RB, 128), F32)
    factor = 2.0 * cfg["tokens"] / sm_o[2:3]
    xs_ref = xs

    for copy in kept[:1]:
        copy.wait()

    @pl.loop(0, TOK // RB)
    def _(r):
        at = pl.ds(pl.multiple_of(r * RB, RB), RB)
        per = SEQ // RB
        img, pos = r // per, pl.multiple_of(lax.rem(r, per) * RB, RB)
        res = y[at]
        kept_rows = jnp.tile(kcol[img, pl.ds(pos, RB)], (1, D // 128))
        xs_ref[img, pl.ds(pos, RB)] = (res * kept_rows).astype(BF)
        error = res - ts[img, pl.ds(pos, RB)].astype(F32)
        squares = error * error * kept_rows
        part = squares[:, 0:128]
        for n in range(1, D // 128):
            part = part + squares[:, n * 128:(n + 1) * 128]
        zb[0:RB, 0:128] += part
        grad = factor * kept_rows * error
        y[at] = grad
        a[at] = grad.astype(BF)

    loss_o[...] = jnp.zeros_like(loss_o) + jnp.sum(zb[0:RB, 0:128]) * (1.0 / D)
    keep(xs, out_o)
    keep(y, gy_o)
    keep(a, gm_o)
    kept[8].wait()
    transposed(a, tb)
    keep(tb, gmt_o)
    for n, copy in enumerate(kept):
        if n not in (0, 1, 8):
            copy.wait()
    for i in range(2):
        for n in range(PIECES):
            piece(i, n, x).wait_send()
    for j in range(1, H):
        extra(sm.at[z, yy, c], sm.at[z, yy, c], 3 + j, place.far(j)).wait_send()
    extra(sm.at[:, yy, c], sm.at[:, yy, c], 2, place.over_y()).wait_send()
    extra(sm.at[:, :, c], sm.at[:, :, c], 3, place.over_c()).wait_send()

    @pl.loop(0, NCH)
    def _(k):
        keep_chunk(k).wait()

        def late():
            for j in range(1, H):
                remote(wg.at[k, :, z, :, c], k, j - 1, place.far(j)).wait_send()
            for i in (H - 1, H, H + 1):
                remote(wg.at[k, x, z, yy, c], k, i, place.over_x()).wait_send()

        def early():
            for j in range(1, H):
                remote(wg.at[k, x, z, yy, c], k, j - 1, place.far(j)).wait_send()
            for i in (H - 1, H, H + 1):
                remote(wg.at[k, x, :, yy, c], k, i, place.over_x()).wait_send()

        either(k, late, early)
        remote(wg.at[k, :, :, :, c], k, H + 2, place.over_c()).wait_send()


def any_spec():
    return pl.BlockSpec(memory_space=pl.ANY)


def vmem_spec():
    return pl.BlockSpec(memory_space=pltpu.VMEM)


def forward(cfg, xin, tin, wq, wo, wu, wd, gain_a, gain_m, mask):
    H, R = cfg["groups"], cfg["rows"]
    NQ, NO, NF = cfg["nq"], cfg["no"], cfg["nf"]
    NCH = NQ + NO + 2 * NF
    IMG = xin.shape[0] // 2
    SEQ, D = 2 * xin.shape[1], xin.shape[2]
    TOK = IMG * SEQ
    GRP = NQ // 3
    wg = (NCH, 2, H, 2, 2, R, CW)
    lhs = (2, D // 2, TOK)
    big = (NF, 2, TOK, CW)
    shapes = [
        (wg, BF), (lhs, BF), ((NQ, 2, IMG, SEQ, CW), BF), ((GRP, 2, IMG, SEQ, 128), F32),
        ((GRP, 2, IMG, SEQ, CW), BF), ((TOK, D), F32), (lhs, BF), (big, BF), (big, BF),
        ((TOK, D), F32), ((TOK, D), BF), (lhs, BF), ((IMG, SEQ, D), BF), ((IMG, SEQ, D), BF), ((IMG, SEQ, D), BF),
        ((8, D), F32), ((8, 128), F32),
    ]
    return pl.pallas_call(
        functools.partial(fwd_kernel, cfg),
        name="gather_forward",
        out_shape=[jax.ShapeDtypeStruct(s, t) for s, t in shapes],
        in_specs=[any_spec()] * 6 + [vmem_spec()] * 3,
        out_specs=[any_spec()] * 15 + [vmem_spec()] * 2,
        scratch_shapes=[
            pltpu.VMEM(wg, BF), pltpu.VMEM((IMG, SEQ, D), BF), pltpu.VMEM((IMG, SEQ, D), BF),
            pltpu.VMEM((H, 2, 2, 8, D), F32), pltpu.VMEM((8, D), F32), pltpu.VMEM((128, -(-SEQ // 128) * 128), F32),
            pltpu.VMEM((IMG, SEQ, 128), F32), pltpu.VMEM((TOK, D), BF),
            pltpu.VMEM((NQ, 2, IMG, SEQ, CW), BF), pltpu.VMEM((GRP, 2, IMG, SEQ, CW), BF),
            pltpu.VMEM((GRP, 2, IMG, SEQ, 128), F32), pltpu.VMEM((TOK, D), F32), pltpu.VMEM((TOK, D), BF),
            pltpu.VMEM(big, BF), pltpu.VMEM(big, BF), pltpu.VMEM((TOK, CW), F32), pltpu.VMEM((TOK, D), F32),
            pltpu.VMEM(lhs, BF),
            pltpu.SemaphoreType.DMA((NCH,)), pltpu.SemaphoreType.DMA((NCH, H + 3)),
            pltpu.SemaphoreType.DMA((NCH, H + 3)), pltpu.SemaphoreType.DMA((H + 4,)),
            pltpu.SemaphoreType.DMA((H + 4,)), pltpu.SemaphoreType.DMA((2, PIECES)),
            pltpu.SemaphoreType.DMA((2, PIECES)), pltpu.SemaphoreType.DMA((NCH,)), pltpu.SemaphoreType.DMA((32,)),
        ],
        compiler_params=pltpu.CompilerParams(
            collective_id=0, has_side_effects=True, vmem_limit_bytes=63 * 2**20
        ),
    )(xin, tin, wq, wo, wu, wd, gain_a, gain_m, mask)


def config(inputs, weights):
    rows = weights[0].shape[0]
    dps = lax.axis_size("dp")
    return {
        "groups": dps // 4,
        "rows": rows,
        "nq": weights[0].shape[1] * weights[0].shape[2] // CW,
        "no": weights[1].shape[1] // CW,
        "nf": weights[2].shape[1] // CW,
        "tokens": float(inputs.shape[0] * inputs.shape[1] * dps * lax.axis_size("mp")),
    }


SLOTS = 3
FAR_AT = 4
WSLOTS = 4
CALLS = (
    (0, 0, 0, 0, 0), (0, 0, 0, 0, 0), (0, 0, 0, 0, 0), (1, 0, 0, 0, 0), (0, 0, 0, 0, 0),
    (1, 0, 0, 0, 0), (0, 0, 0, 0, 0), (1, 0, 0, 0, 0), (0, 1, 0, 0, 0), (1, 0, 0, 0, 0),
    (0, 1, 0, 0, 0), (1, 0, 0, 0, 0), (0, 0, 0, 0, 0), (1, 0, 0, 0, 0), (0, 1, 0, 0, 0),
    (1, 0, 0, 0, 0), (0, 0, 0, 0, 0), (1, 0, 0, 0, 0), (0, 0, 2, 0, 0), (1, 1, 1, 0, 0),
    (1, 0, 0, 0, 0), (0, 0, 0, 0, 0), (0, 0, 0, 0, 0), (1, 1, 0, 1, 0), (0, 0, 0, 0, 0),
    (1, 0, 0, 1, 0), (0, 0, 0, 0, 0), (1, 1, 1, 1, 0), (1, 0, 0, 0, 0), (0, 1, 0, 0, 0),
    (0, 0, 0, 0, 0), (1, 1, 0, 0, 0), (1, 0, 0, 1, 0), (0, 1, 1, 0, 0), (0, 1, 0, 0, 0),
    (0, 0, 0, 0, 0), (0, 0, 0, 0, 0), (1, 0, 0, 0, 0), (0, 1, 0, 0, 0), (1, 0, 3, 1, 0),
    (0, 1, 3, 0, 0), (0, 1, 0, 1, 0), (0, 1, 1, 1, 0), (0, 0, 0, 0, 0), (0, 0, 1, 1, 0),
    (0, 1, 0, 0, 0), (1, 0, 0, 1, 0), (1, 0, 1, 0, 0), (1, 1, 0, 1, 0), (0, 1, 1, 1, 0),
    (0, 0, 1, 1, 0), (0, 1, 1, 1, 0), (0, 1, 0, 2, 0), (0, 0, 0, 0, 0), (0, 1, 1, 1, 0),
    (0, 0, 0, 0, 0), (1, 0, 0, 1, 0), (1, 0, 1, 0, 0), (1, 1, 1, 0, 0), (0, 1, 0, 1, 0),
)
DRAIN = (
    3, 2, 1, 4, 3, 4, 1, 3, 4, 2, 2, 2, 4, 3, 3, 3, 4,
)
OUT_FIRST = 1


def bwd_kernel(cfg, wg, at_i, proj_i, lse_i, o_i, h_i, bnt_i, g_i, gp_i, gy_i, gm_i, gmt_i, out_i, xs_i,
               totals, loss_i, mask, *refs):
    (out_o, ig_o, dq_o, do_o, du_o, dd_o, stat_o,
     q, snd, rcv, near, farr, dw, wb, gb_buf, gpb, gz, zb, gm, lhs1, lhs2, acc, gh, h, o, go, proj, lse, xb, igr, stat, sbuf, zsum,
     core_send, core_recv, credit, near_send, near_recv, far_send, far_recv, extra_send, extra_recv, piece_send, piece_recv,
     wsem, gsem, misc_sem, dw_sem) = refs
    H, R = cfg["groups"], cfg["rows"]
    NQ, NO, NF = cfg["nq"], cfg["no"], cfg["nf"]
    NCH = NQ + NO + 2 * NF
    IMG, SEQ, D = xb.shape
    HALF = SEQ // 2
    TOK = IMG * SEQ
    GRP = NQ // 3
    place = Place(H)
    x, yy, z, c = place.x, place.y, place.z, place.c
    scale = HDIM ** (-0.5)

    def ident(p):
        ff = jnp.where(lax.rem(p, 2) == 0, NQ + NO + NF + p // 2, NQ + NO + p // 2)
        return jnp.where(p < 2 * NF, ff, jnp.where(p < 2 * NF + NO, p - 2 * NF + NQ, p - 2 * NF - NO))

    def relay(p):
        both = (p >= OUT_FIRST) & (p < OUT_FIRST + PIECES)
        first = jnp.where(both, 1, 1 - c)
        xa = jnp.where(first == 1, 1 - x, x)
        ya = jnp.where(first == 1, yy, 1 - yy)
        return xa, ya, jnp.where(first == 1, x, 1 - x), jnp.where(first == 1, 1 - yy, yy)

    loads = []

    def load(src, dst):
        copy = pltpu.make_async_copy(src, dst, misc_sem.at[len(loads)])
        copy.start()
        loads.append(copy)
        return copy

    def wload(n):
        return pltpu.make_async_copy(wg.at[ident(n)], wb.at[lax.rem(n, WSLOTS)], wsem.at[n])

    def gload(j):
        s = lax.rem(j, 2)
        return (pltpu.make_async_copy(g_i.at[j], gb_buf.at[s], gsem.at[j, 0]),
                pltpu.make_async_copy(gp_i.at[j], gpb.at[s], gsem.at[j, 1]))

    gm_l = load(gm_i, gm)
    gmt_l = load(gmt_i, lhs1)
    for j in range(2):
        for copy in gload(jnp.int32(j)):
            copy.start()
    for n in range(WSLOTS):
        wload(jnp.int32(n)).start()
    bnt_l = load(bnt_i, lhs2)
    out_l = load(out_i, xb)
    gy_l = load(gy_i, gh)
    h_l = load(h_i, h)
    o_l = load(o_i, o)
    proj_l = load(proj_i, proj)
    lse_l = load(lse_i, lse)

    def extra(src, dst, i, device):
        return pltpu.make_async_remote_copy(
            src, dst, extra_send.at[i], extra_recv.at[i], device_id=device, device_id_type=MESH
        )

    meet(place)

    def core_copy(p, start=False):
        s = lax.rem(p, SLOTS)
        return pltpu.make_async_remote_copy(
            snd.at[s], rcv.at[s], core_send.at[p], core_recv.at[p], device_id=place.over_c(), device_id_type=MESH
        )

    def near_copy(src, k, i, device):
        return pltpu.make_async_remote_copy(
            src, near.at[k, i], near_send.at[k, i], near_recv.at[k, i], device_id=device, device_id_type=MESH
        )

    def far_copy(k, zd, j):
        return pltpu.make_async_remote_copy(
            q.at[k, x, zd, yy], farr.at[k, j - 1], far_send.at[k, j - 1], far_recv.at[k, j - 1],
            device_id=place.far(j), device_id_type=MESH
        )

    def produce(p, lhs, rhs):
        k = ident(p)
        s = lax.rem(p, SLOTS)
        pl.when(p >= SLOTS)(lambda: core_copy(p - SLOTS).wait_send())

        @pl.loop(0, 2)
        def _(half):
            snd[s, half] = dot(lhs[1 - c], rhs(half)).astype(BF).reshape(H, 2, R, CW)
            q[k, half] = dot(lhs[c], rhs(half)).astype(BF).reshape(H, 2, R, CW)

        pl.when(p >= SLOTS)(lambda: pl.semaphore_wait(credit, 1))
        core_copy(p).start()

    def added(k, xi, yi, others):
        @pl.loop(0, H)
        def _(n):
            total = q[k, xi, n, yi].astype(F32)
            for other in others:
                total = total + near[k, other, n].astype(F32)
            q[k, xi, n, yi] = total.astype(BF)

    def r1(p):
        k = ident(p)
        s = lax.rem(p, SLOTS)
        core_copy(p).wait_recv()

        @pl.loop(0, 2 * H)
        def _(n):
            i, m = n // H, lax.rem(n, H)
            for y2 in range(2):
                q[k, i, m, y2] = (q[k, i, m, y2].astype(F32) + rcv[s, i, m, y2].astype(F32)).astype(BF)

        pl.when(p + SLOTS < NCH)(
            lambda: pl.semaphore_signal(credit, 1, device_id=place.over_c(), device_id_type=MESH)
        )
        xa, ya, xo, yo = relay(p)
        near_copy(q.at[k, 1 - x, :, 1 - yy], k, 0, place.at(z, yo, c, xo)).start()
        near_copy(q.at[k, xo, :, yo], k, 1, place.at(z, yo, c, xo)).start()

    def r2(p):
        k = ident(p)
        xa, ya, xo, yo = relay(p)
        near_copy(q.at[k, 1 - x, :, 1 - yy], k, 0, place.at(z, yo, c, xo)).wait_recv()
        added(k, xa, ya, (0,))
        near_copy(q.at[k, xa, :, ya], k, 2, place.at(z, ya, c, xa)).start()

    def r3(p):
        k = ident(p)
        xa, ya, xo, yo = relay(p)
        near_copy(q.at[k, xo, :, yo], k, 1, place.at(z, yo, c, xo)).wait_recv()
        near_copy(q.at[k, xa, :, ya], k, 2, place.at(z, ya, c, xa)).wait_recv()
        added(k, x, yy, (1, 2))
        for j in range(1, H):
            far_copy(k, lax.rem(z + j, H), j).start()

    def dw_out(k):
        def send(first, count, at):
            @pl.when((k >= first) & (k < first + count))
            def _():
                pltpu.make_async_copy(dw.at[k], at(pl.multiple_of((k - first) * CW, CW)), dw_sem.at[k]).start()

        for part in range(3):
            @pl.when((k < NQ) & (lax.rem(k, 3) == part))
            def _(part=part):
                pltpu.make_async_copy(
                    dw.at[k], dq_o.at[part, :, pl.ds(pl.multiple_of(k // 3 * CW, CW), CW)], dw_sem.at[k]
                ).start()
        send(NQ, NO, lambda n: do_o.at[:, pl.ds(n, CW)])
        send(NQ + NO, NF, lambda n: du_o.at[:, pl.ds(n, CW)])
        send(NQ + NO + NF, NF, lambda n: dd_o.at[:, pl.ds(n, CW)])

    def r4(p):
        k = ident(p)
        total = q[k, x, z, yy].astype(F32)
        for j in range(1, H):
            far_copy(k, lax.rem(z + j, H), j).wait_recv()
            total = total + farr[k, j - 1].astype(F32)
        dw[k] = total
        dw_out(k)

    stages = (r1, r2, r3, r4)

    before = [[sum(call[i] for call in CALLS[:n]) for n in range(len(CALLS) + 1)] for i in range(5)]
    place_no = [0]

    def serve(numbers, index=None):
        for i in (3, 2, 1, 0):
            counts = [CALLS[n][i] for n in numbers]
            starts = [before[i][n] for n in numbers]
            if index is None:
                for n in range(counts[0]):
                    stages[i](jnp.int32(starts[0] + n))
            elif max(counts) == 1:
                pl.when(pick(counts, index) > 0)(lambda i=i, starts=starts: stages[i](pick(starts, index)))
            elif max(counts) > 1:
                first = pick(starts, index)

                @pl.loop(first, first + pick(counts, index))
                def _(n, i=i):
                    stages[i](n)

    def serve_next():
        serve([place_no[0]])
        place_no[0] += 1

    gm_l.wait()
    gmt_l.wait()
    bnt_l.wait()

    def wchunk(n, half):
        return wb[lax.rem(n, WSLOTS), half].reshape(D, CW)

    def wnext(n):
        pl.when(n + WSLOTS < NCH)(lambda: wload(n + WSLOTS).start())

    GB = 64
    PR = HALF // PIECES
    mine = pl.ds(HALF * x, HALF)

    def piece(i, n):
        return pltpu.make_async_remote_copy(
            xb.at[:, pl.ds(HALF * (1 - x) + PR * n, PR)],
            igr.at[:, pl.ds(PR * n, PR)] if i else out_o.at[pl.ds(IMG * x, IMG), pl.ds(PR * n, PR)],
            piece_send.at[i, n], piece_recv.at[i, n], device_id=place.over_x(), device_id_type=MESH
        )

    acc[...] = jnp.zeros_like(acc)
    out_l.wait()
    out_c = pltpu.make_async_copy(xb.at[:, mine], out_o.at[pl.ds(IMG * x, IMG)], misc_sem.at[30])
    out_c.start()

    @pl.loop(0, NF)
    def _(j):
        s = lax.rem(j, 2)
        pl.when(j < PIECES)(lambda: piece(0, j).start())
        gl, gpl = gload(j)
        gl.wait()
        produce(2 * j, lhs1, lambda half: gb_buf[s, half])
        serve([4 * n for n in range(NF)], j)
        gpl.wait()
        wload(2 * j).wait()

        @pl.loop(0, 2)
        def _(half):
            zb[...] = dot(gm[...], wchunk(2 * j, half))

            @pl.loop(0, TOK // GB)
            def _(r):
                at = pl.ds(pl.multiple_of(r * GB, GB), GB)
                gz[half, at] = (zb[at] * gpb[s, half, at].astype(F32)).astype(BF)

        wnext(2 * j)

        @pl.when(j + 2 < NF)
        def _():
            for copy in gload(j + 2):
                copy.start()

        serve([4 * n + 1 for n in range(NF)], j)
        produce(2 * j + 1, lhs2, lambda half: gz[half])
        serve([4 * n + 2 for n in range(NF)], j)
        wload(2 * j + 1).wait()

        @pl.loop(0, 2)
        def _(half):
            acc[...] += dot(gz[half], wchunk(2 * j + 1, half), NT)

        wnext(2 * j + 1)
        serve([4 * n + 3 for n in range(NF)], j)

    place_no[0] = 4 * NF
    RB = 32

    def norm_back(values, grad, gain):
        centre = values - jnp.mean(values, axis=-1, keepdims=True)
        spread = jnp.mean(centre * centre, axis=-1, keepdims=True)
        scaled = lax.rsqrt(spread + EPS)
        unit = centre * scaled
        e = grad * gain
        first = jnp.mean(e, axis=-1, keepdims=True)
        second = jnp.mean(e * unit, axis=-1, keepdims=True)
        return scaled * (e - first - unit * second), grad * unit

    def fold(v):
        return jnp.sum(v.reshape(RB // 8, 8, D), axis=0)

    base = 2 * NF
    stat[...] = jnp.zeros_like(stat)
    gy_l.wait()
    h_l.wait()

    for part in range(2):
        count = TOK // RB // 2

        @pl.loop(part * count, (part + 1) * count)
        def _(r):
            at = pl.ds(pl.multiple_of(r * RB, RB), RB)
            back, product = norm_back(h[at], acc[at], totals[1:2])
            total = gh[at] + back
            gh[at] = total
            gm[at] = total.astype(BF)
            stat[1] += fold(product)

        serve_next()

    def transposed(src, dst):
        @pl.loop(0, D // 128)
        def _(d):
            t = jnp.transpose(src[:, pl.ds(pl.multiple_of(d * 128, 128), 128)].astype(F32))
            t = t.reshape(64 // R, 2, R, TOK)
            for p in range(2):
                dst[p, pl.ds(pl.multiple_of(d * 64, 64), 64)] = t[:, p].reshape(64, TOK).astype(BF)

    at_l = load(at_i, lhs2)
    transposed(gm, lhs1)
    o_l.wait()
    for k in range(NO):
        produce(jnp.int32(base + k), lhs1, lambda half, k=k: o[k, half].reshape(TOK, CW))
        serve_next()
        wload(jnp.int32(base + k)).wait()

        @pl.loop(0, 2)
        def _(half, k=k):
            go[k, half] = dot(gm[...], wchunk(jnp.int32(base + k), half)).astype(BF).reshape(IMG, SEQ, CW)

        wnext(jnp.int32(base + k))
        serve_next()
    proj_l.wait()
    lse_l.wait()
    lane = lax.broadcasted_iota(jnp.int32, (SEQ, CW), 1) // HDIM
    TN = (((0,), (0,)), ((), ()))

    def attend_back(group, u):
        half, i = u // IMG, lax.rem(u, IMG)
        qr, kr, vr = 3 * group, 3 * group + 1, 3 * group + 2
        query, key, val = proj[qr, half, i], proj[kr, half, i], proj[vr, half, i]
        grad = go[group, half, i]
        logs = lse[group, half, i]
        allowed = mask[pl.ds(IMG * x + i, 1)] > 0
        gq = jnp.zeros((SEQ, CW), F32)
        gk = jnp.zeros((SEQ, CW), F32)
        gv = jnp.zeros((SEQ, CW), F32)
        for head in range(CW // HDIM):
            of_head = lane == head
            qm = jnp.where(of_head, query, 0)
            gom = jnp.where(of_head, grad, 0)
            scores = jnp.where(allowed, dot(qm, key, NT) * scale, -1e30)
            soft = jnp.exp(scores - logs[:, head:head + 1])
            gsoft = dot(gom, val, NT)
            inner = jnp.sum(gsoft * soft, axis=-1, keepdims=True)
            gs = (soft * (gsoft - inner)).astype(BF)
            gq = gq + dot(gs, jnp.where(of_head, key, 0))
            gk = gk + dot(gs, qm, TN)
            gv = gv + dot(soft.astype(BF), gom, TN)
        proj[qr, half, i] = (gq * scale).astype(BF)
        proj[kr, half, i] = (gk * scale).astype(BF)
        proj[vr, half, i] = gv.astype(BF)

    acc[...] = jnp.zeros_like(acc)
    at_l.wait()
    out_c.wait()
    for n in range(PIECES):
        piece(0, n).wait_send()
    xs_l = load(xs_i, xb)

    n0 = place_no[0]
    per_group = 2 * IMG + 6
    place_no[0] += per_group * GRP

    def numbers(first, count):
        return [n0 + per_group * group + first + n for group in range(GRP) for n in range(count)]

    @pl.loop(0, GRP)
    def _(group):
        @pl.loop(0, 2 * IMG)
        def _(u):
            serve(numbers(0, 2 * IMG), 2 * IMG * group + u)
            attend_back(group, u)

        @pl.loop(0, 3)
        def _(n):
            serve(numbers(2 * IMG, 3), 3 * group + n)
            k = 3 * group + n
            produce(base + NO + k, lhs2, lambda half: proj[k, half].reshape(TOK, CW))

        @pl.loop(0, 3)
        def _(n):
            serve(numbers(2 * IMG + 3, 3), 3 * group + n)
            k = 3 * group + n
            wload(base + NO + k).wait()

            @pl.loop(0, 2)
            def _(half):
                acc[...] += dot(proj[k, half].reshape(TOK, CW), wchunk(base + NO + k, half), NT)

            wnext(base + NO + k)

    xs_l.wait()
    serve_next()
    per = SEQ // RB

    def finish(img, row, here):
        at = pl.ds(pl.multiple_of(img * SEQ + row, RB), RB)
        back, product = norm_back(xb[img, pl.ds(row, RB)].astype(F32), acc[at], totals[0:1])
        if here:
            gh[at] = gh[at] + back
        else:
            xb[img, pl.ds(row, RB)] = (gh[at] + back).astype(BF)
        stat[0] += fold(product)

    @pl.loop(0, PIECES)
    def _(n):
        @pl.loop(0, IMG)
        def _(img):
            finish(img, pl.multiple_of(HALF * (1 - x) + PR * n, RB), False)

        piece(1, n).start()

    serve_next()

    @pl.loop(0, PIECES)
    def _(n):
        @pl.loop(0, IMG)
        def _(img):
            finish(img, pl.multiple_of(HALF * x + PR * n, RB), True)

    ig_c = [pltpu.make_async_copy(gh.at[pl.ds(pl.multiple_of(i * SEQ + HALF * x, RB), HALF)], ig_o.at[IMG * x + i],
                                  misc_sem.at[26 + i]) for i in range(IMG)]
    for copy in ig_c:
        copy.start()
    ig_far = [pltpu.make_async_copy(acc.at[pl.ds(i * HALF, HALF)], ig_o.at[IMG * (1 - x) + i], misc_sem.at[28 + i])
              for i in range(IMG)]

    def take_far():
        for n in range(PIECES):
            piece(1, n).wait_recv()

        @pl.loop(0, HALF // RB)
        def _(r):
            row = pl.multiple_of(r * RB, RB)
            for i in range(IMG):
                acc[pl.ds(i * HALF + row, RB)] = igr[i, pl.ds(row, RB)].astype(F32)

        for copy in ig_far:
            copy.start()

    row = lax.broadcasted_iota(jnp.int32, (8, D), 0)
    small = jnp.where(row == 0, jnp.sum(stat[0], axis=0, keepdims=True),
                      jnp.where(row == 1, jnp.sum(stat[1], axis=0, keepdims=True),
                                jnp.tile(loss_i[...], (1, D // 128))))
    steps = (place.over_c(), place.over_y(), place.over_x())

    def small_sum(n):
        if 1 <= n <= 3:
            extra(sbuf.at[2 * n - 2], sbuf.at[2 * n - 1], 1 + n, steps[n - 1]).wait()
        value = small if n == 0 else sbuf[2 * n - 2] + sbuf[2 * n - 1] if n < 4 else None
        if n < 3:
            sbuf[2 * n] = value
            extra(sbuf.at[2 * n], sbuf.at[2 * n + 1], 2 + n, steps[n]).start()
        elif n == 3:
            zsum[z] = value
            for j in range(1, H):
                extra(zsum.at[z], zsum.at[z], 4 + j, place.far(j)).start()
        else:
            for j in range(1, H):
                extra(zsum.at[z], zsum.at[lax.rem(z + H - j, H)], 4 + j, place.far(j)).wait()
            total = jnp.sum(zsum[...], axis=0)
            stat_o[...] = jnp.where(row == 2, total / totals[2:3], total)

    done = [before[i][len(CALLS)] for i in range(5)]
    for n, i in enumerate(DRAIN):
        if n == len(DRAIN) - FAR_AT:
            take_far()
        if i < 4:
            stages[i](jnp.int32(done[i]))
        else:
            small_sum(done[i])
        done[i] += 1
    assert done == [NCH] * 4 + [5] and place_no[0] == len(CALLS)

    for copy in ig_c + ig_far:
        copy.wait()
    for n in range(PIECES):
        piece(0, n).wait_recv()
        piece(1, n).wait_send()

    @pl.loop(NCH - SLOTS, NCH)
    def _(p):
        core_copy(p).wait_send()

    @pl.loop(0, NCH)
    def _(k):
        pltpu.make_async_copy(dw.at[k], do_o.at[:, pl.ds(0, CW)], dw_sem.at[k]).wait()
        for i in range(3):
            near_copy(q.at[k, x, :, yy], k, i, place.over_x()).wait_send()
        for j in range(1, H):
            far_copy(k, z, j).wait_send()


def backward(cfg, saved, mask):
    (wg, at, proj, lse, o, h, bnt, g, gp, gy, gm, gmt, out, xs, ts, totals, loss) = saved
    H, R = cfg["groups"], cfg["rows"]
    NQ, NO, NF = cfg["nq"], cfg["no"], cfg["nf"]
    NCH = NQ + NO + 2 * NF
    IMG, SEQ, D = xs.shape
    TOK = IMG * SEQ
    lhs = (2, D // 2, TOK)
    half = (2, H, 2, R, CW)
    vm = pltpu.VMEM
    dma = pltpu.SemaphoreType.DMA
    return pl.pallas_call(
        functools.partial(bwd_kernel, cfg),
        name="backward_reduce",
        out_shape=[
            jax.ShapeDtypeStruct((2 * IMG, SEQ // 2, D), BF), jax.ShapeDtypeStruct((2 * IMG, SEQ // 2, D), F32),
            jax.ShapeDtypeStruct((3, R, NQ // 3 * CW), F32), jax.ShapeDtypeStruct((R, NO * CW), F32),
            jax.ShapeDtypeStruct((R, NF * CW), F32), jax.ShapeDtypeStruct((R, NF * CW), F32),
            jax.ShapeDtypeStruct((8, D), F32),
        ],
        in_specs=[any_spec()] * 14 + [vmem_spec()] * 3,
        out_specs=[any_spec()] * 6 + [vmem_spec()],
        scratch_shapes=[
            vm((NCH,) + half, BF), vm((SLOTS,) + half, BF), vm((SLOTS,) + half, BF),
            vm((NCH, 3, H, R, CW), BF), vm((NCH, H - 1, R, CW), BF), vm((NCH, R, CW), F32),
            vm((WSLOTS, 2, H, 2, 2, R, CW), BF), vm((2, 2, TOK, CW), BF), vm((2, 2, TOK, CW), BF),
            vm((2, TOK, CW), BF), vm((TOK, CW), F32), vm((TOK, D), BF), vm(lhs, BF), vm(lhs, BF),
            vm((TOK, D), F32), vm((TOK, D), F32), vm((TOK, D), F32), vm(o.shape, BF), vm(o.shape, BF),
            vm(proj.shape, BF), vm(lse.shape, F32), vm(xs.shape, BF),
            vm((IMG, SEQ // 2, D), BF), vm((2, 8, D), F32), vm((6, 8, D), F32), vm((H, 8, D), F32),
            dma((NCH,)), dma((NCH,)), pltpu.SemaphoreType.REGULAR, dma((NCH, 3)), dma((NCH, 3)),
            dma((NCH, H - 1)), dma((NCH, H - 1)), dma((H + 4,)), dma((H + 4,)), dma((2, PIECES)), dma((2, PIECES)),
            dma((NCH,)), dma((NF, 2)), dma((32,)), dma((NCH,)),
        ],
        compiler_params=pltpu.CompilerParams(
            collective_id=1, has_side_effects=True, vmem_limit_bytes=63 * 2**20
        ),
    )(wg, at, proj, lse, o, h, bnt, g, gp, gy, gm, gmt, out, xs, totals, loss, mask)


def per_device(
    inputs, teacher, keep_mask, gain_attn, qkv_weight, out_weight, gain_mlp, up_weight, down_weight
):
    cfg = config(inputs, (qkv_weight, out_weight, up_weight, down_weight))
    R = cfg["rows"]
    saved = forward(
        cfg, inputs, teacher, qkv_weight.transpose(1, 0, 2), out_weight, up_weight, down_weight,
        gain_attn.reshape(1, R), gain_mlp.reshape(1, R), keep_mask
    )
    output, input_grad, qkv_grad, out_grad, up_grad, down_grad, stats = backward(cfg, saved, keep_mask)
    gains = lax.dynamic_slice(stats, (0, lax.axis_index("dp") * R), (2, R))
    return (
        output, stats[2, 0], input_grad, gains[0], qkv_grad.transpose(1, 0, 2), out_grad, gains[1], up_grad, down_grad
    )


def solution(mesh):
    rows = P("dp", "mp", None)
    weight = P("dp", "mp")
    qkv = P("dp", None, "mp")
    return jax.shard_map(
        per_device,
        mesh=mesh,
        in_specs=(rows, rows, P("dp", None), P("dp"), qkv, weight, P("dp"), weight, weight),
        out_specs=(rows, P(), rows, P("dp"), qkv, weight, P("dp"), weight, weight),
        check_vma=False,
    )
```

```python
import functools
import jax
import jax.numpy as jnp
from jax import lax
from jax.experimental import pallas as pl
from jax.experimental.pallas import tpu as pltpu
from jax.sharding import PartitionSpec as P

MESH = pl.DeviceIdType.MESH
HDIM = 64
CW = 256
EPS = 1e-06
F32 = jnp.float32
BF = jnp.bfloat16
PIECES = 5
BOTH_X = (0, 1, 2, 3, 4, 8, 10, 12, 14, 17)
Z_LAST = (6, 9, 16)
X_WITH = (0, 1, 2, 3, 4)
T_WITH = (10, 12, 14, 15, 17)
FWD_CALLS = (
    (0, 0, 0), (0, 0, 0), (0, 0), (1, 0, 1, 0, 1, 0, 2, 1, 0, 1, 0, 2, 3, 1, 1, 0, 0, 4, 2, 1, 0, 3, 4, 2, 1, 0), (3,), (2,),
    (4, 1), (), (), (), (3, 2, 2, 2, 0), (1, 1, 1),
    (4, 3, 2, 2, 0, 0, 0), (1, 1), (), (4,), (3, 0, 0, 4), (),
    (3, 3, 2, 2), (1, 1), (4, 0), (), (4,), (3,),
    (2, 2), (4,), (1,), (3, 3, 1, 4), (2, 2), (4,),
    (3, 1), (3, 1, 4), (), (4,), (), (2, 1, 3, 4),
    (), (3, 2, 2, 2, 2, 2, 1, 1, 4), (), (3, 4), (), (3, 2),
    (3,), (2, 4), (3, 4), (3, 3, 4), (3, 4), (4,),
    (4,), (3, 3, 4), (4,),
)
NT = (((1,), (1,)), ((), ()))
NN = (((1,), (0,)), ((), ()))


def dot(a, b, dims=NN):
    return lax.dot_general(a, b, dims, preferred_element_type=F32)


class Place:
    def __init__(self, groups):
        self.groups = groups
        dp = lax.axis_index("dp")
        self.x = lax.axis_index("mp")
        self.c = lax.rem(dp, 2)
        self.y = lax.rem(dp // 2, 2)
        self.z = dp // 4

    def at(self, z, y, c, x):
        return {"dp": (z * 2 + y) * 2 + c, "mp": x}

    def far(self, j):
        return self.at(lax.rem(self.z + j, self.groups), self.y, self.c, self.x)

    def over_x(self):
        return self.at(self.z, self.y, self.c, 1 - self.x)

    def over_y(self):
        return self.at(self.z, 1 - self.y, self.c, self.x)

    def over_c(self):
        return self.at(self.z, self.y, 1 - self.c, self.x)

    def partners(self):
        return [self.far(j) for j in range(1, self.groups)] + [
            self.over_x(), self.over_y(), self.over_c()
        ]


def meet(place):
    barrier = pltpu.get_barrier_semaphore()
    partners = place.partners()
    for partner in partners:
        pl.semaphore_signal(barrier, 1, device_id=partner, device_id_type=MESH)
    pl.semaphore_wait(barrier, len(partners))


def member(k, numbers):
    if isinstance(k, int):
        return k in numbers
    found = False
    for n in numbers:
        found = (k == n) | found
    return found


def pick(table, index):
    value = jnp.int32(table[0])
    for n in range(1, len(table)):
        if table[n] != table[n - 1]:
            value = jnp.where(index >= n, table[n], value)
    return value


def when(cond, body):
    if isinstance(cond, bool):
        if cond:
            body()
    else:
        pl.when(cond)(body)


def fwd_kernel(cfg, xin, tin, wq, wo, wu, wd, gain_a, gain_m, mask, *refs):
    (wg_o, at_o, proj_o, lse_o, o_o, h_o, bnt_o, g_o, gp_o, gy_o, gm_o, gmt_o, out_o, xs_o, ts_o, sm_o, loss_o,
     wg, xs, ts, sm, own_sm, kpad, kcol, a, proj, o, lse, h, bn, g, gp, zb, y, tb,
     local_sem, send_sem, recv_sem, extra_send, extra_recv, piece_send, piece_recv, out_sem, misc_sem) = refs
    H, R = cfg["groups"], cfg["rows"]
    NQ, NO, NF = cfg["nq"], cfg["no"], cfg["nf"]
    NCH = NQ + NO + 2 * NF
    IMG, SEQ, D = xs.shape
    HALF = SEQ // 2
    TOK = IMG * SEQ
    GRP = NQ // 3
    place = Place(H)
    x, yy, z, c = place.x, place.y, place.z, place.c
    scale = HDIM ** (-0.5)

    def remote(ref, k, i, device):
        return pltpu.make_async_remote_copy(
            ref, ref, send_sem.at[k, i], recv_sem.at[k, i], device_id=device, device_id_type=MESH
        )

    def source(k):
        if k < NQ:
            return wq.at[k % 3, :, pl.ds((k // 3) * CW, CW)]
        if k < NQ + NO:
            return wo.at[:, pl.ds(CW * (k - NQ), CW)]
        if k < NQ + NO + NF:
            return wu.at[:, pl.ds(CW * (k - NQ - NO), CW)]
        return wd.at[:, pl.ds(CW * (k - NQ - NO - NF), CW)]

    def own(k):
        return pltpu.make_async_copy(source(k), wg.at[k, x, z, yy, c], local_sem.at[k])

    def own_wait(k):
        pltpu.make_async_copy(wq.at[0, :, pl.ds(0, CW)], wg.at[k, x, z, yy, c], local_sem.at[k]).wait()

    def relay(k):
        both = member(k, BOTH_X)
        first = jnp.where(both, 1, 1 - c) if not isinstance(both, bool) else (1 if both else 1 - c)
        xa = jnp.where(first == 1, 1 - x, x)
        ya = jnp.where(first == 1, yy, 1 - yy)
        return xa, ya, jnp.where(first == 1, x, 1 - x), jnp.where(first == 1, 1 - yy, yy)

    def either(k, late, early):
        last = member(k, Z_LAST)
        if isinstance(last, bool):
            (late if last else early)()
        else:
            pl.when(last)(late)
            pl.when(jnp.logical_not(last))(early)

    def s1(k):
        own_wait(k)
        own_block = wg.at[k, x, z, yy, c]
        xa, ya, xb, yb = relay(k)

        def late():
            remote(own_block, k, H - 1, place.at(z, ya, c, xa)).start()
            remote(own_block, k, H, place.at(z, yb, c, xb)).start()

        def early():
            for j in range(1, H):
                remote(own_block, k, j - 1, place.far(j)).start()

        either(k, late, early)

    def s2(k):
        xa, ya, xb, yb = relay(k)

        def late():
            block = wg.at[k, xa, z, ya, c]
            remote(block, k, H - 1, place.at(z, ya, c, xa)).wait_recv()
            remote(block, k, H + 1, place.at(z, yb, c, xb)).start()

        def early():
            for j in range(1, H):
                remote(wg.at[k, x, lax.rem(z + H - j, H), yy, c], k, j - 1, place.far(j)).wait_recv()
            piece_at(k)
            remote(wg.at[k, x, :, yy, c], k, H - 1, place.at(z, ya, c, xa)).start()
            remote(wg.at[k, x, :, yy, c], k, H, place.at(z, yb, c, xb)).start()

        either(k, late, early)

    def s3(k):
        xa, ya, xb, yb = relay(k)

        def late():
            remote(wg.at[k, xb, z, yb, c], k, H, place.at(z, yb, c, xb)).wait_recv()
            remote(wg.at[k, 1 - x, z, 1 - yy, c], k, H + 1, place.at(z, yb, c, xb)).wait_recv()
            for j in range(1, H):
                remote(wg.at[k, :, z, :, c], k, j - 1, place.far(j)).start()

        def early():
            remote(wg.at[k, xa, :, ya, c], k, H - 1, place.at(z, ya, c, xa)).wait_recv()
            remote(wg.at[k, xa, :, ya, c], k, H + 1, place.at(z, yb, c, xb)).start()

        either(k, late, early)

    def s4(k):
        xa, ya, xb, yb = relay(k)

        def late():
            for j in range(1, H):
                remote(wg.at[k, :, lax.rem(z + H - j, H), :, c], k, j - 1, place.far(j)).wait_recv()

        def early():
            remote(wg.at[k, xb, :, yb, c], k, H, place.at(z, yb, c, xb)).wait_recv()
            remote(wg.at[k, 1 - x, :, 1 - yy, c], k, H + 1, place.at(z, yb, c, xb)).wait_recv()

        either(k, late, early)
        remote(wg.at[k, :, :, :, c], k, H + 2, place.over_c()).start()

    def keep_chunk(k):
        return pltpu.make_async_copy(wg.at[k], wg_o.at[k], out_sem.at[k])

    def s5(k):
        remote(wg.at[k, :, :, :, 1 - c], k, H + 2, place.over_c()).wait_recv()
        keep_chunk(k).start()

    PR = HALF // PIECES

    def piece(i, n, to):
        src, dst = ((xin, xs), (tin, ts))[i]
        return pltpu.make_async_remote_copy(
            src.at[pl.ds(IMG * (1 - x), IMG), pl.ds(PR * n, PR)], dst.at[:, pl.ds(HALF * to + PR * n, PR)],
            piece_send.at[i, n], piece_recv.at[i, n], device_id=place.over_x(), device_id_type=MESH
        )

    def piece_at(k):
        for i, chunks in enumerate((X_WITH, T_WITH)):
            for n, chunk_no in enumerate(chunks):
                when(k == chunk_no, lambda i=i, n=n: piece(i, n, x).start())

    def pieces_in(i):
        for n in range(PIECES):
            piece(i, n, 1 - x).wait_recv()

    def settle(k):
        keep_chunk(k).wait()

        def late():
            for j in range(1, H):
                remote(wg.at[k, :, z, :, c], k, j - 1, place.far(j)).wait_send()
            for i in (H - 1, H, H + 1):
                remote(wg.at[k, x, z, yy, c], k, i, place.over_x()).wait_send()

        def early():
            for j in range(1, H):
                remote(wg.at[k, x, z, yy, c], k, j - 1, place.far(j)).wait_send()
            for i in (H - 1, H, H + 1):
                remote(wg.at[k, x, :, yy, c], k, i, place.over_x()).wait_send()

        either(k, late, early)
        remote(wg.at[k, :, :, :, c], k, H + 2, place.over_c()).wait_send()

    stages = (s1, s2, s3, s4, s5)
    pos = [0] * 5
    place_no = [0]

    def upcoming():
        calls = []
        for i in FWD_CALLS[place_no[0]]:
            calls.append((i, pos[i]))
            pos[i] += 1
        place_no[0] += 1
        return calls

    def serve():
        for i, n in upcoming():
            stages[i](n)

    def serve_in(index, calls, starts):
        for i in (4, 3, 2, 1, 0):
            counts = [call.count(i) for call in calls]
            if max(counts):
                first = pick(starts[i], index)

                @pl.loop(first, first + pick(counts, index))
                def _(n, i=i):
                    stages[i](n)

    def served(count):
        calls = FWD_CALLS[place_no[0]:place_no[0] + count]
        place_no[0] += count
        starts = [[pos[i] + sum(call.count(i) for call in calls[:n]) for n in range(count)] for i in range(5)]
        for i in range(5):
            pos[i] += sum(call.count(i) for call in calls)
        return calls, starts

    kept = []

    def keep(src, dst):
        copy = pltpu.make_async_copy(src, dst, misc_sem.at[len(kept)])
        copy.start()
        kept.append(copy)

    def extra(src, dst, i, device):
        return pltpu.make_async_remote_copy(
            src, dst, extra_send.at[i], extra_recv.at[i], device_id=device, device_id_type=MESH
        )

    for k in range(NCH):
        own(k).start()
    mine = pl.ds(HALF * x, HALF)
    xl = pltpu.make_async_copy(xin.at[pl.ds(IMG * x, IMG)], xs.at[:, mine], misc_sem.at[30])
    tl = pltpu.make_async_copy(tin.at[pl.ds(IMG * x, IMG)], ts.at[:, mine], misc_sem.at[31])
    spread = (lax.broadcasted_iota(jnp.int32, (R, D), 1)
              == lax.broadcasted_iota(jnp.int32, (R, D), 0) + lax.axis_index("dp") * R)
    spread = jnp.where(spread, 1.0, 0.0).astype(BF)
    line = lax.broadcasted_iota(jnp.int32, (8, D), 0)
    own_sm[...] = jnp.where(line == 0, dot(gain_a[...], spread),
                            jnp.where(line == 1, dot(gain_m[...], spread),
                                      jnp.sum(mask[...].astype(F32))))
    sl = pltpu.make_async_copy(own_sm, sm.at[z, yy, c], misc_sem.at[29])
    xl.start()
    tl.start()
    sl.start()
    meet(place)
    sl.wait()
    for j in range(1, H):
        extra(sm.at[z, yy, c], sm.at[z, yy, c], 3 + j, place.far(j)).start()
    serve()
    for j in range(1, H):
        extra(sm.at[z, yy, c], sm.at[lax.rem(z + H - j, H), yy, c], 3 + j, place.far(j)).wait_recv()
    extra(sm.at[:, yy, c], sm.at[:, yy, c], 2, place.over_y()).start()
    serve()
    extra(sm.at[:, 1 - yy, c], sm.at[:, 1 - yy, c], 2, place.over_y()).wait_recv()
    extra(sm.at[:, :, c], sm.at[:, :, c], 3, place.over_c()).start()
    kpad[...] = jnp.zeros_like(kpad)
    for i in range(IMG):
        kpad[:, 0:SEQ] = jnp.broadcast_to(mask[pl.ds(IMG * x + i, 1)].astype(F32), (128, SEQ))
        kcol[i] = jnp.transpose(kpad[...])[0:SEQ]
    serve()
    extra(sm.at[:, :, 1 - c], sm.at[:, :, 1 - c], 3, place.over_c()).wait_recv()
    totals = jnp.sum(sm[...].reshape(H * 4, 8, D), axis=0)
    sm_o[...] = totals
    xl.wait()
    serve()
    pieces_in(0)
    keep(xs, xs_o)

    RB = 64

    def rows_of(ref, r):
        per = SEQ // RB
        return ref[r // per, pl.ds(pl.multiple_of(lax.rem(r, per) * RB, RB), RB)]

    def norm_to(values, gain):
        centre = values - jnp.mean(values, axis=-1, keepdims=True)
        spread = jnp.mean(centre * centre, axis=-1, keepdims=True)
        return (centre * lax.rsqrt(spread + EPS) * gain).astype(BF)

    for part in range(2):
        count = TOK // RB // 2

        @pl.loop(part * count, (part + 1) * count)
        def _(r):
            a[pl.ds(pl.multiple_of(r * RB, RB), RB)] = norm_to(rows_of(xs, r).astype(F32), sm_o[0:1])

        serve()

    def transposed(src, dst):
        @pl.loop(0, D // 128)
        def _(d):
            t = jnp.transpose(src[:, pl.ds(pl.multiple_of(d * 128, 128), 128)].astype(F32))
            t = t.reshape(64 // R, 2, R, TOK)
            for p in range(2):
                dst[p, pl.ds(pl.multiple_of(d * 64, 64), 64)] = t[:, p].reshape(64, TOK).astype(BF)

    transposed(a, tb)
    keep(tb, at_o)
    serve()

    def chunk(k, half):
        return wg[k, half].reshape(D, CW)

    def project(k):
        @pl.loop(0, 2)
        def _(half):
            proj[k, half] = dot(a[...], chunk(k, half)).astype(BF).reshape(IMG, SEQ, CW)

    lane = lax.broadcasted_iota(jnp.int32, (SEQ, CW), 1) // HDIM

    def attend(group, u):
        half, i = u // IMG, lax.rem(u, IMG)
        q = proj[3 * group, half, i]
        key = proj[3 * group + 1, half, i]
        val = proj[3 * group + 2, half, i]
        allowed = mask[pl.ds(IMG * x + i, 1)] > 0
        total = jnp.zeros((SEQ, CW), F32)
        logs = jnp.zeros((SEQ, 128), F32)
        spot = lax.broadcasted_iota(jnp.int32, (SEQ, 128), 1)
        for head in range(CW // HDIM):
            scores = dot(jnp.where(lane == head, q, 0), key, NT) * scale
            scores = jnp.where(allowed, scores, -1e30)
            top = jnp.max(scores, axis=-1, keepdims=True)
            raised = jnp.exp(scores - top)
            norm = jnp.sum(raised, axis=-1, keepdims=True)
            soft = (raised / norm).astype(BF)
            total = total + dot(soft, jnp.where(lane == head, val, 0))
            logs = jnp.where(spot == head, top + jnp.log(norm), logs)
        o[group, half, i] = total.astype(BF)
        lse[group, half, i] = logs

    for group in range(GRP):
        for k in range(3 * group, 3 * group + 3):
            serve()
            project(k)
        places = served(2 * IMG)

        @pl.loop(0, 2 * IMG)
        def _(u, group=group, places=places):
            serve_in(u, *places)
            attend(group, u)

    keep(proj, proj_o)
    keep(lse, lse_o)
    keep(o, o_o)

    def gathered(src, k, half):
        return src[k, half].reshape(TOK, CW)

    h[...] = xs[...].reshape(TOK, D).astype(F32)
    for k in range(NO):
        serve()

        @pl.loop(0, 2)
        def _(half, k=k):
            h[...] += dot(gathered(o, k, half), chunk(NQ + k, half), NT)

    keep(h, h_o)

    for part in range(2):
        count = TOK // RB // 2
        serve()

        @pl.loop(part * count, (part + 1) * count)
        def _(r):
            at = pl.ds(pl.multiple_of(r * RB, RB), RB)
            bn[at] = norm_to(h[at], sm_o[1:2])

    first_up = NQ + NO

    def gelu(k, half):
        GB = 64

        @pl.loop(0, TOK // GB)
        def _(r):
            at = pl.ds(pl.multiple_of(r * GB, GB), GB)
            v = zb[at]
            cdf = 0.5 * (1.0 + lax.erf(v * 0.7071067811865476))
            g[k, half, at] = (v * cdf).astype(BF)
            gp[k, half, at] = (cdf + v * (jnp.exp(-0.5 * (v * v)) * 0.3989422804014327)).astype(BF)

    for k in range(NF):
        serve()
        calls = upcoming()

        @pl.loop(0, 2)
        def _(half, k=k, calls=calls):
            @pl.when(half == 1)
            def _():
                for i, n in calls:
                    stages[i](n)

            zb[...] = dot(bn[...], chunk(first_up + k, half))
            gelu(k, half)

    keep(g, g_o)
    keep(gp, gp_o)
    first_down = first_up + NF
    kept[1].wait()
    serve()
    transposed(bn, tb)
    keep(tb, bnt_o)
    serve()
    y[...] = h[...]

    for k in range(NF):
        serve()

        @pl.loop(0, 2)
        def _(half, k=k):
            y[...] += dot(g[k, half], chunk(first_down + k, half), NT)

        if 1 <= k < NF - 1:
            @pl.loop(3 * k - 3, 3 * k)
            def _(n):
                settle(n)

    assert pos == [NCH] * 5 and place_no[0] == len(FWD_CALLS)
    tl.wait()
    pieces_in(1)
    keep(ts, ts_o)
    zb[0:RB, 0:128] = jnp.zeros((RB, 128), F32)
    factor = 2.0 * cfg["tokens"] / sm_o[2:3]
    xs_ref = xs

    for copy in kept[:1]:
        copy.wait()

    @pl.loop(0, TOK // RB)
    def _(r):
        at = pl.ds(pl.multiple_of(r * RB, RB), RB)
        per = SEQ // RB
        img, pos = r // per, pl.multiple_of(lax.rem(r, per) * RB, RB)
        res = y[at]
        kept_rows = jnp.tile(kcol[img, pl.ds(pos, RB)], (1, D // 128))
        xs_ref[img, pl.ds(pos, RB)] = (res * kept_rows).astype(BF)
        error = res - ts[img, pl.ds(pos, RB)].astype(F32)
        squares = error * error * kept_rows
        part = squares[:, 0:128]
        for n in range(1, D // 128):
            part = part + squares[:, n * 128:(n + 1) * 128]
        zb[0:RB, 0:128] += part
        grad = factor * kept_rows * error
        y[at] = grad
        a[at] = grad.astype(BF)

    loss_o[...] = jnp.zeros_like(loss_o) + jnp.sum(zb[0:RB, 0:128]) * (1.0 / D)
    keep(xs, out_o)
    keep(y, gy_o)
    keep(a, gm_o)
    kept[8].wait()
    transposed(a, tb)
    keep(tb, gmt_o)
    for n, copy in enumerate(kept):
        if n not in (0, 1, 8):
            copy.wait()
    for i in range(2):
        for n in range(PIECES):
            piece(i, n, x).wait_send()
    for j in range(1, H):
        extra(sm.at[z, yy, c], sm.at[z, yy, c], 3 + j, place.far(j)).wait_send()
    extra(sm.at[:, yy, c], sm.at[:, yy, c], 2, place.over_y()).wait_send()
    extra(sm.at[:, :, c], sm.at[:, :, c], 3, place.over_c()).wait_send()

    @pl.loop(NCH - 6, NCH)
    def _(k):
        settle(k)


def any_spec():
    return pl.BlockSpec(memory_space=pl.ANY)


def vmem_spec():
    return pl.BlockSpec(memory_space=pltpu.VMEM)


def forward(cfg, xin, tin, wq, wo, wu, wd, gain_a, gain_m, mask):
    H, R = cfg["groups"], cfg["rows"]
    NQ, NO, NF = cfg["nq"], cfg["no"], cfg["nf"]
    NCH = NQ + NO + 2 * NF
    IMG = xin.shape[0] // 2
    SEQ, D = 2 * xin.shape[1], xin.shape[2]
    TOK = IMG * SEQ
    GRP = NQ // 3
    wg = (NCH, 2, H, 2, 2, R, CW)
    lhs = (2, D // 2, TOK)
    big = (NF, 2, TOK, CW)
    shapes = [
        (wg, BF), (lhs, BF), ((NQ, 2, IMG, SEQ, CW), BF), ((GRP, 2, IMG, SEQ, 128), F32),
        ((GRP, 2, IMG, SEQ, CW), BF), ((TOK, D), F32), (lhs, BF), (big, BF), (big, BF),
        ((TOK, D), F32), ((TOK, D), BF), (lhs, BF), ((IMG, SEQ, D), BF), ((IMG, SEQ, D), BF), ((IMG, SEQ, D), BF),
        ((8, D), F32), ((8, 128), F32),
    ]
    return pl.pallas_call(
        functools.partial(fwd_kernel, cfg),
        name="gather_forward",
        out_shape=[jax.ShapeDtypeStruct(s, t) for s, t in shapes],
        in_specs=[any_spec()] * 6 + [vmem_spec()] * 3,
        out_specs=[any_spec()] * 15 + [vmem_spec()] * 2,
        scratch_shapes=[
            pltpu.VMEM(wg, BF), pltpu.VMEM((IMG, SEQ, D), BF), pltpu.VMEM((IMG, SEQ, D), BF),
            pltpu.VMEM((H, 2, 2, 8, D), F32), pltpu.VMEM((8, D), F32), pltpu.VMEM((128, -(-SEQ // 128) * 128), F32),
            pltpu.VMEM((IMG, SEQ, 128), F32), pltpu.VMEM((TOK, D), BF),
            pltpu.VMEM((NQ, 2, IMG, SEQ, CW), BF), pltpu.VMEM((GRP, 2, IMG, SEQ, CW), BF),
            pltpu.VMEM((GRP, 2, IMG, SEQ, 128), F32), pltpu.VMEM((TOK, D), F32), pltpu.VMEM((TOK, D), BF),
            pltpu.VMEM(big, BF), pltpu.VMEM(big, BF), pltpu.VMEM((TOK, CW), F32), pltpu.VMEM((TOK, D), F32),
            pltpu.VMEM(lhs, BF),
            pltpu.SemaphoreType.DMA((NCH,)), pltpu.SemaphoreType.DMA((NCH, H + 3)),
            pltpu.SemaphoreType.DMA((NCH, H + 3)), pltpu.SemaphoreType.DMA((H + 4,)),
            pltpu.SemaphoreType.DMA((H + 4,)), pltpu.SemaphoreType.DMA((2, PIECES)),
            pltpu.SemaphoreType.DMA((2, PIECES)), pltpu.SemaphoreType.DMA((NCH,)), pltpu.SemaphoreType.DMA((32,)),
        ],
        compiler_params=pltpu.CompilerParams(
            collective_id=0, has_side_effects=True, vmem_limit_bytes=63 * 2**20
        ),
    )(xin, tin, wq, wo, wu, wd, gain_a, gain_m, mask)


def config(inputs, weights):
    rows = weights[0].shape[0]
    dps = lax.axis_size("dp")
    return {
        "groups": dps // 4,
        "rows": rows,
        "nq": weights[0].shape[1] * weights[0].shape[2] // CW,
        "no": weights[1].shape[1] // CW,
        "nf": weights[2].shape[1] // CW,
        "tokens": float(inputs.shape[0] * inputs.shape[1] * dps * lax.axis_size("mp")),
    }


SLOTS = 3
FAR_AT = 4
WSLOTS = 4
BACK_BOTH_X = (0, 4, 5, 10, 12, 15, 18, 23)
Z_FIRST = (2, 14, 22)
CALLS = (
    (0, 0, 0, 0, 0), (0, 0, 0, 0, 0), (1, 0, 0, 0, 0), (0, 0, 0, 0, 0), (1, 0, 0, 0, 0),
    (0, 0, 0, 0, 0), (1, 1, 0, 0, 0), (0, 0, 0, 0, 0), (1, 0, 0, 0, 0), (0, 1, 0, 0, 0),
    (1, 0, 0, 0, 0), (0, 0, 0, 0, 0), (1, 0, 0, 0, 0), (0, 0, 1, 0, 0), (1, 0, 1, 0, 0),
    (0, 0, 0, 0, 0), (1, 0, 0, 0, 0), (0, 3, 0, 0, 0), (1, 0, 0, 0, 0), (0, 0, 0, 1, 0),
    (1, 1, 0, 0, 0), (0, 0, 0, 1, 0), (1, 0, 0, 0, 0), (0, 1, 0, 0, 0), (1, 0, 0, 0, 0),
    (0, 0, 0, 0, 0), (1, 0, 0, 0, 0), (0, 1, 0, 0, 0), (1, 0, 0, 0, 0), (0, 0, 2, 0, 0),
    (1, 0, 0, 0, 0), (0, 0, 1, 0, 0), (1, 1, 0, 0, 0), (0, 0, 2, 0, 0), (0, 1, 1, 0, 0),
    (0, 0, 0, 2, 0), (1, 0, 0, 0, 0), (0, 0, 1, 0, 0), (0, 0, 0, 0, 0), (1, 1, 0, 0, 0),
    (0, 1, 0, 0, 0), (0, 0, 1, 1, 0), (0, 1, 2, 2, 0), (0, 2, 0, 0, 0), (0, 0, 0, 1, 0),
    (1, 1, 0, 0, 0), (1, 0, 1, 1, 0), (1, 0, 0, 0, 0), (0, 0, 1, 1, 0), (0, 1, 0, 1, 0),
    (0, 1, 0, 1, 0), (0, 0, 3, 1, 0), (0, 1, 1, 2, 0), (0, 1, 0, 0, 0), (0, 0, 0, 0, 0),
    (1, 0, 0, 1, 0), (1, 1, 1, 0, 0), (1, 0, 1, 1, 0), (0, 1, 0, 1, 0), (0, 0, 1, 1, 0),
)
DRAIN = (
    4, 4, 2, 4, 1, 1, 3, 2, 4, 3, 2, 3, 3, 4, 3,
)


def bwd_kernel(cfg, wg, at_i, proj_i, lse_i, o_i, h_i, bnt_i, g_i, gp_i, gy_i, gm_i, gmt_i, out_i, xs_i,
               totals, loss_i, mask, *refs):
    (out_o, ig_o, dq_o, do_o, du_o, dd_o, stat_o,
     q, snd, rcv, near, farr, crossed, dw, wb, gb_buf, gpb, gz, zb, gm, lhs1, lhs2, acc, gh, h, o, go, proj, lse, xb, igr, stat, sbuf, zsum,
     core_send, core_recv, credit, near_send, near_recv, far_send, far_recv, extra_send, extra_recv, piece_send, piece_recv,
     wsem, gsem, misc_sem, dw_sem) = refs
    H, R = cfg["groups"], cfg["rows"]
    NQ, NO, NF = cfg["nq"], cfg["no"], cfg["nf"]
    NCH = NQ + NO + 2 * NF
    IMG, SEQ, D = xb.shape
    HALF = SEQ // 2
    TOK = IMG * SEQ
    GRP = NQ // 3
    place = Place(H)
    x, yy, z, c = place.x, place.y, place.z, place.c
    scale = HDIM ** (-0.5)

    def ident(p):
        ff = jnp.where(lax.rem(p, 2) == 0, NQ + NO + NF + p // 2, NQ + NO + p // 2)
        return jnp.where(p < 2 * NF, ff, jnp.where(p < 2 * NF + NO, p - 2 * NF + NQ, p - 2 * NF - NO))

    def relay(p):
        both = member(p, BACK_BOTH_X)
        first = jnp.where(both, 1, 1 - c)
        xa = jnp.where(first == 1, 1 - x, x)
        ya = jnp.where(first == 1, yy, 1 - yy)
        return xa, ya, jnp.where(first == 1, x, 1 - x), jnp.where(first == 1, 1 - yy, yy)

    loads = []

    def load(src, dst):
        copy = pltpu.make_async_copy(src, dst, misc_sem.at[len(loads)])
        copy.start()
        loads.append(copy)
        return copy

    def wload(n):
        return pltpu.make_async_copy(wg.at[ident(n)], wb.at[lax.rem(n, WSLOTS)], wsem.at[n])

    def gload(j):
        s = lax.rem(j, 2)
        return (pltpu.make_async_copy(g_i.at[j], gb_buf.at[s], gsem.at[j, 0]),
                pltpu.make_async_copy(gp_i.at[j], gpb.at[s], gsem.at[j, 1]))

    gm_l = load(gm_i, gm)
    gmt_l = load(gmt_i, lhs1)
    for j in range(2):
        for copy in gload(jnp.int32(j)):
            copy.start()
    for n in range(WSLOTS):
        wload(jnp.int32(n)).start()
    bnt_l = load(bnt_i, lhs2)
    out_l = load(out_i, xb)
    gy_l = load(gy_i, gh)
    h_l = load(h_i, h)
    o_l = load(o_i, o)
    proj_l = load(proj_i, proj)
    lse_l = load(lse_i, lse)

    def extra(src, dst, i, device):
        return pltpu.make_async_remote_copy(
            src, dst, extra_send.at[i], extra_recv.at[i], device_id=device, device_id_type=MESH
        )

    meet(place)

    def core_copy(p, start=False):
        s = lax.rem(p, SLOTS)
        return pltpu.make_async_remote_copy(
            snd.at[s], rcv.at[s], core_send.at[p], core_recv.at[p], device_id=place.over_c(), device_id_type=MESH
        )

    def near_copy(src, k, i, device):
        return pltpu.make_async_remote_copy(
            src, near.at[k, i], near_send.at[k, i], near_recv.at[k, i], device_id=device, device_id_type=MESH
        )

    def crossing(p):
        slot = jnp.int32(0)
        for n, number in enumerate(Z_FIRST):
            slot = jnp.where(p == number, n, slot)
        return slot

    def cross_copy(p, k, j):
        return pltpu.make_async_remote_copy(
            q.at[k, :, lax.rem(z + j, H), :], crossed.at[crossing(p), j - 1], far_send.at[k, j - 1], far_recv.at[k, j - 1],
            device_id=place.far(j), device_id_type=MESH
        )

    def single_copy(src, k, i, device):
        return pltpu.make_async_remote_copy(
            src, near.at[k, i, 0], near_send.at[k, i], near_recv.at[k, i], device_id=device, device_id_type=MESH
        )

    def either(p, first, last):
        crosses = member(p, Z_FIRST)
        pl.when(crosses)(first)
        pl.when(jnp.logical_not(crosses))(last)

    def far_copy(k, zd, j):
        return pltpu.make_async_remote_copy(
            q.at[k, x, zd, yy], farr.at[k, j - 1], far_send.at[k, j - 1], far_recv.at[k, j - 1],
            device_id=place.far(j), device_id_type=MESH
        )

    def produce(p, lhs, rhs):
        k = ident(p)
        s = lax.rem(p, SLOTS)
        pl.when(p >= SLOTS)(lambda: core_copy(p - SLOTS).wait_send())

        @pl.loop(0, 2)
        def _(half):
            snd[s, half] = dot(lhs[1 - c], rhs(half)).astype(BF).reshape(H, 2, R, CW)
            q[k, half] = dot(lhs[c], rhs(half)).astype(BF).reshape(H, 2, R, CW)

        pl.when(p >= SLOTS)(lambda: pl.semaphore_wait(credit, 1))
        core_copy(p).start()

    def added(k, xi, yi, others):
        @pl.loop(0, H)
        def _(n):
            total = q[k, xi, n, yi].astype(F32)
            for other in others:
                total = total + near[k, other, n].astype(F32)
            q[k, xi, n, yi] = total.astype(BF)

    def r1(p):
        k = ident(p)
        s = lax.rem(p, SLOTS)
        core_copy(p).wait_recv()

        @pl.loop(0, 2 * H)
        def _(n):
            i, m = n // H, lax.rem(n, H)
            q[k, i, m] = q[k, i, m] + rcv[s, i, m]

        pl.when(p + SLOTS < NCH)(
            lambda: pl.semaphore_signal(credit, 1, device_id=place.over_c(), device_id_type=MESH)
        )
        xa, ya, xo, yo = relay(p)

        def cross():
            for j in range(1, H):
                cross_copy(p, k, j).start()

        def plain():
            near_copy(q.at[k, 1 - x, :, 1 - yy], k, 0, place.at(z, yo, c, xo)).start()
            near_copy(q.at[k, xo, :, yo], k, 1, place.at(z, yo, c, xo)).start()

        either(p, cross, plain)

    def r2(p):
        k = ident(p)
        xa, ya, xo, yo = relay(p)

        def cross():
            for j in range(1, H):
                cross_copy(p, k, j).wait_recv()
            slot = crossing(p)

            @pl.loop(0, 2)
            def _(i):
                for m in range(2):
                    total = q[k, i, z, m].astype(F32)
                    for j in range(1, H):
                        total = total + crossed[slot, j - 1, i, m].astype(F32)
                    q[k, i, z, m] = total.astype(BF)

            single_copy(q.at[k, 1 - x, z, 1 - yy], k, 0, place.at(z, yo, c, xo)).start()
            single_copy(q.at[k, xo, z, yo], k, 1, place.at(z, yo, c, xo)).start()

        def plain():
            near_copy(q.at[k, 1 - x, :, 1 - yy], k, 0, place.at(z, yo, c, xo)).wait_recv()
            added(k, xa, ya, (0,))
            near_copy(q.at[k, xa, :, ya], k, 2, place.at(z, ya, c, xa)).start()

        either(p, cross, plain)

    def r3(p):
        k = ident(p)
        xa, ya, xo, yo = relay(p)

        def cross():
            single_copy(q.at[k, 1 - x, z, 1 - yy], k, 0, place.at(z, yo, c, xo)).wait_recv()
            q[k, xa, z, ya] = (q[k, xa, z, ya].astype(F32) + near[k, 0, 0].astype(F32)).astype(BF)
            single_copy(q.at[k, xa, z, ya], k, 2, place.at(z, ya, c, xa)).start()

        def plain():
            near_copy(q.at[k, xo, :, yo], k, 1, place.at(z, yo, c, xo)).wait_recv()
            near_copy(q.at[k, xa, :, ya], k, 2, place.at(z, ya, c, xa)).wait_recv()
            added(k, x, yy, (1, 2))
            for j in range(1, H):
                far_copy(k, lax.rem(z + j, H), j).start()

        either(p, cross, plain)

    def dw_out(k):
        def send(first, count, at):
            @pl.when((k >= first) & (k < first + count))
            def _():
                pltpu.make_async_copy(dw.at[k], at(pl.multiple_of((k - first) * CW, CW)), dw_sem.at[k]).start()

        for part in range(3):
            @pl.when((k < NQ) & (lax.rem(k, 3) == part))
            def _(part=part):
                pltpu.make_async_copy(
                    dw.at[k], dq_o.at[part, :, pl.ds(pl.multiple_of(k // 3 * CW, CW), CW)], dw_sem.at[k]
                ).start()
        send(NQ, NO, lambda n: do_o.at[:, pl.ds(n, CW)])
        send(NQ + NO, NF, lambda n: du_o.at[:, pl.ds(n, CW)])
        send(NQ + NO + NF, NF, lambda n: dd_o.at[:, pl.ds(n, CW)])

    def r4(p):
        k = ident(p)
        xa, ya, xo, yo = relay(p)

        def cross():
            single_copy(q.at[k, xo, z, yo], k, 1, place.at(z, yo, c, xo)).wait_recv()
            single_copy(q.at[k, xa, z, ya], k, 2, place.at(z, ya, c, xa)).wait_recv()
            dw[k] = q[k, x, z, yy].astype(F32) + near[k, 1, 0].astype(F32) + near[k, 2, 0].astype(F32)

        def plain():
            total = q[k, x, z, yy].astype(F32)
            for j in range(1, H):
                far_copy(k, lax.rem(z + j, H), j).wait_recv()
                total = total + farr[k, j - 1].astype(F32)
            dw[k] = total

        either(p, cross, plain)
        dw_out(k)

    stages = (r1, r2, r3, r4)

    before = [[sum(call[i] for call in CALLS[:n]) for n in range(len(CALLS) + 1)] for i in range(5)]
    place_no = [0]

    def serve(numbers, index=None):
        for i in (3, 2, 1, 0):
            counts = [CALLS[n][i] for n in numbers]
            starts = [before[i][n] for n in numbers]
            if index is None:
                for n in range(counts[0]):
                    stages[i](jnp.int32(starts[0] + n))
            elif max(counts) == 1:
                pl.when(pick(counts, index) > 0)(lambda i=i, starts=starts: stages[i](pick(starts, index)))
            elif max(counts) > 1:
                first = pick(starts, index)

                @pl.loop(first, first + pick(counts, index))
                def _(n, i=i):
                    stages[i](n)

    def serve_next():
        serve([place_no[0]])
        place_no[0] += 1

    gm_l.wait()
    gmt_l.wait()
    bnt_l.wait()

    def wchunk(n, half):
        return wb[lax.rem(n, WSLOTS), half].reshape(D, CW)

    def wnext(n):
        pl.when(n + WSLOTS < NCH)(lambda: wload(n + WSLOTS).start())

    GB = 64
    PR = HALF // PIECES
    mine = pl.ds(HALF * x, HALF)

    def piece(i, n):
        return pltpu.make_async_remote_copy(
            xb.at[:, pl.ds(HALF * (1 - x) + PR * n, PR)],
            igr.at[:, pl.ds(PR * n, PR)] if i else out_o.at[pl.ds(IMG * x, IMG), pl.ds(PR * n, PR)],
            piece_send.at[i, n], piece_recv.at[i, n], device_id=place.over_x(), device_id_type=MESH
        )

    acc[...] = jnp.zeros_like(acc)
    out_l.wait()
    out_c = pltpu.make_async_copy(xb.at[:, mine], out_o.at[pl.ds(IMG * x, IMG)], misc_sem.at[30])
    out_c.start()

    @pl.loop(0, NF)
    def _(j):
        s = lax.rem(j, 2)
        pl.when(j < PIECES)(lambda: piece(0, j).start())
        gl, gpl = gload(j)
        gl.wait()
        produce(2 * j, lhs1, lambda half: gb_buf[s, half])
        serve([4 * n for n in range(NF)], j)
        gpl.wait()
        wload(2 * j).wait()

        @pl.loop(0, 2)
        def _(half):
            zb[...] = dot(gm[...], wchunk(2 * j, half))

            @pl.loop(0, TOK // GB)
            def _(r):
                at = pl.ds(pl.multiple_of(r * GB, GB), GB)
                gz[half, at] = (zb[at] * gpb[s, half, at].astype(F32)).astype(BF)

        wnext(2 * j)

        @pl.when(j + 2 < NF)
        def _():
            for copy in gload(j + 2):
                copy.start()

        serve([4 * n + 1 for n in range(NF)], j)
        produce(2 * j + 1, lhs2, lambda half: gz[half])
        serve([4 * n + 2 for n in range(NF)], j)
        wload(2 * j + 1).wait()

        @pl.loop(0, 2)
        def _(half):
            acc[...] += dot(gz[half], wchunk(2 * j + 1, half), NT)

        wnext(2 * j + 1)
        serve([4 * n + 3 for n in range(NF)], j)

    place_no[0] = 4 * NF
    RB = 32

    def norm_back(values, grad, gain):
        centre = values - jnp.mean(values, axis=-1, keepdims=True)
        spread = jnp.mean(centre * centre, axis=-1, keepdims=True)
        scaled = lax.rsqrt(spread + EPS)
        unit = centre * scaled
        e = grad * gain
        first = jnp.mean(e, axis=-1, keepdims=True)
        second = jnp.mean(e * unit, axis=-1, keepdims=True)
        return scaled * (e - first - unit * second), grad * unit

    def fold(v):
        return jnp.sum(v.reshape(-1, 8, D), axis=0)

    base = 2 * NF
    stat[...] = jnp.zeros_like(stat)
    gy_l.wait()
    h_l.wait()

    for part in range(2):
        count = TOK // GB // 2

        @pl.loop(part * count, (part + 1) * count)
        def _(r):
            at = pl.ds(pl.multiple_of(r * GB, GB), GB)
            back, product = norm_back(h[at], acc[at], totals[1:2])
            total = gh[at] + back
            gh[at] = total
            gm[at] = total.astype(BF)
            stat[1] += fold(product)

        serve_next()

    def transposed(src, dst):
        @pl.loop(0, D // 128)
        def _(d):
            t = jnp.transpose(src[:, pl.ds(pl.multiple_of(d * 128, 128), 128)].astype(F32))
            t = t.reshape(64 // R, 2, R, TOK)
            for p in range(2):
                dst[p, pl.ds(pl.multiple_of(d * 64, 64), 64)] = t[:, p].reshape(64, TOK).astype(BF)

    at_l = load(at_i, lhs2)
    transposed(gm, lhs1)
    o_l.wait()
    for k in range(NO):
        produce(jnp.int32(base + k), lhs1, lambda half, k=k: o[k, half].reshape(TOK, CW))
        serve_next()
        wload(jnp.int32(base + k)).wait()

        @pl.loop(0, 2)
        def _(half, k=k):
            go[k, half] = dot(gm[...], wchunk(jnp.int32(base + k), half)).astype(BF).reshape(IMG, SEQ, CW)

        wnext(jnp.int32(base + k))
        serve_next()
    proj_l.wait()
    lse_l.wait()
    lane = lax.broadcasted_iota(jnp.int32, (SEQ, CW), 1) // HDIM
    TN = (((0,), (0,)), ((), ()))

    def attend_back(group, u):
        half, i = u // IMG, lax.rem(u, IMG)
        qr, kr, vr = 3 * group, 3 * group + 1, 3 * group + 2
        query, key, val = proj[qr, half, i], proj[kr, half, i], proj[vr, half, i]
        grad = go[group, half, i]
        logs = lse[group, half, i]
        allowed = mask[pl.ds(IMG * x + i, 1)] > 0
        gq = jnp.zeros((SEQ, CW), F32)
        gk = jnp.zeros((SEQ, CW), F32)
        gv = jnp.zeros((SEQ, CW), F32)
        for head in range(CW // HDIM):
            of_head = lane == head
            qm = jnp.where(of_head, query, 0)
            gom = jnp.where(of_head, grad, 0)
            scores = jnp.where(allowed, dot(qm, key, NT) * scale, -1e30)
            soft = jnp.exp(scores - logs[:, head:head + 1])
            gsoft = dot(gom, val, NT)
            inner = jnp.sum(gsoft * soft, axis=-1, keepdims=True)
            gs = (soft * (gsoft - inner)).astype(BF)
            gq = gq + dot(gs, jnp.where(of_head, key, 0))
            gk = gk + dot(gs, qm, TN)
            gv = gv + dot(soft.astype(BF), gom, TN)
        proj[qr, half, i] = (gq * scale).astype(BF)
        proj[kr, half, i] = (gk * scale).astype(BF)
        proj[vr, half, i] = gv.astype(BF)

    acc[...] = jnp.zeros_like(acc)
    at_l.wait()
    out_c.wait()
    for n in range(PIECES):
        piece(0, n).wait_send()
    xs_l = load(xs_i, xb)

    n0 = place_no[0]
    per_group = 2 * IMG + 6
    place_no[0] += per_group * GRP

    def numbers(first, count):
        return [n0 + per_group * group + first + n for group in range(GRP) for n in range(count)]

    @pl.loop(0, GRP)
    def _(group):
        @pl.loop(0, 2 * IMG)
        def _(u):
            serve(numbers(0, 2 * IMG), 2 * IMG * group + u)
            attend_back(group, u)

        @pl.loop(0, 3)
        def _(n):
            serve(numbers(2 * IMG, 3), 3 * group + n)
            k = 3 * group + n
            produce(base + NO + k, lhs2, lambda half: proj[k, half].reshape(TOK, CW))

        @pl.loop(0, 3)
        def _(n):
            serve(numbers(2 * IMG + 3, 3), 3 * group + n)
            k = 3 * group + n
            wload(base + NO + k).wait()

            @pl.loop(0, 2)
            def _(half):
                acc[...] += dot(proj[k, half].reshape(TOK, CW), wchunk(base + NO + k, half), NT)

            wnext(base + NO + k)

    xs_l.wait()
    serve_next()
    per = SEQ // RB

    def finish(img, row, here):
        at = pl.ds(pl.multiple_of(img * SEQ + row, RB), RB)
        back, product = norm_back(xb[img, pl.ds(row, RB)].astype(F32), acc[at], totals[0:1])
        if here:
            gh[at] = gh[at] + back
        else:
            xb[img, pl.ds(row, RB)] = (gh[at] + back).astype(BF)
        stat[0] += fold(product)

    @pl.loop(0, PIECES)
    def _(n):
        @pl.loop(0, IMG)
        def _(img):
            finish(img, pl.multiple_of(HALF * (1 - x) + PR * n, RB), False)

        piece(1, n).start()

    serve_next()

    @pl.loop(0, PIECES)
    def _(n):
        @pl.loop(0, IMG)
        def _(img):
            finish(img, pl.multiple_of(HALF * x + PR * n, RB), True)

    ig_c = [pltpu.make_async_copy(gh.at[pl.ds(pl.multiple_of(i * SEQ + HALF * x, RB), HALF)], ig_o.at[IMG * x + i],
                                  misc_sem.at[26 + i]) for i in range(IMG)]
    for copy in ig_c:
        copy.start()
    ig_far = [pltpu.make_async_copy(acc.at[pl.ds(i * HALF, HALF)], ig_o.at[IMG * (1 - x) + i], misc_sem.at[28 + i])
              for i in range(IMG)]

    def take_far():
        for n in range(PIECES):
            piece(1, n).wait_recv()

        @pl.loop(0, HALF // RB)
        def _(r):
            row = pl.multiple_of(r * RB, RB)
            for i in range(IMG):
                acc[pl.ds(i * HALF + row, RB)] = igr[i, pl.ds(row, RB)].astype(F32)

        for copy in ig_far:
            copy.start()

    row = lax.broadcasted_iota(jnp.int32, (8, D), 0)
    small = jnp.where(row == 0, jnp.sum(stat[0], axis=0, keepdims=True),
                      jnp.where(row == 1, jnp.sum(stat[1], axis=0, keepdims=True),
                                jnp.tile(loss_i[...], (1, D // 128))))
    steps = (place.over_c(), place.over_y(), place.over_x())

    def small_sum(n):
        if 1 <= n <= 3:
            extra(sbuf.at[2 * n - 2], sbuf.at[2 * n - 1], 1 + n, steps[n - 1]).wait()
        value = small if n == 0 else sbuf[2 * n - 2] + sbuf[2 * n - 1] if n < 4 else None
        if n < 3:
            sbuf[2 * n] = value
            extra(sbuf.at[2 * n], sbuf.at[2 * n + 1], 2 + n, steps[n]).start()
        elif n == 3:
            zsum[z] = value
            for j in range(1, H):
                extra(zsum.at[z], zsum.at[z], 4 + j, place.far(j)).start()
        else:
            for j in range(1, H):
                extra(zsum.at[z], zsum.at[lax.rem(z + H - j, H)], 4 + j, place.far(j)).wait()
            total = jnp.sum(zsum[...], axis=0)
            stat_o[...] = jnp.where(row == 2, total / totals[2:3], total)

    def settle(p):
        k = ident(p)
        pltpu.make_async_copy(dw.at[k], do_o.at[:, pl.ds(0, CW)], dw_sem.at[k]).wait()

        def cross():
            for j in range(1, H):
                cross_copy(p, k, j).wait_send()
            for i in range(3):
                single_copy(q.at[k, x, z, yy], k, i, place.over_x()).wait_send()

        def plain():
            for i in range(3):
                near_copy(q.at[k, x, :, yy], k, i, place.over_x()).wait_send()
            for j in range(1, H):
                far_copy(k, z, j).wait_send()

        either(p, cross, plain)

    done = [before[i][len(CALLS)] for i in range(5)]
    settled = [0]
    for n, i in enumerate(DRAIN):
        if n == len(DRAIN) - FAR_AT:
            take_far()
        if settled[0] + 2 <= min(done[3], NCH - 6):
            for p in range(settled[0], settled[0] + 2):
                settle(jnp.int32(p))
            settled[0] += 2
        if i < 4:
            stages[i](jnp.int32(done[i]))
        else:
            small_sum(done[i])
        done[i] += 1
    assert done == [NCH] * 4 + [5] and place_no[0] == len(CALLS)

    for copy in ig_c + ig_far:
        copy.wait()
    for n in range(PIECES):
        piece(0, n).wait_recv()
        piece(1, n).wait_send()

    @pl.loop(NCH - SLOTS, NCH)
    def _(p):
        core_copy(p).wait_send()

    @pl.loop(settled[0], NCH)
    def _(p):
        settle(p)


def backward(cfg, saved, mask):
    (wg, at, proj, lse, o, h, bnt, g, gp, gy, gm, gmt, out, xs, ts, totals, loss) = saved
    H, R = cfg["groups"], cfg["rows"]
    NQ, NO, NF = cfg["nq"], cfg["no"], cfg["nf"]
    NCH = NQ + NO + 2 * NF
    IMG, SEQ, D = xs.shape
    TOK = IMG * SEQ
    lhs = (2, D // 2, TOK)
    half = (2, H, 2, R, CW)
    vm = pltpu.VMEM
    dma = pltpu.SemaphoreType.DMA
    return pl.pallas_call(
        functools.partial(bwd_kernel, cfg),
        name="backward_reduce",
        out_shape=[
            jax.ShapeDtypeStruct((2 * IMG, SEQ // 2, D), BF), jax.ShapeDtypeStruct((2 * IMG, SEQ // 2, D), F32),
            jax.ShapeDtypeStruct((3, R, NQ // 3 * CW), F32), jax.ShapeDtypeStruct((R, NO * CW), F32),
            jax.ShapeDtypeStruct((R, NF * CW), F32), jax.ShapeDtypeStruct((R, NF * CW), F32),
            jax.ShapeDtypeStruct((8, D), F32),
        ],
        in_specs=[any_spec()] * 14 + [vmem_spec()] * 3,
        out_specs=[any_spec()] * 6 + [vmem_spec()],
        scratch_shapes=[
            vm((NCH,) + half, BF), vm((SLOTS,) + half, BF), vm((SLOTS,) + half, BF),
            vm((NCH, 3, H, R, CW), BF), vm((NCH, H - 1, R, CW), BF),
            vm((max(len(Z_FIRST), 1), H - 1, 2, 2, R, CW), BF), vm((NCH, R, CW), F32),
            vm((WSLOTS, 2, H, 2, 2, R, CW), BF), vm((2, 2, TOK, CW), BF), vm((2, 2, TOK, CW), BF),
            vm((2, TOK, CW), BF), vm((TOK, CW), F32), vm((TOK, D), BF), vm(lhs, BF), vm(lhs, BF),
            vm((TOK, D), F32), vm((TOK, D), F32), vm((TOK, D), F32), vm(o.shape, BF), vm(o.shape, BF),
            vm(proj.shape, BF), vm(lse.shape, F32), vm(xs.shape, BF),
            vm((IMG, SEQ // 2, D), BF), vm((2, 8, D), F32), vm((6, 8, D), F32), vm((H, 8, D), F32),
            dma((NCH,)), dma((NCH,)), pltpu.SemaphoreType.REGULAR, dma((NCH, 3)), dma((NCH, 3)),
            dma((NCH, H - 1)), dma((NCH, H - 1)), dma((H + 4,)), dma((H + 4,)), dma((2, PIECES)), dma((2, PIECES)),
            dma((NCH,)), dma((NF, 2)), dma((32,)), dma((NCH,)),
        ],
        compiler_params=pltpu.CompilerParams(
            collective_id=1, has_side_effects=True, vmem_limit_bytes=63 * 2**20
        ),
    )(wg, at, proj, lse, o, h, bnt, g, gp, gy, gm, gmt, out, xs, totals, loss, mask)


def per_device(
    inputs, teacher, keep_mask, gain_attn, qkv_weight, out_weight, gain_mlp, up_weight, down_weight
):
    cfg = config(inputs, (qkv_weight, out_weight, up_weight, down_weight))
    R = cfg["rows"]
    saved = forward(
        cfg, inputs, teacher, qkv_weight.transpose(1, 0, 2), out_weight, up_weight, down_weight,
        gain_attn.reshape(1, R), gain_mlp.reshape(1, R), keep_mask
    )
    output, input_grad, qkv_grad, out_grad, up_grad, down_grad, stats = backward(cfg, saved, keep_mask)
    gains = lax.dynamic_slice(stats, (0, lax.axis_index("dp") * R), (2, R))
    return (
        output, stats[2, 0], input_grad, gains[0], qkv_grad.transpose(1, 0, 2), out_grad, gains[1], up_grad, down_grad
    )


def solution(mesh):
    rows = P("dp", "mp", None)
    weight = P("dp", "mp")
    qkv = P("dp", None, "mp")
    return jax.shard_map(
        per_device,
        mesh=mesh,
        in_specs=(rows, rows, P("dp", None), P("dp"), qkv, weight, P("dp"), weight, weight),
        out_specs=(rows, P(), rows, P("dp"), qkv, weight, P("dp"), weight, weight),
        check_vma=False,
    )
```

```python
import functools
import jax
import jax.numpy as jnp
from jax import lax
from jax.experimental import pallas as pl
from jax.experimental.pallas import tpu as pltpu
from jax.sharding import PartitionSpec as P

MESH = pl.DeviceIdType.MESH
HDIM = 64
CW = 256
EPS = 1e-06
F32 = jnp.float32
BF = jnp.bfloat16
PIECES = 5
BOTH_X = (0, 1, 2, 3, 4, 8, 10, 12, 14, 17)
Z_LAST = (6, 9, 16)
X_WITH = (0, 1, 2, 3, 4)
T_WITH = (10, 12, 14, 15, 17)
FWD_CALLS = (
    (0, 0, 0), (0, 0, 0), (0, 0), (1, 0, 1, 0, 1, 0, 2, 1, 0, 1, 0, 2, 3, 1, 1, 0, 0, 4, 2, 1, 0, 3, 4, 2, 1, 0), (3,), (2,),
    (4, 1), (), (), (), (3, 2, 2, 2, 0), (1, 1, 1),
    (4, 3, 2, 2, 0, 0, 0), (1, 1), (), (4,), (3, 0, 0, 4), (),
    (3, 3, 2, 2), (1, 1), (4, 0), (), (4,), (3,),
    (2, 2), (4,), (1,), (3, 3, 1, 4), (2, 2), (4,),
    (3, 1), (3, 1, 4), (), (4,), (), (2, 1, 3, 4),
    (), (3, 2, 2, 2, 2, 2, 1, 1, 4), (), (3, 4), (), (3, 2),
    (3,), (2, 4), (3, 4), (3, 3, 4), (3, 4), (4,),
    (4,), (3, 3, 4), (4,),
)
NT = (((1,), (1,)), ((), ()))
NN = (((1,), (0,)), ((), ()))


def dot(a, b, dims=NN):
    return lax.dot_general(a, b, dims, preferred_element_type=F32)


class Place:
    def __init__(self, groups):
        self.groups = groups
        dp = lax.axis_index("dp")
        self.x = lax.axis_index("mp")
        self.c = lax.rem(dp, 2)
        self.y = lax.rem(dp // 2, 2)
        self.z = dp // 4

    def at(self, z, y, c, x):
        return {"dp": (z * 2 + y) * 2 + c, "mp": x}

    def far(self, j):
        return self.at(lax.rem(self.z + j, self.groups), self.y, self.c, self.x)

    def over_x(self):
        return self.at(self.z, self.y, self.c, 1 - self.x)

    def over_y(self):
        return self.at(self.z, 1 - self.y, self.c, self.x)

    def over_c(self):
        return self.at(self.z, self.y, 1 - self.c, self.x)

    def partners(self):
        return [self.far(j) for j in range(1, self.groups)] + [
            self.over_x(), self.over_y(), self.over_c()
        ]


def meet(place):
    barrier = pltpu.get_barrier_semaphore()
    partners = place.partners()
    for partner in partners:
        pl.semaphore_signal(barrier, 1, device_id=partner, device_id_type=MESH)
    pl.semaphore_wait(barrier, len(partners))


def member(k, numbers):
    if isinstance(k, int):
        return k in numbers
    found = False
    for n in numbers:
        found = (k == n) | found
    return found


def pick(table, index):
    value = jnp.int32(table[0])
    for n in range(1, len(table)):
        if table[n] != table[n - 1]:
            value = jnp.where(index >= n, table[n], value)
    return value


def when(cond, body):
    if isinstance(cond, bool):
        if cond:
            body()
    else:
        pl.when(cond)(body)


def fwd_kernel(cfg, xin, tin, wq, wo, wu, wd, gain_a, gain_m, mask, *refs):
    (wg_o, at_o, proj_o, lse_o, o_o, h_o, bnt_o, g_o, gp_o, gy_o, gm_o, gmt_o, out_o, xs_o, ts_o, sm_o, loss_o,
     wg, xs, ts, sm, own_sm, kpad, kcol, a, proj, o, lse, h, bn, g, gp, zb, y, tb,
     local_sem, send_sem, recv_sem, extra_send, extra_recv, piece_send, piece_recv, out_sem, misc_sem) = refs
    H, R = cfg["groups"], cfg["rows"]
    NQ, NO, NF = cfg["nq"], cfg["no"], cfg["nf"]
    NCH = NQ + NO + 2 * NF
    IMG, SEQ, D = xs.shape
    HALF = SEQ // 2
    TOK = IMG * SEQ
    GRP = NQ // 3
    place = Place(H)
    x, yy, z, c = place.x, place.y, place.z, place.c
    scale = HDIM ** (-0.5)

    def remote(ref, k, i, device):
        return pltpu.make_async_remote_copy(
            ref, ref, send_sem.at[k, i], recv_sem.at[k, i], device_id=device, device_id_type=MESH
        )

    def source(k):
        if k < NQ:
            return wq.at[k % 3, :, pl.ds((k // 3) * CW, CW)]
        if k < NQ + NO:
            return wo.at[:, pl.ds(CW * (k - NQ), CW)]
        if k < NQ + NO + NF:
            return wu.at[:, pl.ds(CW * (k - NQ - NO), CW)]
        return wd.at[:, pl.ds(CW * (k - NQ - NO - NF), CW)]

    def own(k):
        return pltpu.make_async_copy(source(k), wg.at[k, x, z, yy, c], local_sem.at[k])

    def own_wait(k):
        pltpu.make_async_copy(wq.at[0, :, pl.ds(0, CW)], wg.at[k, x, z, yy, c], local_sem.at[k]).wait()

    def relay(k):
        both = member(k, BOTH_X)
        first = jnp.where(both, 1, 1 - c) if not isinstance(both, bool) else (1 if both else 1 - c)
        xa = jnp.where(first == 1, 1 - x, x)
        ya = jnp.where(first == 1, yy, 1 - yy)
        return xa, ya, jnp.where(first == 1, x, 1 - x), jnp.where(first == 1, 1 - yy, yy)

    def either(k, late, early):
        last = member(k, Z_LAST)
        if isinstance(last, bool):
            (late if last else early)()
        else:
            pl.when(last)(late)
            pl.when(jnp.logical_not(last))(early)

    def s1(k):
        own_wait(k)
        own_block = wg.at[k, x, z, yy, c]
        xa, ya, xb, yb = relay(k)

        def late():
            remote(own_block, k, H - 1, place.at(z, ya, c, xa)).start()
            remote(own_block, k, H, place.at(z, yb, c, xb)).start()

        def early():
            for j in range(1, H):
                remote(own_block, k, j - 1, place.far(j)).start()

        either(k, late, early)

    def s2(k):
        xa, ya, xb, yb = relay(k)

        def late():
            block = wg.at[k, xa, z, ya, c]
            remote(block, k, H - 1, place.at(z, ya, c, xa)).wait_recv()
            remote(block, k, H + 1, place.at(z, yb, c, xb)).start()

        def early():
            for j in range(1, H):
                remote(wg.at[k, x, lax.rem(z + H - j, H), yy, c], k, j - 1, place.far(j)).wait_recv()
            piece_at(k)
            remote(wg.at[k, x, :, yy, c], k, H - 1, place.at(z, ya, c, xa)).start()
            remote(wg.at[k, x, :, yy, c], k, H, place.at(z, yb, c, xb)).start()

        either(k, late, early)

    def s3(k):
        xa, ya, xb, yb = relay(k)

        def late():
            remote(wg.at[k, xb, z, yb, c], k, H, place.at(z, yb, c, xb)).wait_recv()
            remote(wg.at[k, 1 - x, z, 1 - yy, c], k, H + 1, place.at(z, yb, c, xb)).wait_recv()
            for j in range(1, H):
                remote(wg.at[k, :, z, :, c], k, j - 1, place.far(j)).start()

        def early():
            remote(wg.at[k, xa, :, ya, c], k, H - 1, place.at(z, ya, c, xa)).wait_recv()
            remote(wg.at[k, xa, :, ya, c], k, H + 1, place.at(z, yb, c, xb)).start()

        either(k, late, early)

    def s4(k):
        xa, ya, xb, yb = relay(k)

        def late():
            for j in range(1, H):
                remote(wg.at[k, :, lax.rem(z + H - j, H), :, c], k, j - 1, place.far(j)).wait_recv()

        def early():
            remote(wg.at[k, xb, :, yb, c], k, H, place.at(z, yb, c, xb)).wait_recv()
            remote(wg.at[k, 1 - x, :, 1 - yy, c], k, H + 1, place.at(z, yb, c, xb)).wait_recv()

        either(k, late, early)
        remote(wg.at[k, :, :, :, c], k, H + 2, place.over_c()).start()

    def keep_chunk(k):
        return pltpu.make_async_copy(wg.at[k], wg_o.at[k], out_sem.at[k])

    def s5(k):
        remote(wg.at[k, :, :, :, 1 - c], k, H + 2, place.over_c()).wait_recv()
        keep_chunk(k).start()

    PR = HALF // PIECES

    def piece(i, n, to):
        src, dst = ((xin, xs), (tin, ts))[i]
        return pltpu.make_async_remote_copy(
            src.at[pl.ds(IMG * (1 - x), IMG), pl.ds(PR * n, PR)], dst.at[:, pl.ds(HALF * to + PR * n, PR)],
            piece_send.at[i, n], piece_recv.at[i, n], device_id=place.over_x(), device_id_type=MESH
        )

    def piece_at(k):
        for i, chunks in enumerate((X_WITH, T_WITH)):
            for n, chunk_no in enumerate(chunks):
                when(k == chunk_no, lambda i=i, n=n: piece(i, n, x).start())

    def pieces_in(i):
        for n in range(PIECES):
            piece(i, n, 1 - x).wait_recv()

    def settle(k):
        keep_chunk(k).wait()

        def late():
            for j in range(1, H):
                remote(wg.at[k, :, z, :, c], k, j - 1, place.far(j)).wait_send()
            for i in (H - 1, H, H + 1):
                remote(wg.at[k, x, z, yy, c], k, i, place.over_x()).wait_send()

        def early():
            for j in range(1, H):
                remote(wg.at[k, x, z, yy, c], k, j - 1, place.far(j)).wait_send()
            for i in (H - 1, H, H + 1):
                remote(wg.at[k, x, :, yy, c], k, i, place.over_x()).wait_send()

        either(k, late, early)
        remote(wg.at[k, :, :, :, c], k, H + 2, place.over_c()).wait_send()

    stages = (s1, s2, s3, s4, s5)
    pos = [0] * 5
    place_no = [0]

    def upcoming():
        calls = []
        for i in FWD_CALLS[place_no[0]]:
            calls.append((i, pos[i]))
            pos[i] += 1
        place_no[0] += 1
        return calls

    def serve():
        for i, n in upcoming():
            stages[i](n)

    def serve_in(index, calls, starts):
        for i in (4, 3, 2, 1, 0):
            counts = [call.count(i) for call in calls]
            if max(counts):
                first = pick(starts[i], index)

                @pl.loop(first, first + pick(counts, index))
                def _(n, i=i):
                    stages[i](n)

    def served(count):
        calls = FWD_CALLS[place_no[0]:place_no[0] + count]
        place_no[0] += count
        starts = [[pos[i] + sum(call.count(i) for call in calls[:n]) for n in range(count)] for i in range(5)]
        for i in range(5):
            pos[i] += sum(call.count(i) for call in calls)
        return calls, starts

    kept = []

    def keep(src, dst):
        copy = pltpu.make_async_copy(src, dst, misc_sem.at[len(kept)])
        copy.start()
        kept.append(copy)

    def extra(src, dst, i, device):
        return pltpu.make_async_remote_copy(
            src, dst, extra_send.at[i], extra_recv.at[i], device_id=device, device_id_type=MESH
        )

    for k in range(NCH):
        own(k).start()
    mine = pl.ds(HALF * x, HALF)
    xl = pltpu.make_async_copy(xin.at[pl.ds(IMG * x, IMG)], xs.at[:, mine], misc_sem.at[30])
    tl = pltpu.make_async_copy(tin.at[pl.ds(IMG * x, IMG)], ts.at[:, mine], misc_sem.at[31])
    spread = (lax.broadcasted_iota(jnp.int32, (R, D), 1)
              == lax.broadcasted_iota(jnp.int32, (R, D), 0) + lax.axis_index("dp") * R)
    spread = jnp.where(spread, 1.0, 0.0).astype(BF)
    line = lax.broadcasted_iota(jnp.int32, (8, D), 0)
    own_sm[...] = jnp.where(line == 0, dot(gain_a[...], spread),
                            jnp.where(line == 1, dot(gain_m[...], spread),
                                      jnp.sum(mask[...].astype(F32))))
    sl = pltpu.make_async_copy(own_sm, sm.at[z, yy, c], misc_sem.at[29])
    xl.start()
    tl.start()
    sl.start()
    meet(place)
    sl.wait()
    for j in range(1, H):
        extra(sm.at[z, yy, c], sm.at[z, yy, c], 3 + j, place.far(j)).start()
    serve()
    for j in range(1, H):
        extra(sm.at[z, yy, c], sm.at[lax.rem(z + H - j, H), yy, c], 3 + j, place.far(j)).wait_recv()
    extra(sm.at[:, yy, c], sm.at[:, yy, c], 2, place.over_y()).start()
    serve()
    extra(sm.at[:, 1 - yy, c], sm.at[:, 1 - yy, c], 2, place.over_y()).wait_recv()
    extra(sm.at[:, :, c], sm.at[:, :, c], 3, place.over_c()).start()
    kpad[...] = jnp.zeros_like(kpad)
    for i in range(IMG):
        kpad[:, 0:SEQ] = jnp.broadcast_to(mask[pl.ds(IMG * x + i, 1)].astype(F32), (128, SEQ))
        kcol[i] = jnp.transpose(kpad[...])[0:SEQ]
    serve()
    extra(sm.at[:, :, 1 - c], sm.at[:, :, 1 - c], 3, place.over_c()).wait_recv()
    totals = jnp.sum(sm[...].reshape(H * 4, 8, D), axis=0)
    sm_o[...] = totals
    xl.wait()
    serve()
    pieces_in(0)
    keep(xs, xs_o)

    RB = 64

    def rows_of(ref, r):
        per = SEQ // RB
        return ref[r // per, pl.ds(pl.multiple_of(lax.rem(r, per) * RB, RB), RB)]

    def norm_to(values, gain):
        centre = values - jnp.mean(values, axis=-1, keepdims=True)
        spread = jnp.mean(centre * centre, axis=-1, keepdims=True)
        return (centre * lax.rsqrt(spread + EPS) * gain).astype(BF)

    for part in range(2):
        count = TOK // RB // 2

        @pl.loop(part * count, (part + 1) * count)
        def _(r):
            a[pl.ds(pl.multiple_of(r * RB, RB), RB)] = norm_to(rows_of(xs, r).astype(F32), sm_o[0:1])

        serve()

    def transposed(src, dst):
        @pl.loop(0, D // 128)
        def _(d):
            t = jnp.transpose(src[:, pl.ds(pl.multiple_of(d * 128, 128), 128)].astype(F32))
            t = t.reshape(64 // R, 2, R, TOK)
            for p in range(2):
                dst[p, pl.ds(pl.multiple_of(d * 64, 64), 64)] = t[:, p].reshape(64, TOK).astype(BF)

    transposed(a, tb)
    keep(tb, at_o)
    serve()

    def chunk(k, half):
        return wg[k, half].reshape(D, CW)

    def project(k):
        @pl.loop(0, 2)
        def _(half):
            proj[k, half] = dot(a[...], chunk(k, half)).astype(BF).reshape(IMG, SEQ, CW)

    lane = lax.broadcasted_iota(jnp.int32, (SEQ, CW), 1) // HDIM

    def attend(group, u):
        half, i = u // IMG, lax.rem(u, IMG)
        q = proj[3 * group, half, i]
        key = proj[3 * group + 1, half, i]
        val = proj[3 * group + 2, half, i]
        allowed = mask[pl.ds(IMG * x + i, 1)] > 0
        total = jnp.zeros((SEQ, CW), F32)
        logs = jnp.zeros((SEQ, 128), F32)
        spot = lax.broadcasted_iota(jnp.int32, (SEQ, 128), 1)
        for head in range(CW // HDIM):
            scores = dot(jnp.where(lane == head, q, 0), key, NT) * scale
            scores = jnp.where(allowed, scores, -1e30)
            top = jnp.max(scores, axis=-1, keepdims=True)
            raised = jnp.exp(scores - top)
            norm = jnp.sum(raised, axis=-1, keepdims=True)
            soft = (raised / norm).astype(BF)
            total = total + dot(soft, jnp.where(lane == head, val, 0))
            logs = jnp.where(spot == head, top + jnp.log(norm), logs)
        o[group, half, i] = total.astype(BF)
        lse[group, half, i] = logs

    for group in range(GRP):
        for k in range(3 * group, 3 * group + 3):
            serve()
            project(k)
        places = served(2 * IMG)

        @pl.loop(0, 2 * IMG)
        def _(u, group=group, places=places):
            serve_in(u, *places)
            attend(group, u)

    keep(proj, proj_o)
    keep(lse, lse_o)
    keep(o, o_o)

    def gathered(src, k, half):
        return src[k, half].reshape(TOK, CW)

    h[...] = xs[...].reshape(TOK, D).astype(F32)
    for k in range(NO):
        serve()

        @pl.loop(0, 2)
        def _(half, k=k):
            h[...] += dot(gathered(o, k, half), chunk(NQ + k, half), NT)

    keep(h, h_o)

    for part in range(2):
        count = TOK // RB // 2
        serve()

        @pl.loop(part * count, (part + 1) * count)
        def _(r):
            at = pl.ds(pl.multiple_of(r * RB, RB), RB)
            bn[at] = norm_to(h[at], sm_o[1:2])

    first_up = NQ + NO

    def gelu(k, half):
        GB = 64

        @pl.loop(0, TOK // GB)
        def _(r):
            at = pl.ds(pl.multiple_of(r * GB, GB), GB)
            v = zb[at]
            cdf = 0.5 * (1.0 + lax.erf(v * 0.7071067811865476))
            g[k, half, at] = (v * cdf).astype(BF)
            gp[k, half, at] = (cdf + v * (jnp.exp(-0.5 * (v * v)) * 0.3989422804014327)).astype(BF)

    for k in range(NF):
        serve()
        calls = upcoming()

        @pl.loop(0, 2)
        def _(half, k=k, calls=calls):
            @pl.when(half == 1)
            def _():
                for i, n in calls:
                    stages[i](n)

            zb[...] = dot(bn[...], chunk(first_up + k, half))
            gelu(k, half)

    keep(g, g_o)
    keep(gp, gp_o)
    first_down = first_up + NF
    kept[1].wait()
    serve()
    transposed(bn, tb)
    keep(tb, bnt_o)
    serve()
    y[...] = h[...]

    for k in range(NF):
        serve()

        @pl.loop(0, 2)
        def _(half, k=k):
            y[...] += dot(g[k, half], chunk(first_down + k, half), NT)

        if 1 <= k < NF - 1:
            @pl.loop(3 * k - 3, 3 * k)
            def _(n):
                settle(n)

    assert pos == [NCH] * 5 and place_no[0] == len(FWD_CALLS)
    tl.wait()
    pieces_in(1)
    keep(ts, ts_o)
    zb[0:RB, 0:128] = jnp.zeros((RB, 128), F32)
    factor = 2.0 * cfg["tokens"] / sm_o[2:3]
    xs_ref = xs

    for copy in kept[:1]:
        copy.wait()

    @pl.loop(0, TOK // RB)
    def _(r):
        at = pl.ds(pl.multiple_of(r * RB, RB), RB)
        per = SEQ // RB
        img, pos = r // per, pl.multiple_of(lax.rem(r, per) * RB, RB)
        res = y[at]
        kept_rows = jnp.tile(kcol[img, pl.ds(pos, RB)], (1, D // 128))
        xs_ref[img, pl.ds(pos, RB)] = (res * kept_rows).astype(BF)
        error = res - ts[img, pl.ds(pos, RB)].astype(F32)
        squares = error * error * kept_rows
        part = squares[:, 0:128]
        for n in range(1, D // 128):
            part = part + squares[:, n * 128:(n + 1) * 128]
        zb[0:RB, 0:128] += part
        grad = factor * kept_rows * error
        y[at] = grad
        a[at] = grad.astype(BF)

    loss_o[...] = jnp.zeros_like(loss_o) + jnp.sum(zb[0:RB, 0:128]) * (1.0 / D)
    keep(xs, out_o)
    keep(y, gy_o)
    keep(a, gm_o)
    kept[8].wait()
    transposed(a, tb)
    keep(tb, gmt_o)
    for n, copy in enumerate(kept):
        if n not in (0, 1, 8):
            copy.wait()
    for i in range(2):
        for n in range(PIECES):
            piece(i, n, x).wait_send()
    for j in range(1, H):
        extra(sm.at[z, yy, c], sm.at[z, yy, c], 3 + j, place.far(j)).wait_send()
    extra(sm.at[:, yy, c], sm.at[:, yy, c], 2, place.over_y()).wait_send()
    extra(sm.at[:, :, c], sm.at[:, :, c], 3, place.over_c()).wait_send()

    @pl.loop(NCH - 6, NCH)
    def _(k):
        settle(k)


def any_spec():
    return pl.BlockSpec(memory_space=pl.ANY)


def vmem_spec():
    return pl.BlockSpec(memory_space=pltpu.VMEM)


def forward(cfg, xin, tin, wq, wo, wu, wd, gain_a, gain_m, mask):
    H, R = cfg["groups"], cfg["rows"]
    NQ, NO, NF = cfg["nq"], cfg["no"], cfg["nf"]
    NCH = NQ + NO + 2 * NF
    IMG = xin.shape[0] // 2
    SEQ, D = 2 * xin.shape[1], xin.shape[2]
    TOK = IMG * SEQ
    GRP = NQ // 3
    wg = (NCH, 2, H, 2, 2, R, CW)
    lhs = (2, D // 2, TOK)
    big = (NF, 2, TOK, CW)
    shapes = [
        (wg, BF), (lhs, BF), ((NQ, 2, IMG, SEQ, CW), BF), ((GRP, 2, IMG, SEQ, 128), F32),
        ((GRP, 2, IMG, SEQ, CW), BF), ((TOK, D), F32), (lhs, BF), (big, BF), (big, BF),
        ((TOK, D), F32), ((TOK, D), BF), (lhs, BF), ((IMG, SEQ, D), BF), ((IMG, SEQ, D), BF), ((IMG, SEQ, D), BF),
        ((8, D), F32), ((8, 128), F32),
    ]
    return pl.pallas_call(
        functools.partial(fwd_kernel, cfg),
        name="gather_forward",
        out_shape=[jax.ShapeDtypeStruct(s, t) for s, t in shapes],
        in_specs=[any_spec()] * 6 + [vmem_spec()] * 3,
        out_specs=[any_spec()] * 15 + [vmem_spec()] * 2,
        scratch_shapes=[
            pltpu.VMEM(wg, BF), pltpu.VMEM((IMG, SEQ, D), BF), pltpu.VMEM((IMG, SEQ, D), BF),
            pltpu.VMEM((H, 2, 2, 8, D), F32), pltpu.VMEM((8, D), F32), pltpu.VMEM((128, -(-SEQ // 128) * 128), F32),
            pltpu.VMEM((IMG, SEQ, 128), F32), pltpu.VMEM((TOK, D), BF),
            pltpu.VMEM((NQ, 2, IMG, SEQ, CW), BF), pltpu.VMEM((GRP, 2, IMG, SEQ, CW), BF),
            pltpu.VMEM((GRP, 2, IMG, SEQ, 128), F32), pltpu.VMEM((TOK, D), F32), pltpu.VMEM((TOK, D), BF),
            pltpu.VMEM(big, BF), pltpu.VMEM(big, BF), pltpu.VMEM((TOK, CW), F32), pltpu.VMEM((TOK, D), F32),
            pltpu.VMEM(lhs, BF),
            pltpu.SemaphoreType.DMA((NCH,)), pltpu.SemaphoreType.DMA((NCH, H + 3)),
            pltpu.SemaphoreType.DMA((NCH, H + 3)), pltpu.SemaphoreType.DMA((H + 4,)),
            pltpu.SemaphoreType.DMA((H + 4,)), pltpu.SemaphoreType.DMA((2, PIECES)),
            pltpu.SemaphoreType.DMA((2, PIECES)), pltpu.SemaphoreType.DMA((NCH,)), pltpu.SemaphoreType.DMA((32,)),
        ],
        compiler_params=pltpu.CompilerParams(
            collective_id=0, has_side_effects=True, vmem_limit_bytes=63 * 2**20
        ),
    )(xin, tin, wq, wo, wu, wd, gain_a, gain_m, mask)


def config(inputs, weights):
    rows = weights[0].shape[0]
    dps = lax.axis_size("dp")
    return {
        "groups": dps // 4,
        "rows": rows,
        "nq": weights[0].shape[1] * weights[0].shape[2] // CW,
        "no": weights[1].shape[1] // CW,
        "nf": weights[2].shape[1] // CW,
        "tokens": float(inputs.shape[0] * inputs.shape[1] * dps * lax.axis_size("mp")),
    }


SLOTS = 3
FAR_AT = 4
WSLOTS = 4
BACK_BOTH_X = (6, 7, 8, 9, 14, 15, 23)
Z_FIRST = (3, 11, 22)
CALLS = (
    (0, 0, 0, 0, 0), (0, 0, 0, 0, 0), (0, 0, 0, 0, 0), (1, 0, 0, 0, 0), (1, 0, 0, 0, 0),
    (0, 0, 0, 0, 0), (1, 0, 0, 0, 0), (0, 1, 0, 0, 0), (1, 0, 0, 0, 0), (0, 0, 0, 0, 0),
    (1, 0, 0, 0, 0), (0, 0, 1, 0, 0), (1, 1, 0, 0, 0), (0, 0, 0, 0, 0), (1, 0, 0, 0, 0),
    (0, 0, 0, 0, 0), (1, 1, 0, 0, 0), (0, 0, 1, 0, 0), (1, 0, 0, 0, 0), (0, 1, 0, 0, 0),
    (1, 0, 0, 0, 0), (0, 1, 0, 1, 0), (1, 0, 1, 0, 0), (0, 0, 0, 1, 0), (1, 0, 0, 0, 0),
    (0, 3, 0, 0, 0), (1, 0, 0, 0, 0), (0, 0, 0, 1, 0), (1, 0, 0, 0, 0), (0, 1, 0, 0, 0),
    (1, 0, 0, 0, 0), (0, 0, 1, 0, 0), (1, 0, 0, 0, 0), (0, 1, 0, 0, 0), (0, 0, 1, 0, 0),
    (0, 0, 0, 0, 0), (0, 2, 0, 0, 0), (1, 0, 3, 0, 0), (1, 0, 0, 0, 0), (0, 1, 0, 0, 0),
    (0, 0, 1, 3, 0), (0, 1, 1, 1, 0), (0, 0, 1, 1, 0), (0, 1, 0, 1, 0), (0, 0, 0, 0, 0),
    (0, 0, 0, 0, 0), (1, 0, 0, 1, 0), (1, 1, 0, 0, 0), (1, 0, 3, 1, 0), (0, 1, 1, 0, 0),
    (0, 1, 1, 2, 0), (0, 1, 1, 1, 0), (0, 1, 1, 1, 0), (0, 0, 0, 1, 0), (0, 0, 1, 0, 0),
    (1, 0, 0, 0, 0), (0, 1, 1, 1, 0), (1, 0, 0, 1, 0), (1, 1, 0, 0, 0), (0, 0, 1, 1, 0),
)
DRAIN = (
    3, 2, 4, 4, 4, 1, 1, 3, 2, 4, 3, 2, 3, 4, 3,
)


def bwd_kernel(cfg, wg, at_i, proj_i, lse_i, o_i, h_i, bnt_i, g_i, gp_i, gy_i, gm_i, gmt_i, out_i, xs_i,
               totals, loss_i, mask, *refs):
    (out_o, ig_o, dq_o, do_o, du_o, dd_o, stat_o,
     q, snd, rcv, near, farr, crossed, dw, wb, gb_buf, gpb, gz, zb, gm, lhs1, lhs2, acc, gh, h, o, go, proj, lse, xb, igr, stat, sbuf, zsum,
     core_send, core_recv, credit, near_send, near_recv, far_send, far_recv, extra_send, extra_recv, piece_send, piece_recv,
     wsem, gsem, misc_sem, dw_sem) = refs
    H, R = cfg["groups"], cfg["rows"]
    NQ, NO, NF = cfg["nq"], cfg["no"], cfg["nf"]
    NCH = NQ + NO + 2 * NF
    IMG, SEQ, D = xb.shape
    HALF = SEQ // 2
    TOK = IMG * SEQ
    GRP = NQ // 3
    place = Place(H)
    x, yy, z, c = place.x, place.y, place.z, place.c
    scale = HDIM ** (-0.5)

    def ident(p):
        ff = jnp.where(lax.rem(p, 2) == 0, NQ + NO + NF + p // 2, NQ + NO + p // 2)
        return jnp.where(p < 2 * NF, ff, jnp.where(p < 2 * NF + NO, p - 2 * NF + NQ, p - 2 * NF - NO))

    def relay(p):
        both = member(p, BACK_BOTH_X)
        first = jnp.where(both, 1, 1 - c)
        xa = jnp.where(first == 1, 1 - x, x)
        ya = jnp.where(first == 1, yy, 1 - yy)
        return xa, ya, jnp.where(first == 1, x, 1 - x), jnp.where(first == 1, 1 - yy, yy)

    loads = []

    def load(src, dst):
        copy = pltpu.make_async_copy(src, dst, misc_sem.at[len(loads)])
        copy.start()
        loads.append(copy)
        return copy

    def wload(n):
        return pltpu.make_async_copy(wg.at[ident(n)], wb.at[lax.rem(n, WSLOTS)], wsem.at[n])

    def gload(j):
        s = lax.rem(j, 2)
        return (pltpu.make_async_copy(g_i.at[j], gb_buf.at[s], gsem.at[j, 0]),
                pltpu.make_async_copy(gp_i.at[j], gpb.at[s], gsem.at[j, 1]))

    gm_l = load(gm_i, gm)
    gmt_l = load(gmt_i, lhs1)
    for j in range(2):
        for copy in gload(jnp.int32(j)):
            copy.start()
    for n in range(WSLOTS):
        wload(jnp.int32(n)).start()
    bnt_l = load(bnt_i, lhs2)
    out_l = load(out_i, xb)
    gy_l = load(gy_i, gh)
    h_l = load(h_i, h)
    o_l = load(o_i, o)
    proj_l = load(proj_i, proj)
    lse_l = load(lse_i, lse)

    def extra(src, dst, i, device):
        return pltpu.make_async_remote_copy(
            src, dst, extra_send.at[i], extra_recv.at[i], device_id=device, device_id_type=MESH
        )

    meet(place)

    def core_copy(p, start=False):
        s = lax.rem(p, SLOTS)
        return pltpu.make_async_remote_copy(
            snd.at[s], rcv.at[s], core_send.at[p], core_recv.at[p], device_id=place.over_c(), device_id_type=MESH
        )

    def near_copy(src, k, i, device):
        return pltpu.make_async_remote_copy(
            src, near.at[k, i], near_send.at[k, i], near_recv.at[k, i], device_id=device, device_id_type=MESH
        )

    def crossing(p):
        slot = jnp.int32(0)
        for n, number in enumerate(Z_FIRST):
            slot = jnp.where(p == number, n, slot)
        return slot

    def cross_copy(p, k, j):
        return pltpu.make_async_remote_copy(
            q.at[k, :, lax.rem(z + j, H), :], crossed.at[crossing(p), j - 1], far_send.at[k, j - 1], far_recv.at[k, j - 1],
            device_id=place.far(j), device_id_type=MESH
        )

    def single_copy(src, k, i, device):
        return pltpu.make_async_remote_copy(
            src, near.at[k, i, 0], near_send.at[k, i], near_recv.at[k, i], device_id=device, device_id_type=MESH
        )

    def either(p, first, last):
        crosses = member(p, Z_FIRST)
        pl.when(crosses)(first)
        pl.when(jnp.logical_not(crosses))(last)

    def far_copy(k, zd, j):
        return pltpu.make_async_remote_copy(
            q.at[k, x, zd, yy], farr.at[k, j - 1], far_send.at[k, j - 1], far_recv.at[k, j - 1],
            device_id=place.far(j), device_id_type=MESH
        )

    def produce(p, lhs, rhs):
        k = ident(p)
        s = lax.rem(p, SLOTS)
        pl.when(p >= SLOTS)(lambda: core_copy(p - SLOTS).wait_send())

        @pl.loop(0, 2)
        def _(half):
            snd[s, half] = dot(lhs[1 - c], rhs(half)).astype(BF).reshape(H, 2, R, CW)
            q[k, half] = dot(lhs[c], rhs(half)).astype(BF).reshape(H, 2, R, CW)

        pl.when(p >= SLOTS)(lambda: pl.semaphore_wait(credit, 1))
        core_copy(p).start()

    def added(k, xi, yi, others):
        @pl.loop(0, H)
        def _(n):
            total = q[k, xi, n, yi].astype(F32)
            for other in others:
                total = total + near[k, other, n].astype(F32)
            q[k, xi, n, yi] = total.astype(BF)

    def r1(p):
        k = ident(p)
        s = lax.rem(p, SLOTS)
        core_copy(p).wait_recv()

        @pl.loop(0, 2 * H)
        def _(n):
            i, m = n // H, lax.rem(n, H)
            q[k, i, m] = q[k, i, m] + rcv[s, i, m]

        pl.when(p + SLOTS < NCH)(
            lambda: pl.semaphore_signal(credit, 1, device_id=place.over_c(), device_id_type=MESH)
        )
        xa, ya, xo, yo = relay(p)

        def cross():
            for j in range(1, H):
                cross_copy(p, k, j).start()

        def plain():
            near_copy(q.at[k, 1 - x, :, 1 - yy], k, 0, place.at(z, yo, c, xo)).start()
            near_copy(q.at[k, xo, :, yo], k, 1, place.at(z, yo, c, xo)).start()

        either(p, cross, plain)

    def r2(p):
        k = ident(p)
        xa, ya, xo, yo = relay(p)

        def cross():
            for j in range(1, H):
                cross_copy(p, k, j).wait_recv()
            slot = crossing(p)

            @pl.loop(0, 2)
            def _(i):
                for m in range(2):
                    total = q[k, i, z, m].astype(F32)
                    for j in range(1, H):
                        total = total + crossed[slot, j - 1, i, m].astype(F32)
                    q[k, i, z, m] = total.astype(BF)

            single_copy(q.at[k, 1 - x, z, 1 - yy], k, 0, place.at(z, yo, c, xo)).start()
            single_copy(q.at[k, xo, z, yo], k, 1, place.at(z, yo, c, xo)).start()

        def plain():
            near_copy(q.at[k, 1 - x, :, 1 - yy], k, 0, place.at(z, yo, c, xo)).wait_recv()
            added(k, xa, ya, (0,))
            near_copy(q.at[k, xa, :, ya], k, 2, place.at(z, ya, c, xa)).start()

        either(p, cross, plain)

    def r3(p):
        k = ident(p)
        xa, ya, xo, yo = relay(p)

        def cross():
            single_copy(q.at[k, 1 - x, z, 1 - yy], k, 0, place.at(z, yo, c, xo)).wait_recv()
            q[k, xa, z, ya] = (q[k, xa, z, ya].astype(F32) + near[k, 0, 0].astype(F32)).astype(BF)
            single_copy(q.at[k, xa, z, ya], k, 2, place.at(z, ya, c, xa)).start()

        def plain():
            near_copy(q.at[k, xo, :, yo], k, 1, place.at(z, yo, c, xo)).wait_recv()
            near_copy(q.at[k, xa, :, ya], k, 2, place.at(z, ya, c, xa)).wait_recv()
            added(k, x, yy, (1, 2))
            for j in range(1, H):
                far_copy(k, lax.rem(z + j, H), j).start()

        either(p, cross, plain)

    def dw_out(k):
        def send(first, count, at):
            @pl.when((k >= first) & (k < first + count))
            def _():
                pltpu.make_async_copy(dw.at[k], at(pl.multiple_of((k - first) * CW, CW)), dw_sem.at[k]).start()

        for part in range(3):
            @pl.when((k < NQ) & (lax.rem(k, 3) == part))
            def _(part=part):
                pltpu.make_async_copy(
                    dw.at[k], dq_o.at[part, :, pl.ds(pl.multiple_of(k // 3 * CW, CW), CW)], dw_sem.at[k]
                ).start()
        send(NQ, NO, lambda n: do_o.at[:, pl.ds(n, CW)])
        send(NQ + NO, NF, lambda n: du_o.at[:, pl.ds(n, CW)])
        send(NQ + NO + NF, NF, lambda n: dd_o.at[:, pl.ds(n, CW)])

    def r4(p):
        k = ident(p)
        xa, ya, xo, yo = relay(p)

        def cross():
            single_copy(q.at[k, xo, z, yo], k, 1, place.at(z, yo, c, xo)).wait_recv()
            single_copy(q.at[k, xa, z, ya], k, 2, place.at(z, ya, c, xa)).wait_recv()
            dw[k] = q[k, x, z, yy].astype(F32) + near[k, 1, 0].astype(F32) + near[k, 2, 0].astype(F32)

        def plain():
            total = q[k, x, z, yy].astype(F32)
            for j in range(1, H):
                far_copy(k, lax.rem(z + j, H), j).wait_recv()
                total = total + farr[k, j - 1].astype(F32)
            dw[k] = total

        either(p, cross, plain)
        dw_out(k)

    stages = (r1, r2, r3, r4)

    before = [[sum(call[i] for call in CALLS[:n]) for n in range(len(CALLS) + 1)] for i in range(5)]
    place_no = [0]

    def serve(numbers, index=None):
        for i in (3, 2, 1, 0):
            counts = [CALLS[n][i] for n in numbers]
            starts = [before[i][n] for n in numbers]
            if index is None:
                for n in range(counts[0]):
                    stages[i](jnp.int32(starts[0] + n))
            elif max(counts) == 1:
                pl.when(pick(counts, index) > 0)(lambda i=i, starts=starts: stages[i](pick(starts, index)))
            elif max(counts) > 1:
                first = pick(starts, index)

                @pl.loop(first, first + pick(counts, index))
                def _(n, i=i):
                    stages[i](n)

    def serve_next():
        serve([place_no[0]])
        place_no[0] += 1

    gm_l.wait()
    gmt_l.wait()
    bnt_l.wait()

    def wchunk(n, half):
        return wb[lax.rem(n, WSLOTS), half].reshape(D, CW)

    def wnext(n):
        pl.when(n + WSLOTS < NCH)(lambda: wload(n + WSLOTS).start())

    GB = 64
    PR = HALF // PIECES
    mine = pl.ds(HALF * x, HALF)

    def piece(i, n):
        return pltpu.make_async_remote_copy(
            xb.at[:, pl.ds(HALF * (1 - x) + PR * n, PR)],
            igr.at[:, pl.ds(PR * n, PR)] if i else out_o.at[pl.ds(IMG * x, IMG), pl.ds(PR * n, PR)],
            piece_send.at[i, n], piece_recv.at[i, n], device_id=place.over_x(), device_id_type=MESH
        )

    acc[...] = jnp.zeros_like(acc)
    out_l.wait()
    out_c = pltpu.make_async_copy(xb.at[:, mine], out_o.at[pl.ds(IMG * x, IMG)], misc_sem.at[30])
    out_c.start()

    @pl.loop(0, NF)
    def _(j):
        s = lax.rem(j, 2)
        pl.when(j < PIECES)(lambda: piece(0, j).start())
        gl, gpl = gload(j)
        gl.wait()
        produce(2 * j, lhs1, lambda half: gb_buf[s, half])
        serve([4 * n for n in range(NF)], j)
        gpl.wait()
        wload(2 * j).wait()

        @pl.loop(0, 2)
        def _(half):
            zb[...] = dot(gm[...], wchunk(2 * j, half))

            @pl.loop(0, TOK // GB)
            def _(r):
                at = pl.ds(pl.multiple_of(r * GB, GB), GB)
                gz[half, at] = (zb[at] * gpb[s, half, at].astype(F32)).astype(BF)

        wnext(2 * j)

        @pl.when(j + 2 < NF)
        def _():
            for copy in gload(j + 2):
                copy.start()

        serve([4 * n + 1 for n in range(NF)], j)
        produce(2 * j + 1, lhs2, lambda half: gz[half])
        serve([4 * n + 2 for n in range(NF)], j)
        wload(2 * j + 1).wait()

        @pl.loop(0, 2)
        def _(half):
            acc[...] += dot(gz[half], wchunk(2 * j + 1, half), NT)

        wnext(2 * j + 1)
        serve([4 * n + 3 for n in range(NF)], j)

    place_no[0] = 4 * NF
    RB = 32

    def norm_back(values, grad, gain):
        centre = values - jnp.mean(values, axis=-1, keepdims=True)
        spread = jnp.mean(centre * centre, axis=-1, keepdims=True)
        scaled = lax.rsqrt(spread + EPS)
        unit = centre * scaled
        e = grad * gain
        first = jnp.mean(e, axis=-1, keepdims=True)
        second = jnp.mean(e * unit, axis=-1, keepdims=True)
        return scaled * (e - first - unit * second), grad * unit

    def fold(v):
        return jnp.sum(v.reshape(-1, 8, D), axis=0)

    base = 2 * NF
    stat[...] = jnp.zeros_like(stat)
    gy_l.wait()
    h_l.wait()

    for part in range(2):
        count = TOK // GB // 2

        @pl.loop(part * count, (part + 1) * count)
        def _(r):
            at = pl.ds(pl.multiple_of(r * GB, GB), GB)
            back, product = norm_back(h[at], acc[at], totals[1:2])
            total = gh[at] + back
            gh[at] = total
            gm[at] = total.astype(BF)
            stat[1] += fold(product)

        serve_next()

    def transposed(src, dst):
        @pl.loop(0, D // 128)
        def _(d):
            t = jnp.transpose(src[:, pl.ds(pl.multiple_of(d * 128, 128), 128)].astype(F32))
            t = t.reshape(64 // R, 2, R, TOK)
            for p in range(2):
                dst[p, pl.ds(pl.multiple_of(d * 64, 64), 64)] = t[:, p].reshape(64, TOK).astype(BF)

    at_l = load(at_i, lhs2)
    transposed(gm, lhs1)
    o_l.wait()
    for k in range(NO):
        produce(jnp.int32(base + k), lhs1, lambda half, k=k: o[k, half].reshape(TOK, CW))
        serve_next()
        wload(jnp.int32(base + k)).wait()

        @pl.loop(0, 2)
        def _(half, k=k):
            go[k, half] = dot(gm[...], wchunk(jnp.int32(base + k), half)).astype(BF).reshape(IMG, SEQ, CW)

        wnext(jnp.int32(base + k))
        serve_next()
    proj_l.wait()
    lse_l.wait()
    lane = lax.broadcasted_iota(jnp.int32, (SEQ, CW), 1) // HDIM
    TN = (((0,), (0,)), ((), ()))

    def attend_back(group, u):
        half, i = u // IMG, lax.rem(u, IMG)
        qr, kr, vr = 3 * group, 3 * group + 1, 3 * group + 2
        query, key, val = proj[qr, half, i], proj[kr, half, i], proj[vr, half, i]
        grad = go[group, half, i]
        logs = lse[group, half, i]
        allowed = mask[pl.ds(IMG * x + i, 1)] > 0
        gq = jnp.zeros((SEQ, CW), F32)
        gk = jnp.zeros((SEQ, CW), F32)
        gv = jnp.zeros((SEQ, CW), F32)
        for head in range(CW // HDIM):
            of_head = lane == head
            qm = jnp.where(of_head, query, 0)
            gom = jnp.where(of_head, grad, 0)
            scores = jnp.where(allowed, dot(qm, key, NT) * scale, -1e30)
            soft = jnp.exp(scores - logs[:, head:head + 1])
            gsoft = dot(gom, val, NT)
            inner = jnp.sum(gsoft * soft, axis=-1, keepdims=True)
            gs = (soft * (gsoft - inner)).astype(BF)
            gq = gq + dot(gs, jnp.where(of_head, key, 0))
            gk = gk + dot(gs, qm, TN)
            gv = gv + dot(soft.astype(BF), gom, TN)
        proj[qr, half, i] = (gq * scale).astype(BF)
        proj[kr, half, i] = (gk * scale).astype(BF)
        proj[vr, half, i] = gv.astype(BF)

    acc[...] = jnp.zeros_like(acc)
    at_l.wait()
    out_c.wait()
    for n in range(PIECES):
        piece(0, n).wait_send()
    xs_l = load(xs_i, xb)

    n0 = place_no[0]
    per_group = 2 * IMG + 6
    place_no[0] += per_group * GRP

    def numbers(first, count):
        return [n0 + per_group * group + first + n for group in range(GRP) for n in range(count)]

    @pl.loop(0, GRP)
    def _(group):
        @pl.loop(0, 2 * IMG)
        def _(u):
            serve(numbers(0, 2 * IMG), 2 * IMG * group + u)
            attend_back(group, u)

        @pl.loop(0, 3)
        def _(n):
            serve(numbers(2 * IMG, 3), 3 * group + n)
            k = 3 * group + n
            produce(base + NO + k, lhs2, lambda half: proj[k, half].reshape(TOK, CW))

        @pl.loop(0, 3)
        def _(n):
            serve(numbers(2 * IMG + 3, 3), 3 * group + n)
            k = 3 * group + n
            wload(base + NO + k).wait()

            @pl.loop(0, 2)
            def _(half):
                acc[...] += dot(proj[k, half].reshape(TOK, CW), wchunk(base + NO + k, half), NT)

            wnext(base + NO + k)

    xs_l.wait()
    serve_next()
    per = SEQ // RB

    def finish(img, row, here):
        at = pl.ds(pl.multiple_of(img * SEQ + row, RB), RB)
        back, product = norm_back(xb[img, pl.ds(row, RB)].astype(F32), acc[at], totals[0:1])
        if here:
            gh[at] = gh[at] + back
        else:
            xb[img, pl.ds(row, RB)] = (gh[at] + back).astype(BF)
        stat[0] += fold(product)

    @pl.loop(0, PIECES)
    def _(n):
        @pl.loop(0, IMG)
        def _(img):
            finish(img, pl.multiple_of(HALF * (1 - x) + PR * n, RB), False)

        piece(1, n).start()

    serve_next()

    @pl.loop(0, PIECES)
    def _(n):
        @pl.loop(0, IMG)
        def _(img):
            finish(img, pl.multiple_of(HALF * x + PR * n, RB), True)

    ig_c = [pltpu.make_async_copy(gh.at[pl.ds(pl.multiple_of(i * SEQ + HALF * x, RB), HALF)], ig_o.at[IMG * x + i],
                                  misc_sem.at[26 + i]) for i in range(IMG)]
    for copy in ig_c:
        copy.start()
    ig_far = [pltpu.make_async_copy(acc.at[pl.ds(i * HALF, HALF)], ig_o.at[IMG * (1 - x) + i], misc_sem.at[28 + i])
              for i in range(IMG)]

    def take_far():
        for n in range(PIECES):
            piece(1, n).wait_recv()

        @pl.loop(0, HALF // RB)
        def _(r):
            row = pl.multiple_of(r * RB, RB)
            for i in range(IMG):
                acc[pl.ds(i * HALF + row, RB)] = igr[i, pl.ds(row, RB)].astype(F32)

        for copy in ig_far:
            copy.start()

    row = lax.broadcasted_iota(jnp.int32, (8, D), 0)
    small = jnp.where(row == 0, jnp.sum(stat[0], axis=0, keepdims=True),
                      jnp.where(row == 1, jnp.sum(stat[1], axis=0, keepdims=True),
                                jnp.tile(loss_i[...], (1, D // 128))))
    steps = (place.over_c(), place.over_y(), place.over_x())

    def small_sum(n):
        if 1 <= n <= 3:
            extra(sbuf.at[2 * n - 2], sbuf.at[2 * n - 1], 1 + n, steps[n - 1]).wait()
        value = small if n == 0 else sbuf[2 * n - 2] + sbuf[2 * n - 1] if n < 4 else None
        if n < 3:
            sbuf[2 * n] = value
            extra(sbuf.at[2 * n], sbuf.at[2 * n + 1], 2 + n, steps[n]).start()
        elif n == 3:
            zsum[z] = value
            for j in range(1, H):
                extra(zsum.at[z], zsum.at[z], 4 + j, place.far(j)).start()
        else:
            for j in range(1, H):
                extra(zsum.at[z], zsum.at[lax.rem(z + H - j, H)], 4 + j, place.far(j)).wait()
            total = jnp.sum(zsum[...], axis=0)
            stat_o[...] = jnp.where(row == 2, total / totals[2:3], total)

    def settle(p):
        k = ident(p)
        pltpu.make_async_copy(dw.at[k], do_o.at[:, pl.ds(0, CW)], dw_sem.at[k]).wait()

        def cross():
            for j in range(1, H):
                cross_copy(p, k, j).wait_send()
            for i in range(3):
                single_copy(q.at[k, x, z, yy], k, i, place.over_x()).wait_send()

        def plain():
            for i in range(3):
                near_copy(q.at[k, x, :, yy], k, i, place.over_x()).wait_send()
            for j in range(1, H):
                far_copy(k, z, j).wait_send()

        either(p, cross, plain)

    done = [before[i][len(CALLS)] for i in range(5)]
    settled = [0]
    for n, i in enumerate(DRAIN):
        if n == len(DRAIN) - FAR_AT:
            take_far()
        if settled[0] + 2 <= min(done[3], NCH - 6):
            for p in range(settled[0], settled[0] + 2):
                settle(jnp.int32(p))
            settled[0] += 2
        if i < 4:
            stages[i](jnp.int32(done[i]))
        else:
            small_sum(done[i])
        done[i] += 1
    assert done == [NCH] * 4 + [5] and place_no[0] == len(CALLS)

    for copy in ig_c + ig_far:
        copy.wait()
    for n in range(PIECES):
        piece(0, n).wait_recv()
        piece(1, n).wait_send()

    @pl.loop(NCH - SLOTS, NCH)
    def _(p):
        core_copy(p).wait_send()

    @pl.loop(settled[0], NCH)
    def _(p):
        settle(p)


def backward(cfg, saved, mask):
    (wg, at, proj, lse, o, h, bnt, g, gp, gy, gm, gmt, out, xs, ts, totals, loss) = saved
    H, R = cfg["groups"], cfg["rows"]
    NQ, NO, NF = cfg["nq"], cfg["no"], cfg["nf"]
    NCH = NQ + NO + 2 * NF
    IMG, SEQ, D = xs.shape
    TOK = IMG * SEQ
    lhs = (2, D // 2, TOK)
    half = (2, H, 2, R, CW)
    vm = pltpu.VMEM
    dma = pltpu.SemaphoreType.DMA
    return pl.pallas_call(
        functools.partial(bwd_kernel, cfg),
        name="backward_reduce",
        out_shape=[
            jax.ShapeDtypeStruct((2 * IMG, SEQ // 2, D), BF), jax.ShapeDtypeStruct((2 * IMG, SEQ // 2, D), F32),
            jax.ShapeDtypeStruct((3, R, NQ // 3 * CW), F32), jax.ShapeDtypeStruct((R, NO * CW), F32),
            jax.ShapeDtypeStruct((R, NF * CW), F32), jax.ShapeDtypeStruct((R, NF * CW), F32),
            jax.ShapeDtypeStruct((8, D), F32),
        ],
        in_specs=[any_spec()] * 14 + [vmem_spec()] * 3,
        out_specs=[any_spec()] * 6 + [vmem_spec()],
        scratch_shapes=[
            vm((NCH,) + half, BF), vm((SLOTS,) + half, BF), vm((SLOTS,) + half, BF),
            vm((NCH, 3, H, R, CW), BF), vm((NCH, H - 1, R, CW), BF),
            vm((max(len(Z_FIRST), 1), H - 1, 2, 2, R, CW), BF), vm((NCH, R, CW), F32),
            vm((WSLOTS, 2, H, 2, 2, R, CW), BF), vm((2, 2, TOK, CW), BF), vm((2, 2, TOK, CW), BF),
            vm((2, TOK, CW), BF), vm((TOK, CW), F32), vm((TOK, D), BF), vm(lhs, BF), vm(lhs, BF),
            vm((TOK, D), F32), vm((TOK, D), F32), vm((TOK, D), F32), vm(o.shape, BF), vm(o.shape, BF),
            vm(proj.shape, BF), vm(lse.shape, F32), vm(xs.shape, BF),
            vm((IMG, SEQ // 2, D), BF), vm((2, 8, D), F32), vm((6, 8, D), F32), vm((H, 8, D), F32),
            dma((NCH,)), dma((NCH,)), pltpu.SemaphoreType.REGULAR, dma((NCH, 3)), dma((NCH, 3)),
            dma((NCH, H - 1)), dma((NCH, H - 1)), dma((H + 4,)), dma((H + 4,)), dma((2, PIECES)), dma((2, PIECES)),
            dma((NCH,)), dma((NF, 2)), dma((32,)), dma((NCH,)),
        ],
        compiler_params=pltpu.CompilerParams(
            collective_id=1, has_side_effects=True, vmem_limit_bytes=63 * 2**20
        ),
    )(wg, at, proj, lse, o, h, bnt, g, gp, gy, gm, gmt, out, xs, totals, loss, mask)


def per_device(
    inputs, teacher, keep_mask, gain_attn, qkv_weight, out_weight, gain_mlp, up_weight, down_weight
):
    cfg = config(inputs, (qkv_weight, out_weight, up_weight, down_weight))
    R = cfg["rows"]
    saved = forward(
        cfg, inputs, teacher, qkv_weight.transpose(1, 0, 2), out_weight, up_weight, down_weight,
        gain_attn.reshape(1, R), gain_mlp.reshape(1, R), keep_mask
    )
    output, input_grad, qkv_grad, out_grad, up_grad, down_grad, stats = backward(cfg, saved, keep_mask)
    gains = lax.dynamic_slice(stats, (0, lax.axis_index("dp") * R), (2, R))
    return (
        output, stats[2, 0], input_grad, gains[0], qkv_grad.transpose(1, 0, 2), out_grad, gains[1], up_grad, down_grad
    )


def solution(mesh):
    rows = P("dp", "mp", None)
    weight = P("dp", "mp")
    qkv = P("dp", None, "mp")
    return jax.shard_map(
        per_device,
        mesh=mesh,
        in_specs=(rows, rows, P("dp", None), P("dp"), qkv, weight, P("dp"), weight, weight),
        out_specs=(rows, P(), rows, P("dp"), qkv, weight, P("dp"), weight, weight),
        check_vma=False,
    )
```

```python
import functools
import jax
import jax.numpy as jnp
from jax import lax
from jax.experimental import pallas as pl
from jax.experimental.pallas import tpu as pltpu
from jax.sharding import PartitionSpec as P

MESH = pl.DeviceIdType.MESH
HDIM = 64
CW = 256
EPS = 1e-06
F32 = jnp.float32
BF = jnp.bfloat16
PIECES = 5
BOTH_X = (0, 1, 2, 3, 4, 5, 8, 10, 14, 17, 19)
Z_LAST = (6, 13, 17)
X_WITH = (0, 1, 2, 3, 4)
T_WITH = (5, 11, 14, 16, 19)
FWD_CALLS = (
    (0, 0, 0), (0, 0, 0), (0, 0), (1, 0, 1, 0, 1, 0, 2, 1, 0, 1, 0, 3, 2, 1, 0, 4, 2, 1, 0, 3, 4, 2, 1, 0), (3,), (3, 2),
    (4, 1), (), (), (), (4, 2, 0), (3, 2, 1),
    (2, 1, 0), (4, 1, 0), (), (), (3, 2, 2, 1, 1, 0, 0, 0, 4), (),
    (), (2,), (3, 3, 1), (2, 1, 0, 0, 4), (3, 2, 4), (1,),
    (4, 3), (), (4, 2), (), (3, 1), (4,),
    (2, 2), (2, 3, 1, 1, 1, 4), (3,), (4,), (2, 2), (1, 1, 3, 3, 3, 4),
    (), (4,), (3,), (4,), (), (4,),
    (), (), (2, 2, 2, 2, 3, 1, 3, 4), (4,), (3, 2, 3, 4), (3, 4),
    (3, 4), (3, 4), (4,),
)
NT = (((1,), (1,)), ((), ()))
NN = (((1,), (0,)), ((), ()))


def dot(a, b, dims=NN):
    return lax.dot_general(a, b, dims, preferred_element_type=F32)


class Place:
    def __init__(self, groups):
        self.groups = groups
        dp = lax.axis_index("dp")
        self.x = lax.axis_index("mp")
        self.c = lax.rem(dp, 2)
        self.y = lax.rem(dp // 2, 2)
        self.z = dp // 4

    def at(self, z, y, c, x):
        return {"dp": (z * 2 + y) * 2 + c, "mp": x}

    def far(self, j):
        return self.at(lax.rem(self.z + j, self.groups), self.y, self.c, self.x)

    def over_x(self):
        return self.at(self.z, self.y, self.c, 1 - self.x)

    def over_y(self):
        return self.at(self.z, 1 - self.y, self.c, self.x)

    def over_c(self):
        return self.at(self.z, self.y, 1 - self.c, self.x)

    def partners(self):
        return [self.far(j) for j in range(1, self.groups)] + [
            self.over_x(), self.over_y(), self.over_c()
        ]


def meet(place):
    barrier = pltpu.get_barrier_semaphore()
    partners = place.partners()
    for partner in partners:
        pl.semaphore_signal(barrier, 1, device_id=partner, device_id_type=MESH)
    pl.semaphore_wait(barrier, len(partners))


def member(k, numbers):
    if isinstance(k, int):
        return k in numbers
    found = False
    for n in numbers:
        found = (k == n) | found
    return found


def pick(table, index):
    value = jnp.int32(table[0])
    for n in range(1, len(table)):
        if table[n] != table[n - 1]:
            value = jnp.where(index >= n, table[n], value)
    return value


def when(cond, body):
    if isinstance(cond, bool):
        if cond:
            body()
    else:
        pl.when(cond)(body)


def fwd_kernel(cfg, xin, tin, wq, wo, wu, wd, gain_a, gain_m, mask, *refs):
    (wg_o, at_o, proj_o, lse_o, o_o, h_o, bnt_o, g_o, gp_o, gy_o, gm_o, gmt_o, out_o, xs_o, ts_o, sm_o, loss_o,
     wg, xs, ts, sm, own_sm, kpad, kcol, a, proj, o, lse, h, bn, g, gp, zb, y, tb,
     local_sem, send_sem, recv_sem, extra_send, extra_recv, piece_send, piece_recv, out_sem, misc_sem) = refs
    H, R = cfg["groups"], cfg["rows"]
    NQ, NO, NF = cfg["nq"], cfg["no"], cfg["nf"]
    NCH = NQ + NO + 2 * NF
    IMG, SEQ, D = xs.shape
    HALF = SEQ // 2
    TOK = IMG * SEQ
    GRP = NQ // 3
    place = Place(H)
    x, yy, z, c = place.x, place.y, place.z, place.c
    scale = HDIM ** (-0.5)

    def remote(ref, k, i, device):
        return pltpu.make_async_remote_copy(
            ref, ref, send_sem.at[k, i], recv_sem.at[k, i], device_id=device, device_id_type=MESH
        )

    def source(k):
        if k < NQ:
            return wq.at[k % 3, :, pl.ds((k // 3) * CW, CW)]
        if k < NQ + NO:
            return wo.at[:, pl.ds(CW * (k - NQ), CW)]
        if k < NQ + NO + NF:
            return wu.at[:, pl.ds(CW * (k - NQ - NO), CW)]
        return wd.at[:, pl.ds(CW * (k - NQ - NO - NF), CW)]

    def own(k):
        return pltpu.make_async_copy(source(k), wg.at[k, x, z, yy, c], local_sem.at[k])

    def own_wait(k):
        pltpu.make_async_copy(wq.at[0, :, pl.ds(0, CW)], wg.at[k, x, z, yy, c], local_sem.at[k]).wait()

    def relay(k):
        both = member(k, BOTH_X)
        first = jnp.where(both, 1, 1 - c) if not isinstance(both, bool) else (1 if both else 1 - c)
        xa = jnp.where(first == 1, 1 - x, x)
        ya = jnp.where(first == 1, yy, 1 - yy)
        return xa, ya, jnp.where(first == 1, x, 1 - x), jnp.where(first == 1, 1 - yy, yy)

    def either(k, late, early):
        last = member(k, Z_LAST)
        if isinstance(last, bool):
            (late if last else early)()
        else:
            pl.when(last)(late)
            pl.when(jnp.logical_not(last))(early)

    def s1(k):
        own_wait(k)
        own_block = wg.at[k, x, z, yy, c]
        xa, ya, xb, yb = relay(k)

        def late():
            remote(own_block, k, H - 1, place.at(z, ya, c, xa)).start()
            remote(own_block, k, H, place.at(z, yb, c, xb)).start()

        def early():
            for j in range(1, H):
                remote(own_block, k, j - 1, place.far(j)).start()

        either(k, late, early)

    def s2(k):
        xa, ya, xb, yb = relay(k)

        def late():
            block = wg.at[k, xa, z, ya, c]
            remote(block, k, H - 1, place.at(z, ya, c, xa)).wait_recv()
            remote(block, k, H + 1, place.at(z, yb, c, xb)).start()

        def early():
            for j in range(1, H):
                remote(wg.at[k, x, lax.rem(z + H - j, H), yy, c], k, j - 1, place.far(j)).wait_recv()
            piece_at(k)
            remote(wg.at[k, x, :, yy, c], k, H - 1, place.at(z, ya, c, xa)).start()
            remote(wg.at[k, x, :, yy, c], k, H, place.at(z, yb, c, xb)).start()

        either(k, late, early)

    def s3(k):
        xa, ya, xb, yb = relay(k)

        def late():
            remote(wg.at[k, xb, z, yb, c], k, H, place.at(z, yb, c, xb)).wait_recv()
            remote(wg.at[k, 1 - x, z, 1 - yy, c], k, H + 1, place.at(z, yb, c, xb)).wait_recv()
            for j in range(1, H):
                remote(wg.at[k, :, z, :, c], k, j - 1, place.far(j)).start()

        def early():
            remote(wg.at[k, xa, :, ya, c], k, H - 1, place.at(z, ya, c, xa)).wait_recv()
            remote(wg.at[k, xa, :, ya, c], k, H + 1, place.at(z, yb, c, xb)).start()

        either(k, late, early)

    def s4(k):
        xa, ya, xb, yb = relay(k)

        def late():
            for j in range(1, H):
                remote(wg.at[k, :, lax.rem(z + H - j, H), :, c], k, j - 1, place.far(j)).wait_recv()

        def early():
            remote(wg.at[k, xb, :, yb, c], k, H, place.at(z, yb, c, xb)).wait_recv()
            remote(wg.at[k, 1 - x, :, 1 - yy, c], k, H + 1, place.at(z, yb, c, xb)).wait_recv()

        either(k, late, early)
        remote(wg.at[k, :, :, :, c], k, H + 2, place.over_c()).start()

    def keep_chunk(k):
        return pltpu.make_async_copy(wg.at[k], wg_o.at[k], out_sem.at[k])

    def s5(k):
        remote(wg.at[k, :, :, :, 1 - c], k, H + 2, place.over_c()).wait_recv()
        keep_chunk(k).start()

    PR = HALF // PIECES

    def piece(i, n, to):
        src, dst = ((xin, xs), (tin, ts))[i]
        return pltpu.make_async_remote_copy(
            src.at[pl.ds(IMG * (1 - x), IMG), pl.ds(PR * n, PR)], dst.at[:, pl.ds(HALF * to + PR * n, PR)],
            piece_send.at[i, n], piece_recv.at[i, n], device_id=place.over_x(), device_id_type=MESH
        )

    def piece_at(k):
        for i, chunks in enumerate((X_WITH, T_WITH)):
            for n, chunk_no in enumerate(chunks):
                when(k == chunk_no, lambda i=i, n=n: piece(i, n, x).start())

    def pieces_in(i):
        for n in range(PIECES):
            piece(i, n, 1 - x).wait_recv()

    def settle(k):
        keep_chunk(k).wait()

        def late():
            for j in range(1, H):
                remote(wg.at[k, :, z, :, c], k, j - 1, place.far(j)).wait_send()
            for i in (H - 1, H, H + 1):
                remote(wg.at[k, x, z, yy, c], k, i, place.over_x()).wait_send()

        def early():
            for j in range(1, H):
                remote(wg.at[k, x, z, yy, c], k, j - 1, place.far(j)).wait_send()
            for i in (H - 1, H, H + 1):
                remote(wg.at[k, x, :, yy, c], k, i, place.over_x()).wait_send()

        either(k, late, early)
        remote(wg.at[k, :, :, :, c], k, H + 2, place.over_c()).wait_send()

    stages = (s1, s2, s3, s4, s5)
    pos = [0] * 5
    place_no = [0]

    def upcoming():
        calls = []
        for i in FWD_CALLS[place_no[0]]:
            calls.append((i, pos[i]))
            pos[i] += 1
        place_no[0] += 1
        return calls

    def serve():
        for i, n in upcoming():
            stages[i](n)

    def serve_in(index, calls, starts):
        for i in (4, 3, 2, 1, 0):
            counts = [call.count(i) for call in calls]
            if max(counts):
                first = pick(starts[i], index)

                @pl.loop(first, first + pick(counts, index))
                def _(n, i=i):
                    stages[i](n)

    def served(count):
        calls = FWD_CALLS[place_no[0]:place_no[0] + count]
        place_no[0] += count
        starts = [[pos[i] + sum(call.count(i) for call in calls[:n]) for n in range(count)] for i in range(5)]
        for i in range(5):
            pos[i] += sum(call.count(i) for call in calls)
        return calls, starts

    kept = []

    def keep(src, dst):
        copy = pltpu.make_async_copy(src, dst, misc_sem.at[len(kept)])
        copy.start()
        kept.append(copy)

    def extra(src, dst, i, device):
        return pltpu.make_async_remote_copy(
            src, dst, extra_send.at[i], extra_recv.at[i], device_id=device, device_id_type=MESH
        )

    for k in range(NCH):
        own(k).start()
    mine = pl.ds(HALF * x, HALF)
    xl = pltpu.make_async_copy(xin.at[pl.ds(IMG * x, IMG)], xs.at[:, mine], misc_sem.at[30])
    tl = pltpu.make_async_copy(tin.at[pl.ds(IMG * x, IMG)], ts.at[:, mine], misc_sem.at[31])
    spread = (lax.broadcasted_iota(jnp.int32, (R, D), 1)
              == lax.broadcasted_iota(jnp.int32, (R, D), 0) + lax.axis_index("dp") * R)
    spread = jnp.where(spread, 1.0, 0.0).astype(BF)
    line = lax.broadcasted_iota(jnp.int32, (8, D), 0)
    own_sm[...] = jnp.where(line == 0, dot(gain_a[...], spread),
                            jnp.where(line == 1, dot(gain_m[...], spread),
                                      jnp.sum(mask[...].astype(F32))))
    sl = pltpu.make_async_copy(own_sm, sm.at[z, yy, c], misc_sem.at[29])
    xl.start()
    tl.start()
    sl.start()
    meet(place)
    sl.wait()
    for j in range(1, H):
        extra(sm.at[z, yy, c], sm.at[z, yy, c], 3 + j, place.far(j)).start()
    serve()
    for j in range(1, H):
        extra(sm.at[z, yy, c], sm.at[lax.rem(z + H - j, H), yy, c], 3 + j, place.far(j)).wait_recv()
    extra(sm.at[:, yy, c], sm.at[:, yy, c], 2, place.over_y()).start()
    serve()
    extra(sm.at[:, 1 - yy, c], sm.at[:, 1 - yy, c], 2, place.over_y()).wait_recv()
    extra(sm.at[:, :, c], sm.at[:, :, c], 3, place.over_c()).start()
    kpad[...] = jnp.zeros_like(kpad)
    for i in range(IMG):
        kpad[:, 0:SEQ] = jnp.broadcast_to(mask[pl.ds(IMG * x + i, 1)].astype(F32), (128, SEQ))
        kcol[i] = jnp.transpose(kpad[...])[0:SEQ]
    serve()
    extra(sm.at[:, :, 1 - c], sm.at[:, :, 1 - c], 3, place.over_c()).wait_recv()
    totals = jnp.sum(sm[...].reshape(H * 4, 8, D), axis=0)
    sm_o[...] = totals
    xl.wait()
    serve()
    pieces_in(0)
    keep(xs, xs_o)

    RB = 64

    def rows_of(ref, r):
        per = SEQ // RB
        return ref[r // per, pl.ds(pl.multiple_of(lax.rem(r, per) * RB, RB), RB)]

    def norm_to(values, gain):
        centre = values - jnp.mean(values, axis=-1, keepdims=True)
        spread = jnp.mean(centre * centre, axis=-1, keepdims=True)
        return (centre * lax.rsqrt(spread + EPS) * gain).astype(BF)

    for part in range(2):
        count = TOK // RB // 2

        @pl.loop(part * count, (part + 1) * count)
        def _(r):
            a[pl.ds(pl.multiple_of(r * RB, RB), RB)] = norm_to(rows_of(xs, r).astype(F32), sm_o[0:1])

        serve()

    def transposed(src, dst):
        @pl.loop(0, D // 128)
        def _(d):
            t = jnp.transpose(src[:, pl.ds(pl.multiple_of(d * 128, 128), 128)].astype(F32))
            t = t.reshape(64 // R, 2, R, TOK)
            for p in range(2):
                dst[p, pl.ds(pl.multiple_of(d * 64, 64), 64)] = t[:, p].reshape(64, TOK).astype(BF)

    transposed(a, tb)
    keep(tb, at_o)
    serve()

    def chunk(k, half):
        return wg[k, half].reshape(D, CW)

    def project(k):
        @pl.loop(0, 2)
        def _(half):
            proj[k, half] = dot(a[...], chunk(k, half)).astype(BF).reshape(IMG, SEQ, CW)

    lane = lax.broadcasted_iota(jnp.int32, (SEQ, CW), 1) // HDIM

    def attend(group, u):
        half, i = u // IMG, lax.rem(u, IMG)
        q = proj[3 * group, half, i]
        key = proj[3 * group + 1, half, i]
        val = proj[3 * group + 2, half, i]
        allowed = mask[pl.ds(IMG * x + i, 1)] > 0
        total = jnp.zeros((SEQ, CW), F32)
        logs = jnp.zeros((SEQ, 128), F32)
        spot = lax.broadcasted_iota(jnp.int32, (SEQ, 128), 1)
        for head in range(CW // HDIM):
            scores = dot(jnp.where(lane == head, q, 0), key, NT) * scale
            scores = jnp.where(allowed, scores, -1e30)
            top = jnp.max(scores, axis=-1, keepdims=True)
            raised = jnp.exp(scores - top)
            norm = jnp.sum(raised, axis=-1, keepdims=True)
            soft = (raised / norm).astype(BF)
            total = total + dot(soft, jnp.where(lane == head, val, 0))
            logs = jnp.where(spot == head, top + jnp.log(norm), logs)
        o[group, half, i] = total.astype(BF)
        lse[group, half, i] = logs

    for group in range(GRP):
        for k in range(3 * group, 3 * group + 3):
            serve()
            project(k)
        places = served(2 * IMG)

        @pl.loop(0, 2 * IMG)
        def _(u, group=group, places=places):
            serve_in(u, *places)
            attend(group, u)

    keep(proj, proj_o)
    keep(lse, lse_o)
    keep(o, o_o)

    def gathered(src, k, half):
        return src[k, half].reshape(TOK, CW)

    h[...] = xs[...].reshape(TOK, D).astype(F32)
    for k in range(NO):
        serve()

        @pl.loop(0, 2)
        def _(half, k=k):
            h[...] += dot(gathered(o, k, half), chunk(NQ + k, half), NT)

    keep(h, h_o)

    for part in range(2):
        count = TOK // RB // 2
        serve()

        @pl.loop(part * count, (part + 1) * count)
        def _(r):
            at = pl.ds(pl.multiple_of(r * RB, RB), RB)
            bn[at] = norm_to(h[at], sm_o[1:2])

    first_up = NQ + NO

    def gelu(k, half):
        GB = 64

        @pl.loop(0, TOK // GB)
        def _(r):
            at = pl.ds(pl.multiple_of(r * GB, GB), GB)
            v = zb[at]
            cdf = 0.5 * (1.0 + lax.erf(v * 0.7071067811865476))
            g[k, half, at] = (v * cdf).astype(BF)
            gp[k, half, at] = (cdf + v * (jnp.exp(-0.5 * (v * v)) * 0.3989422804014327)).astype(BF)

    for k in range(NF):
        serve()
        calls = upcoming()

        @pl.loop(0, 2)
        def _(half, k=k, calls=calls):
            @pl.when(half == 1)
            def _():
                for i, n in calls:
                    stages[i](n)

            zb[...] = dot(bn[...], chunk(first_up + k, half))
            gelu(k, half)

    keep(g, g_o)
    keep(gp, gp_o)
    first_down = first_up + NF
    kept[1].wait()
    serve()
    transposed(bn, tb)
    keep(tb, bnt_o)
    serve()
    y[...] = h[...]

    for k in range(NF):
        serve()

        @pl.loop(0, 2)
        def _(half, k=k):
            y[...] += dot(g[k, half], chunk(first_down + k, half), NT)

        if 1 <= k < NF - 1:
            @pl.loop(3 * k - 3, 3 * k)
            def _(n):
                settle(n)

    assert pos == [NCH] * 5 and place_no[0] == len(FWD_CALLS)
    tl.wait()
    pieces_in(1)
    keep(ts, ts_o)
    zb[0:RB, 0:128] = jnp.zeros((RB, 128), F32)
    factor = 2.0 * cfg["tokens"] / sm_o[2:3]
    xs_ref = xs

    for copy in kept[:1]:
        copy.wait()

    @pl.loop(0, TOK // RB)
    def _(r):
        at = pl.ds(pl.multiple_of(r * RB, RB), RB)
        per = SEQ // RB
        img, pos = r // per, pl.multiple_of(lax.rem(r, per) * RB, RB)
        res = y[at]
        kept_rows = jnp.tile(kcol[img, pl.ds(pos, RB)], (1, D // 128))
        xs_ref[img, pl.ds(pos, RB)] = (res * kept_rows).astype(BF)
        error = res - ts[img, pl.ds(pos, RB)].astype(F32)
        squares = error * error * kept_rows
        part = squares[:, 0:128]
        for n in range(1, D // 128):
            part = part + squares[:, n * 128:(n + 1) * 128]
        zb[0:RB, 0:128] += part
        grad = factor * kept_rows * error
        y[at] = grad
        a[at] = grad.astype(BF)

    loss_o[...] = jnp.zeros_like(loss_o) + jnp.sum(zb[0:RB, 0:128]) * (1.0 / D)
    keep(xs, out_o)
    keep(y, gy_o)
    keep(a, gm_o)
    kept[8].wait()
    transposed(a, tb)
    keep(tb, gmt_o)
    for n, copy in enumerate(kept):
        if n not in (0, 1, 8):
            copy.wait()
    for i in range(2):
        for n in range(PIECES):
            piece(i, n, x).wait_send()
    for j in range(1, H):
        extra(sm.at[z, yy, c], sm.at[z, yy, c], 3 + j, place.far(j)).wait_send()
    extra(sm.at[:, yy, c], sm.at[:, yy, c], 2, place.over_y()).wait_send()
    extra(sm.at[:, :, c], sm.at[:, :, c], 3, place.over_c()).wait_send()

    @pl.loop(NCH - 6, NCH)
    def _(k):
        settle(k)


def any_spec():
    return pl.BlockSpec(memory_space=pl.ANY)


def vmem_spec():
    return pl.BlockSpec(memory_space=pltpu.VMEM)


def forward(cfg, xin, tin, wq, wo, wu, wd, gain_a, gain_m, mask):
    H, R = cfg["groups"], cfg["rows"]
    NQ, NO, NF = cfg["nq"], cfg["no"], cfg["nf"]
    NCH = NQ + NO + 2 * NF
    IMG = xin.shape[0] // 2
    SEQ, D = 2 * xin.shape[1], xin.shape[2]
    TOK = IMG * SEQ
    GRP = NQ // 3
    wg = (NCH, 2, H, 2, 2, R, CW)
    lhs = (2, D // 2, TOK)
    big = (NF, 2, TOK, CW)
    shapes = [
        (wg, BF), (lhs, BF), ((NQ, 2, IMG, SEQ, CW), BF), ((GRP, 2, IMG, SEQ, 128), F32),
        ((GRP, 2, IMG, SEQ, CW), BF), ((TOK, D), F32), (lhs, BF), (big, BF), (big, BF),
        ((TOK, D), F32), ((TOK, D), BF), (lhs, BF), ((IMG, SEQ, D), BF), ((IMG, SEQ, D), BF), ((IMG, SEQ, D), BF),
        ((8, D), F32), ((8, 128), F32),
    ]
    return pl.pallas_call(
        functools.partial(fwd_kernel, cfg),
        name="gather_forward",
        out_shape=[jax.ShapeDtypeStruct(s, t) for s, t in shapes],
        in_specs=[any_spec()] * 6 + [vmem_spec()] * 3,
        out_specs=[any_spec()] * 15 + [vmem_spec()] * 2,
        scratch_shapes=[
            pltpu.VMEM(wg, BF), pltpu.VMEM((IMG, SEQ, D), BF), pltpu.VMEM((IMG, SEQ, D), BF),
            pltpu.VMEM((H, 2, 2, 8, D), F32), pltpu.VMEM((8, D), F32), pltpu.VMEM((128, -(-SEQ // 128) * 128), F32),
            pltpu.VMEM((IMG, SEQ, 128), F32), pltpu.VMEM((TOK, D), BF),
            pltpu.VMEM((NQ, 2, IMG, SEQ, CW), BF), pltpu.VMEM((GRP, 2, IMG, SEQ, CW), BF),
            pltpu.VMEM((GRP, 2, IMG, SEQ, 128), F32), pltpu.VMEM((TOK, D), F32), pltpu.VMEM((TOK, D), BF),
            pltpu.VMEM(big, BF), pltpu.VMEM(big, BF), pltpu.VMEM((TOK, CW), F32), pltpu.VMEM((TOK, D), F32),
            pltpu.VMEM(lhs, BF),
            pltpu.SemaphoreType.DMA((NCH,)), pltpu.SemaphoreType.DMA((NCH, H + 3)),
            pltpu.SemaphoreType.DMA((NCH, H + 3)), pltpu.SemaphoreType.DMA((H + 4,)),
            pltpu.SemaphoreType.DMA((H + 4,)), pltpu.SemaphoreType.DMA((2, PIECES)),
            pltpu.SemaphoreType.DMA((2, PIECES)), pltpu.SemaphoreType.DMA((NCH,)), pltpu.SemaphoreType.DMA((32,)),
        ],
        compiler_params=pltpu.CompilerParams(
            collective_id=0, has_side_effects=True, vmem_limit_bytes=63 * 2**20
        ),
    )(xin, tin, wq, wo, wu, wd, gain_a, gain_m, mask)


def config(inputs, weights):
    rows = weights[0].shape[0]
    dps = lax.axis_size("dp")
    return {
        "groups": dps // 4,
        "rows": rows,
        "nq": weights[0].shape[1] * weights[0].shape[2] // CW,
        "no": weights[1].shape[1] // CW,
        "nf": weights[2].shape[1] // CW,
        "tokens": float(inputs.shape[0] * inputs.shape[1] * dps * lax.axis_size("mp")),
    }


SLOTS = 3
FAR_AT = 4
WSLOTS = 4
BACK_BOTH_X = (6, 7, 8, 9, 14, 15, 23)
Z_FIRST = (3, 11, 22)
CALLS = (
    (0, 0, 0, 0, 0), (0, 0, 0, 0, 0), (0, 0, 0, 0, 0), (1, 0, 0, 0, 0), (1, 0, 0, 0, 0),
    (0, 0, 0, 0, 0), (1, 0, 0, 0, 0), (0, 1, 0, 0, 0), (1, 0, 0, 0, 0), (0, 0, 0, 0, 0),
    (1, 0, 0, 0, 0), (0, 0, 1, 0, 0), (1, 1, 0, 0, 0), (0, 0, 0, 0, 0), (1, 0, 0, 0, 0),
    (0, 0, 0, 0, 0), (1, 1, 0, 0, 0), (0, 0, 1, 0, 0), (1, 0, 0, 0, 0), (0, 1, 0, 0, 0),
    (1, 0, 0, 0, 0), (0, 1, 0, 1, 0), (1, 0, 1, 0, 0), (0, 0, 0, 1, 0), (1, 0, 0, 0, 0),
    (0, 3, 0, 0, 0), (1, 0, 0, 0, 0), (0, 0, 0, 1, 0), (1, 0, 0, 0, 0), (0, 1, 0, 0, 0),
    (1, 0, 0, 0, 0), (0, 0, 1, 0, 0), (1, 0, 0, 0, 0), (0, 1, 0, 0, 0), (0, 0, 1, 0, 0),
    (0, 0, 0, 0, 0), (0, 2, 0, 0, 0), (1, 0, 3, 0, 0), (1, 0, 0, 0, 0), (0, 1, 0, 0, 0),
    (0, 0, 1, 3, 0), (0, 1, 1, 1, 0), (0, 0, 1, 1, 0), (0, 1, 0, 1, 0), (0, 0, 0, 0, 0),
    (0, 0, 0, 0, 0), (1, 0, 0, 1, 0), (1, 1, 0, 0, 0), (1, 0, 3, 1, 0), (0, 1, 1, 0, 0),
    (0, 1, 1, 2, 0), (0, 1, 1, 1, 0), (0, 1, 1, 1, 0), (0, 0, 0, 1, 0), (0, 0, 1, 0, 0),
    (1, 0, 0, 0, 0), (0, 1, 1, 1, 0), (1, 0, 0, 1, 0), (1, 1, 0, 0, 0), (0, 0, 1, 1, 0),
)
DRAIN = (
    3, 2, 4, 4, 4, 1, 1, 3, 2, 4, 3, 2, 3, 4, 3,
)


def bwd_kernel(cfg, wg, at_i, proj_i, lse_i, o_i, h_i, bnt_i, g_i, gp_i, gy_i, gm_i, gmt_i, out_i, xs_i,
               totals, loss_i, mask, *refs):
    (out_o, ig_o, dq_o, do_o, du_o, dd_o, stat_o,
     q, snd, rcv, near, farr, crossed, dw, wb, gb_buf, gpb, gz, zb, gm, lhs1, lhs2, acc, gh, h, o, go, proj, lse, xb, igr, stat, sbuf, zsum,
     core_send, core_recv, credit, near_send, near_recv, far_send, far_recv, extra_send, extra_recv, piece_send, piece_recv,
     wsem, gsem, misc_sem, dw_sem) = refs
    H, R = cfg["groups"], cfg["rows"]
    NQ, NO, NF = cfg["nq"], cfg["no"], cfg["nf"]
    NCH = NQ + NO + 2 * NF
    IMG, SEQ, D = xb.shape
    HALF = SEQ // 2
    TOK = IMG * SEQ
    GRP = NQ // 3
    place = Place(H)
    x, yy, z, c = place.x, place.y, place.z, place.c
    scale = HDIM ** (-0.5)

    def ident(p):
        ff = jnp.where(lax.rem(p, 2) == 0, NQ + NO + NF + p // 2, NQ + NO + p // 2)
        return jnp.where(p < 2 * NF, ff, jnp.where(p < 2 * NF + NO, p - 2 * NF + NQ, p - 2 * NF - NO))

    def relay(p):
        both = member(p, BACK_BOTH_X)
        first = jnp.where(both, 1, 1 - c)
        xa = jnp.where(first == 1, 1 - x, x)
        ya = jnp.where(first == 1, yy, 1 - yy)
        return xa, ya, jnp.where(first == 1, x, 1 - x), jnp.where(first == 1, 1 - yy, yy)

    loads = []

    def load(src, dst):
        copy = pltpu.make_async_copy(src, dst, misc_sem.at[len(loads)])
        copy.start()
        loads.append(copy)
        return copy

    def wload(n):
        return pltpu.make_async_copy(wg.at[ident(n)], wb.at[lax.rem(n, WSLOTS)], wsem.at[n])

    def gload(j):
        s = lax.rem(j, 2)
        return (pltpu.make_async_copy(g_i.at[j], gb_buf.at[s], gsem.at[j, 0]),
                pltpu.make_async_copy(gp_i.at[j], gpb.at[s], gsem.at[j, 1]))

    gm_l = load(gm_i, gm)
    gmt_l = load(gmt_i, lhs1)
    for j in range(2):
        for copy in gload(jnp.int32(j)):
            copy.start()
    for n in range(WSLOTS):
        wload(jnp.int32(n)).start()
    bnt_l = load(bnt_i, lhs2)
    out_l = load(out_i, xb)
    gy_l = load(gy_i, gh)
    h_l = load(h_i, h)
    o_l = load(o_i, o)
    proj_l = load(proj_i, proj)
    lse_l = load(lse_i, lse)

    def extra(src, dst, i, device):
        return pltpu.make_async_remote_copy(
            src, dst, extra_send.at[i], extra_recv.at[i], device_id=device, device_id_type=MESH
        )

    meet(place)

    def core_copy(p, start=False):
        s = lax.rem(p, SLOTS)
        return pltpu.make_async_remote_copy(
            snd.at[s], rcv.at[s], core_send.at[p], core_recv.at[p], device_id=place.over_c(), device_id_type=MESH
        )

    def near_copy(src, k, i, device):
        return pltpu.make_async_remote_copy(
            src, near.at[k, i], near_send.at[k, i], near_recv.at[k, i], device_id=device, device_id_type=MESH
        )

    def crossing(p):
        slot = jnp.int32(0)
        for n, number in enumerate(Z_FIRST):
            slot = jnp.where(p == number, n, slot)
        return slot

    def cross_copy(p, k, j):
        return pltpu.make_async_remote_copy(
            q.at[k, :, lax.rem(z + j, H), :], crossed.at[crossing(p), j - 1], far_send.at[k, j - 1], far_recv.at[k, j - 1],
            device_id=place.far(j), device_id_type=MESH
        )

    def single_copy(src, k, i, device):
        return pltpu.make_async_remote_copy(
            src, near.at[k, i, 0], near_send.at[k, i], near_recv.at[k, i], device_id=device, device_id_type=MESH
        )

    def either(p, first, last):
        crosses = member(p, Z_FIRST)
        pl.when(crosses)(first)
        pl.when(jnp.logical_not(crosses))(last)

    def far_copy(k, zd, j):
        return pltpu.make_async_remote_copy(
            q.at[k, x, zd, yy], farr.at[k, j - 1], far_send.at[k, j - 1], far_recv.at[k, j - 1],
            device_id=place.far(j), device_id_type=MESH
        )

    def produce(p, lhs, rhs):
        k = ident(p)
        s = lax.rem(p, SLOTS)
        pl.when(p >= SLOTS)(lambda: core_copy(p - SLOTS).wait_send())

        @pl.loop(0, 2)
        def _(half):
            snd[s, half] = dot(lhs[1 - c], rhs(half)).astype(BF).reshape(H, 2, R, CW)
            q[k, half] = dot(lhs[c], rhs(half)).astype(BF).reshape(H, 2, R, CW)

        pl.when(p >= SLOTS)(lambda: pl.semaphore_wait(credit, 1))
        core_copy(p).start()

    def added(k, xi, yi, others):
        @pl.loop(0, H)
        def _(n):
            total = q[k, xi, n, yi].astype(F32)
            for other in others:
                total = total + near[k, other, n].astype(F32)
            q[k, xi, n, yi] = total.astype(BF)

    def r1(p):
        k = ident(p)
        s = lax.rem(p, SLOTS)
        core_copy(p).wait_recv()

        @pl.loop(0, 2 * H)
        def _(n):
            i, m = n // H, lax.rem(n, H)
            q[k, i, m] = q[k, i, m] + rcv[s, i, m]

        pl.when(p + SLOTS < NCH)(
            lambda: pl.semaphore_signal(credit, 1, device_id=place.over_c(), device_id_type=MESH)
        )
        xa, ya, xo, yo = relay(p)

        def cross():
            for j in range(1, H):
                cross_copy(p, k, j).start()

        def plain():
            near_copy(q.at[k, 1 - x, :, 1 - yy], k, 0, place.at(z, yo, c, xo)).start()
            near_copy(q.at[k, xo, :, yo], k, 1, place.at(z, yo, c, xo)).start()

        either(p, cross, plain)

    def r2(p):
        k = ident(p)
        xa, ya, xo, yo = relay(p)

        def cross():
            for j in range(1, H):
                cross_copy(p, k, j).wait_recv()
            slot = crossing(p)

            @pl.loop(0, 2)
            def _(i):
                for m in range(2):
                    total = q[k, i, z, m].astype(F32)
                    for j in range(1, H):
                        total = total + crossed[slot, j - 1, i, m].astype(F32)
                    q[k, i, z, m] = total.astype(BF)

            single_copy(q.at[k, 1 - x, z, 1 - yy], k, 0, place.at(z, yo, c, xo)).start()
            single_copy(q.at[k, xo, z, yo], k, 1, place.at(z, yo, c, xo)).start()

        def plain():
            near_copy(q.at[k, 1 - x, :, 1 - yy], k, 0, place.at(z, yo, c, xo)).wait_recv()
            added(k, xa, ya, (0,))
            near_copy(q.at[k, xa, :, ya], k, 2, place.at(z, ya, c, xa)).start()

        either(p, cross, plain)

    def r3(p):
        k = ident(p)
        xa, ya, xo, yo = relay(p)

        def cross():
            single_copy(q.at[k, 1 - x, z, 1 - yy], k, 0, place.at(z, yo, c, xo)).wait_recv()
            q[k, xa, z, ya] = (q[k, xa, z, ya].astype(F32) + near[k, 0, 0].astype(F32)).astype(BF)
            single_copy(q.at[k, xa, z, ya], k, 2, place.at(z, ya, c, xa)).start()

        def plain():
            near_copy(q.at[k, xo, :, yo], k, 1, place.at(z, yo, c, xo)).wait_recv()
            near_copy(q.at[k, xa, :, ya], k, 2, place.at(z, ya, c, xa)).wait_recv()
            added(k, x, yy, (1, 2))
            for j in range(1, H):
                far_copy(k, lax.rem(z + j, H), j).start()

        either(p, cross, plain)

    def dw_out(k):
        def send(first, count, at):
            @pl.when((k >= first) & (k < first + count))
            def _():
                pltpu.make_async_copy(dw.at[k], at(pl.multiple_of((k - first) * CW, CW)), dw_sem.at[k]).start()

        for part in range(3):
            @pl.when((k < NQ) & (lax.rem(k, 3) == part))
            def _(part=part):
                pltpu.make_async_copy(
                    dw.at[k], dq_o.at[part, :, pl.ds(pl.multiple_of(k // 3 * CW, CW), CW)], dw_sem.at[k]
                ).start()
        send(NQ, NO, lambda n: do_o.at[:, pl.ds(n, CW)])
        send(NQ + NO, NF, lambda n: du_o.at[:, pl.ds(n, CW)])
        send(NQ + NO + NF, NF, lambda n: dd_o.at[:, pl.ds(n, CW)])

    def r4(p):
        k = ident(p)
        xa, ya, xo, yo = relay(p)

        def cross():
            single_copy(q.at[k, xo, z, yo], k, 1, place.at(z, yo, c, xo)).wait_recv()
            single_copy(q.at[k, xa, z, ya], k, 2, place.at(z, ya, c, xa)).wait_recv()
            dw[k] = q[k, x, z, yy].astype(F32) + near[k, 1, 0].astype(F32) + near[k, 2, 0].astype(F32)

        def plain():
            total = q[k, x, z, yy].astype(F32)
            for j in range(1, H):
                far_copy(k, lax.rem(z + j, H), j).wait_recv()
                total = total + farr[k, j - 1].astype(F32)
            dw[k] = total

        either(p, cross, plain)
        dw_out(k)

    stages = (r1, r2, r3, r4)

    before = [[sum(call[i] for call in CALLS[:n]) for n in range(len(CALLS) + 1)] for i in range(5)]
    place_no = [0]

    def serve(numbers, index=None):
        for i in (3, 2, 1, 0):
            counts = [CALLS[n][i] for n in numbers]
            starts = [before[i][n] for n in numbers]
            if index is None:
                for n in range(counts[0]):
                    stages[i](jnp.int32(starts[0] + n))
            elif max(counts) == 1:
                pl.when(pick(counts, index) > 0)(lambda i=i, starts=starts: stages[i](pick(starts, index)))
            elif max(counts) > 1:
                first = pick(starts, index)

                @pl.loop(first, first + pick(counts, index))
                def _(n, i=i):
                    stages[i](n)

    def serve_next():
        serve([place_no[0]])
        place_no[0] += 1

    gm_l.wait()
    gmt_l.wait()
    bnt_l.wait()

    def wchunk(n, half):
        return wb[lax.rem(n, WSLOTS), half].reshape(D, CW)

    def wnext(n):
        pl.when(n + WSLOTS < NCH)(lambda: wload(n + WSLOTS).start())

    GB = 64
    PR = HALF // PIECES
    mine = pl.ds(HALF * x, HALF)

    def piece(i, n):
        return pltpu.make_async_remote_copy(
            xb.at[:, pl.ds(HALF * (1 - x) + PR * n, PR)],
            igr.at[:, pl.ds(PR * n, PR)] if i else out_o.at[pl.ds(IMG * x, IMG), pl.ds(PR * n, PR)],
            piece_send.at[i, n], piece_recv.at[i, n], device_id=place.over_x(), device_id_type=MESH
        )

    acc[...] = jnp.zeros_like(acc)
    out_l.wait()
    out_c = pltpu.make_async_copy(xb.at[:, mine], out_o.at[pl.ds(IMG * x, IMG)], misc_sem.at[30])
    out_c.start()

    @pl.loop(0, NF)
    def _(j):
        s = lax.rem(j, 2)
        pl.when(j < PIECES)(lambda: piece(0, j).start())
        gl, gpl = gload(j)
        gl.wait()
        produce(2 * j, lhs1, lambda half: gb_buf[s, half])
        serve([4 * n for n in range(NF)], j)
        gpl.wait()
        wload(2 * j).wait()

        @pl.loop(0, 2)
        def _(half):
            zb[...] = dot(gm[...], wchunk(2 * j, half))

            @pl.loop(0, TOK // GB)
            def _(r):
                at = pl.ds(pl.multiple_of(r * GB, GB), GB)
                gz[half, at] = (zb[at] * gpb[s, half, at].astype(F32)).astype(BF)

        wnext(2 * j)

        @pl.when(j + 2 < NF)
        def _():
            for copy in gload(j + 2):
                copy.start()

        serve([4 * n + 1 for n in range(NF)], j)
        produce(2 * j + 1, lhs2, lambda half: gz[half])
        serve([4 * n + 2 for n in range(NF)], j)
        wload(2 * j + 1).wait()

        @pl.loop(0, 2)
        def _(half):
            acc[...] += dot(gz[half], wchunk(2 * j + 1, half), NT)

        wnext(2 * j + 1)
        serve([4 * n + 3 for n in range(NF)], j)

    place_no[0] = 4 * NF
    RB = 32

    def norm_back(values, grad, gain):
        centre = values - jnp.mean(values, axis=-1, keepdims=True)
        spread = jnp.mean(centre * centre, axis=-1, keepdims=True)
        scaled = lax.rsqrt(spread + EPS)
        unit = centre * scaled
        e = grad * gain
        first = jnp.mean(e, axis=-1, keepdims=True)
        second = jnp.mean(e * unit, axis=-1, keepdims=True)
        return scaled * (e - first - unit * second), grad * unit

    def fold(v):
        return jnp.sum(v.reshape(-1, 8, D), axis=0)

    base = 2 * NF
    stat[...] = jnp.zeros_like(stat)
    gy_l.wait()
    h_l.wait()

    for part in range(2):
        count = TOK // GB // 2

        @pl.loop(part * count, (part + 1) * count)
        def _(r):
            at = pl.ds(pl.multiple_of(r * GB, GB), GB)
            back, product = norm_back(h[at], acc[at], totals[1:2])
            total = gh[at] + back
            gh[at] = total
            gm[at] = total.astype(BF)
            stat[1] += fold(product)

        serve_next()

    def transposed(src, dst):
        @pl.loop(0, D // 128)
        def _(d):
            t = jnp.transpose(src[:, pl.ds(pl.multiple_of(d * 128, 128), 128)].astype(F32))
            t = t.reshape(64 // R, 2, R, TOK)
            for p in range(2):
                dst[p, pl.ds(pl.multiple_of(d * 64, 64), 64)] = t[:, p].reshape(64, TOK).astype(BF)

    at_l = load(at_i, lhs2)
    transposed(gm, lhs1)
    o_l.wait()
    for k in range(NO):
        produce(jnp.int32(base + k), lhs1, lambda half, k=k: o[k, half].reshape(TOK, CW))
        serve_next()
        wload(jnp.int32(base + k)).wait()

        @pl.loop(0, 2)
        def _(half, k=k):
            go[k, half] = dot(gm[...], wchunk(jnp.int32(base + k), half)).astype(BF).reshape(IMG, SEQ, CW)

        wnext(jnp.int32(base + k))
        serve_next()
    proj_l.wait()
    lse_l.wait()
    lane = lax.broadcasted_iota(jnp.int32, (SEQ, CW), 1) // HDIM
    TN = (((0,), (0,)), ((), ()))

    def attend_back(group, u):
        half, i = u // IMG, lax.rem(u, IMG)
        qr, kr, vr = 3 * group, 3 * group + 1, 3 * group + 2
        query, key, val = proj[qr, half, i], proj[kr, half, i], proj[vr, half, i]
        grad = go[group, half, i]
        logs = lse[group, half, i]
        allowed = mask[pl.ds(IMG * x + i, 1)] > 0
        gq = jnp.zeros((SEQ, CW), F32)
        gk = jnp.zeros((SEQ, CW), F32)
        gv = jnp.zeros((SEQ, CW), F32)
        for head in range(CW // HDIM):
            of_head = lane == head
            qm = jnp.where(of_head, query, 0)
            gom = jnp.where(of_head, grad, 0)
            scores = jnp.where(allowed, dot(qm, key, NT) * scale, -1e30)
            soft = jnp.exp(scores - logs[:, head:head + 1])
            gsoft = dot(gom, val, NT)
            inner = jnp.sum(gsoft * soft, axis=-1, keepdims=True)
            gs = (soft * (gsoft - inner)).astype(BF)
            gq = gq + dot(gs, jnp.where(of_head, key, 0))
            gk = gk + dot(gs, qm, TN)
            gv = gv + dot(soft.astype(BF), gom, TN)
        proj[qr, half, i] = (gq * scale).astype(BF)
        proj[kr, half, i] = (gk * scale).astype(BF)
        proj[vr, half, i] = gv.astype(BF)

    acc[...] = jnp.zeros_like(acc)
    at_l.wait()
    out_c.wait()
    for n in range(PIECES):
        piece(0, n).wait_send()
    xs_l = load(xs_i, xb)

    n0 = place_no[0]
    per_group = 2 * IMG + 6
    place_no[0] += per_group * GRP

    def numbers(first, count):
        return [n0 + per_group * group + first + n for group in range(GRP) for n in range(count)]

    @pl.loop(0, GRP)
    def _(group):
        @pl.loop(0, 2 * IMG)
        def _(u):
            serve(numbers(0, 2 * IMG), 2 * IMG * group + u)
            attend_back(group, u)

        @pl.loop(0, 3)
        def _(n):
            serve(numbers(2 * IMG, 3), 3 * group + n)
            k = 3 * group + n
            produce(base + NO + k, lhs2, lambda half: proj[k, half].reshape(TOK, CW))

        @pl.loop(0, 3)
        def _(n):
            serve(numbers(2 * IMG + 3, 3), 3 * group + n)
            k = 3 * group + n
            wload(base + NO + k).wait()

            @pl.loop(0, 2)
            def _(half):
                acc[...] += dot(proj[k, half].reshape(TOK, CW), wchunk(base + NO + k, half), NT)

            wnext(base + NO + k)

    xs_l.wait()
    serve_next()
    per = SEQ // RB

    def finish(img, row, here):
        at = pl.ds(pl.multiple_of(img * SEQ + row, RB), RB)
        back, product = norm_back(xb[img, pl.ds(row, RB)].astype(F32), acc[at], totals[0:1])
        if here:
            gh[at] = gh[at] + back
        else:
            xb[img, pl.ds(row, RB)] = (gh[at] + back).astype(BF)
        stat[0] += fold(product)

    @pl.loop(0, PIECES)
    def _(n):
        @pl.loop(0, IMG)
        def _(img):
            finish(img, pl.multiple_of(HALF * (1 - x) + PR * n, RB), False)

        piece(1, n).start()

    serve_next()

    @pl.loop(0, PIECES)
    def _(n):
        @pl.loop(0, IMG)
        def _(img):
            finish(img, pl.multiple_of(HALF * x + PR * n, RB), True)

    ig_c = [pltpu.make_async_copy(gh.at[pl.ds(pl.multiple_of(i * SEQ + HALF * x, RB), HALF)], ig_o.at[IMG * x + i],
                                  misc_sem.at[26 + i]) for i in range(IMG)]
    for copy in ig_c:
        copy.start()
    ig_far = [pltpu.make_async_copy(acc.at[pl.ds(i * HALF, HALF)], ig_o.at[IMG * (1 - x) + i], misc_sem.at[28 + i])
              for i in range(IMG)]

    def take_far():
        for n in range(PIECES):
            piece(1, n).wait_recv()

        @pl.loop(0, HALF // RB)
        def _(r):
            row = pl.multiple_of(r * RB, RB)
            for i in range(IMG):
                acc[pl.ds(i * HALF + row, RB)] = igr[i, pl.ds(row, RB)].astype(F32)

        for copy in ig_far:
            copy.start()

    row = lax.broadcasted_iota(jnp.int32, (8, D), 0)
    small = jnp.where(row == 0, jnp.sum(stat[0], axis=0, keepdims=True),
                      jnp.where(row == 1, jnp.sum(stat[1], axis=0, keepdims=True),
                                jnp.tile(loss_i[...], (1, D // 128))))
    steps = (place.over_c(), place.over_y(), place.over_x())

    def small_sum(n):
        if 1 <= n <= 3:
            extra(sbuf.at[2 * n - 2], sbuf.at[2 * n - 1], 1 + n, steps[n - 1]).wait()
        value = small if n == 0 else sbuf[2 * n - 2] + sbuf[2 * n - 1] if n < 4 else None
        if n < 3:
            sbuf[2 * n] = value
            extra(sbuf.at[2 * n], sbuf.at[2 * n + 1], 2 + n, steps[n]).start()
        elif n == 3:
            zsum[z] = value
            for j in range(1, H):
                extra(zsum.at[z], zsum.at[z], 4 + j, place.far(j)).start()
        else:
            for j in range(1, H):
                extra(zsum.at[z], zsum.at[lax.rem(z + H - j, H)], 4 + j, place.far(j)).wait()
            total = jnp.sum(zsum[...], axis=0)
            stat_o[...] = jnp.where(row == 2, total / totals[2:3], total)

    def settle(p):
        k = ident(p)
        pltpu.make_async_copy(dw.at[k], do_o.at[:, pl.ds(0, CW)], dw_sem.at[k]).wait()

        def cross():
            for j in range(1, H):
                cross_copy(p, k, j).wait_send()
            for i in range(3):
                single_copy(q.at[k, x, z, yy], k, i, place.over_x()).wait_send()

        def plain():
            for i in range(3):
                near_copy(q.at[k, x, :, yy], k, i, place.over_x()).wait_send()
            for j in range(1, H):
                far_copy(k, z, j).wait_send()

        either(p, cross, plain)

    done = [before[i][len(CALLS)] for i in range(5)]
    settled = [0]
    for n, i in enumerate(DRAIN):
        if n == len(DRAIN) - FAR_AT:
            take_far()
        if settled[0] + 2 <= min(done[3], NCH - 6):
            for p in range(settled[0], settled[0] + 2):
                settle(jnp.int32(p))
            settled[0] += 2
        if i < 4:
            stages[i](jnp.int32(done[i]))
        else:
            small_sum(done[i])
        done[i] += 1
    assert done == [NCH] * 4 + [5] and place_no[0] == len(CALLS)

    for copy in ig_c + ig_far:
        copy.wait()
    for n in range(PIECES):
        piece(0, n).wait_recv()
        piece(1, n).wait_send()

    @pl.loop(NCH - SLOTS, NCH)
    def _(p):
        core_copy(p).wait_send()

    @pl.loop(settled[0], NCH)
    def _(p):
        settle(p)


def backward(cfg, saved, mask):
    (wg, at, proj, lse, o, h, bnt, g, gp, gy, gm, gmt, out, xs, ts, totals, loss) = saved
    H, R = cfg["groups"], cfg["rows"]
    NQ, NO, NF = cfg["nq"], cfg["no"], cfg["nf"]
    NCH = NQ + NO + 2 * NF
    IMG, SEQ, D = xs.shape
    TOK = IMG * SEQ
    lhs = (2, D // 2, TOK)
    half = (2, H, 2, R, CW)
    vm = pltpu.VMEM
    dma = pltpu.SemaphoreType.DMA
    return pl.pallas_call(
        functools.partial(bwd_kernel, cfg),
        name="backward_reduce",
        out_shape=[
            jax.ShapeDtypeStruct((2 * IMG, SEQ // 2, D), BF), jax.ShapeDtypeStruct((2 * IMG, SEQ // 2, D), F32),
            jax.ShapeDtypeStruct((3, R, NQ // 3 * CW), F32), jax.ShapeDtypeStruct((R, NO * CW), F32),
            jax.ShapeDtypeStruct((R, NF * CW), F32), jax.ShapeDtypeStruct((R, NF * CW), F32),
            jax.ShapeDtypeStruct((8, D), F32),
        ],
        in_specs=[any_spec()] * 14 + [vmem_spec()] * 3,
        out_specs=[any_spec()] * 6 + [vmem_spec()],
        scratch_shapes=[
            vm((NCH,) + half, BF), vm((SLOTS,) + half, BF), vm((SLOTS,) + half, BF),
            vm((NCH, 3, H, R, CW), BF), vm((NCH, H - 1, R, CW), BF),
            vm((max(len(Z_FIRST), 1), H - 1, 2, 2, R, CW), BF), vm((NCH, R, CW), F32),
            vm((WSLOTS, 2, H, 2, 2, R, CW), BF), vm((2, 2, TOK, CW), BF), vm((2, 2, TOK, CW), BF),
            vm((2, TOK, CW), BF), vm((TOK, CW), F32), vm((TOK, D), BF), vm(lhs, BF), vm(lhs, BF),
            vm((TOK, D), F32), vm((TOK, D), F32), vm((TOK, D), F32), vm(o.shape, BF), vm(o.shape, BF),
            vm(proj.shape, BF), vm(lse.shape, F32), vm(xs.shape, BF),
            vm((IMG, SEQ // 2, D), BF), vm((2, 8, D), F32), vm((6, 8, D), F32), vm((H, 8, D), F32),
            dma((NCH,)), dma((NCH,)), pltpu.SemaphoreType.REGULAR, dma((NCH, 3)), dma((NCH, 3)),
            dma((NCH, H - 1)), dma((NCH, H - 1)), dma((H + 4,)), dma((H + 4,)), dma((2, PIECES)), dma((2, PIECES)),
            dma((NCH,)), dma((NF, 2)), dma((32,)), dma((NCH,)),
        ],
        compiler_params=pltpu.CompilerParams(
            collective_id=1, has_side_effects=True, vmem_limit_bytes=63 * 2**20
        ),
    )(wg, at, proj, lse, o, h, bnt, g, gp, gy, gm, gmt, out, xs, totals, loss, mask)


def per_device(
    inputs, teacher, keep_mask, gain_attn, qkv_weight, out_weight, gain_mlp, up_weight, down_weight
):
    cfg = config(inputs, (qkv_weight, out_weight, up_weight, down_weight))
    R = cfg["rows"]
    saved = forward(
        cfg, inputs, teacher, qkv_weight.transpose(1, 0, 2), out_weight, up_weight, down_weight,
        gain_attn.reshape(1, R), gain_mlp.reshape(1, R), keep_mask
    )
    output, input_grad, qkv_grad, out_grad, up_grad, down_grad, stats = backward(cfg, saved, keep_mask)
    gains = lax.dynamic_slice(stats, (0, lax.axis_index("dp") * R), (2, R))
    return (
        output, stats[2, 0], input_grad, gains[0], qkv_grad.transpose(1, 0, 2), out_grad, gains[1], up_grad, down_grad
    )


def solution(mesh):
    rows = P("dp", "mp", None)
    weight = P("dp", "mp")
    qkv = P("dp", None, "mp")
    return jax.shard_map(
        per_device,
        mesh=mesh,
        in_specs=(rows, rows, P("dp", None), P("dp"), qkv, weight, P("dp"), weight, weight),
        out_specs=(rows, P(), rows, P("dp"), qkv, weight, P("dp"), weight, weight),
        check_vma=False,
    )
```
